256 devices in a mesh: stream: 32 (over z, y), item: 8 (over x, core).
Axes of the slice: x: 4, y: 4, z: 8, core: 2. Of those that a mesh axis runs over, the one named last changes fastest.
Arguments:
- event_items: int32 [131072], P('stream'), may hold values from 0 to 262143, as said below
- event_sessions: int32 [131072], P('stream'), may hold values from 0 to 8191, never falling along the last dimension, each value on 1 to 64 neighbouring positions
- sketch_bits: int32 [15, 262144], P(None, 'item'), may hold values from 0 to 262143
Outputs:
- sketch: float32 [128, 256], P('stream')
The draws below stay inside these ranges and needn't reach their ends.
Inputs may be any that keep to these rules, and one draw needn't show every extreme that they name: `event_items`: item 262144 - 1 occurs at least once.
All inputs are finite; a program needn't handle non-finite values.
Results may differ from the reference program's by a relative error of at most 0.0006.
Values may be sent and summed in bfloat16 or wider, within the bound.
No kernel may reach another device: no remote copies, remote signals or barrier semaphores. Data moves between devices by JAX's collectives and lax.ppermute only.
A program may use at most 128 MiB of HBM per device.

```python
import math
import jax
import jax.numpy as jnp
import numpy as np
from jax import lax

ITEMS = 262144
SKETCH = 256
WINDOW = 15
WORDS = 15
EVENTS = 131072
ROWS = 128


def draw_event_items(key, part):
    first_key, second_key, third_key = jax.random.split(jax.random.fold_in(key, 7), 3)
    picker = jax.random.randint(first_key, (EVENTS,), 0, 2)
    row_items = jax.random.randint(second_key, (EVENTS,), 0, ROWS)
    wide_items = jax.random.randint(third_key, (EVENTS,), 0, ITEMS)
    chosen = jnp.where(picker == 0, row_items, wide_items)
    return chosen.at[EVENTS // 2].set(ITEMS - 1).astype(jnp.int32)


def place_ends(values, own_key, low, high):
    dims = values.shape
    index_at = [jax.random.randint(jax.random.fold_in(own_key, axis), (), 0, dims[axis]) for axis in range(len(dims))]
    values = values.at[tuple(index_at)].set(low)
    longest = dims.index(max(dims))
    index_at[longest] = (index_at[longest] + 1) % dims[longest]
    return values.at[tuple(index_at)].set(high)


def split_up(count, total, most, slope):
    weights = [(1 << 20) // math.isqrt(rank ** slope) + 1 for rank in range(2, count + 1)]
    rest, given = total - most - (count - 1), [1] * (count - 1)
    while rest > 0:
        candidates = [i for i in range(count - 1) if given[i] < most]
        pool, remaining = sum([weights[i] for i in candidates]), rest
        for i in candidates:
            more = min(most - given[i], max(1, remaining * weights[i] // pool), rest)
            given[i] = given[i] + more
            rest = rest - more
    return np.array([most] + given)


def uneven(rng, count, total, bound, lean):
    if count == 2:
        one = jax.random.randint(rng, (), max(1, total - bound), min(bound, total - 1) + 1)
        return jnp.stack([one, total - one])
    tallies = jnp.asarray(split_up(count, total, bound, lean), jnp.int32)
    pairs = (count - 1) // 2
    giver, receiver = tallies[1:1 + 2 * pairs:2], tallies[2:2 + 2 * pairs:2]
    room = jnp.minimum(giver - 1, bound - receiver)
    passed = jax.random.randint(jax.random.fold_in(rng, 1), (pairs,), 0, 1 << 20) % (room + 1)
    tallies = tallies.at[1:1 + 2 * pairs:2].set(giver - passed).at[2:2 + 2 * pairs:2].set(receiver + passed)
    return tallies[jax.random.permutation(jax.random.fold_in(rng, 2), count)]


def setup_inputs(seed: int = 0) -> dict:
    key_of = jax.random.split(jax.random.key(seed), 4)
    return {
        "event_items": draw_event_items(jax.random.fold_in(key_of[3], 71), 0),
        "event_sessions": jnp.searchsorted(jnp.cumsum(uneven(key_of[1], EVENTS // 16, EVENTS, 64, 0)), jnp.arange(EVENTS), side="right").astype(jnp.int32),
        "sketch_bits": place_ends(jax.random.randint(key_of[2], (WORDS, ITEMS), 0, 2 ** 18), jax.random.fold_in(key_of[2], 1), 0, (2 ** 18) - 1).astype(jnp.int32),
    }


def pointwise(count_block, row_margin, col_margin, pair_total):
    log_ratio = jnp.log(jnp.maximum(count_block, 1.0)) + jnp.log(pair_total) - jnp.log(jnp.maximum(row_margin, 1.0)) - jnp.log(jnp.maximum(col_margin, 1.0))
    return jnp.where(count_block > 0, jnp.maximum(log_ratio, 0.0), 0.0)

def sign_table(bit_block, sketch_width):
    word_count = bit_block.shape[0]
    spread = jnp.repeat(bit_block, 18, axis=0, total_repeat_length=word_count * 18)[:sketch_width]
    bit_shift = (jnp.arange(sketch_width, dtype=jnp.int32) % 18)[:, None]
    return (2 * jnp.bitwise_and(jnp.right_shift(spread, bit_shift), 1) - 1).astype(jnp.float32)

def reference(event_items, event_sessions, sketch_bits):
    position = jnp.arange(EVENTS, dtype=jnp.int32)
    partners = []
    weights = []
    for offset in range(1, WINDOW + 1):
        for direction in (1, -1):
            other_pos = position + direction * offset
            inside = (other_pos >= 0) & (other_pos < EVENTS)
            clipped = jnp.clip(other_pos, 0, EVENTS - 1).astype(jnp.int32)
            linked = inside & (event_sessions[clipped] == event_sessions)
            partners.append(event_items[clipped])
            weights.append(linked.astype(jnp.float32))
    partner_all = jnp.concatenate(partners)
    weight_all = jnp.concatenate(weights)
    owner_all = jnp.tile(event_items, 2 * WINDOW)
    margin = jnp.zeros((ITEMS,), jnp.float32).at[partner_all].add(weight_all)
    hit_row = owner_all < ROWS
    counts = jnp.zeros((ROWS, ITEMS), jnp.float32).at[jnp.where(hit_row, owner_all, 0), partner_all].add(jnp.where(hit_row, weight_all, 0.0))
    pair_total = jnp.sum(margin)
    row_margin = margin[:ROWS]
    block_width = math.gcd(ITEMS, 8192)

    def accumulate(block_index, summed):
        first_col = (block_index * block_width).astype(jnp.int32)
        count_block = lax.dynamic_slice_in_dim(counts, first_col, block_width, 1)
        col_margin = lax.dynamic_slice_in_dim(margin, first_col, block_width, 0)
        bit_block = lax.dynamic_slice_in_dim(sketch_bits, first_col, block_width, 1)
        positive = pointwise(count_block, row_margin[:, None], col_margin[None, :], pair_total)
        sign_rows = sign_table(bit_block, SKETCH)
        return summed + lax.dot_general(positive, sign_rows, (((1,), (1,)), ((), ())), precision=lax.Precision.HIGHEST, preferred_element_type=jnp.float32)
    summed = lax.fori_loop(0, ITEMS // block_width, accumulate, jnp.zeros((ROWS, SKETCH), jnp.float32))
    return summed / math.sqrt(EVENTS)
```

```python
import math

import jax
import jax.numpy as jnp
from jax import lax
from jax.experimental import pallas as pl
from jax.experimental.pallas import tpu as pltpu
from jax.sharding import PartitionSpec as P

SKETCH = 256
WINDOW = 15
ROWS = 128
ROWS_DEV = 4
LANES = 128
SLABS = 32
BANDS = 8
SLAB_ROWS = 32
HALF_ROWS = SLAB_ROWS // 2
PAYLOAD = 32
EVENT_ROWS = SLABS * SLAB_ROWS
OWNED = 1024
COLS = OWNED + ROWS
WORD_BITS = 18
WORDS = 15
SLOTS = 384
PAD = 8
MARGIN_ROW, TOTAL_ROW, BITS_ROW = 24, 25, 26
VMEM_BYTES = 48 << 20


def iota(shape, axis, dtype=jnp.int32):
    out = lax.broadcasted_iota(jnp.int32, shape, axis)
    return out if dtype == jnp.int32 else out.astype(dtype)


def nt_dot(left, right):
    return lax.dot_general(
        left, right, (((1,), (1,)), ((), ())), preferred_element_type=jnp.float32
    )


def hot(mask):
    return jnp.where(mask, 1.0, 0.0)


def pack_kernel(where, items_ref, sessions_ref, bits_ref, out_ref):
    _, band = where()
    half = lax.rem(band, 2)
    items, sessions = items_ref[...], sessions_ref[...]
    shape = items.shape
    row, lane = iota(shape, 0), iota(shape, 1)
    above = jnp.where(row == 0, -1, pltpu.roll(sessions, 1, 0))
    below = jnp.where(row == SLAB_ROWS - 1, -1, pltpu.roll(sessions, SLAB_ROWS - 1, 0))
    weights = jnp.zeros(shape, jnp.float32)
    for d in range(1, WINDOW + 1):
        earlier = pltpu.roll(jnp.where(lane >= LANES - d, above, sessions), d, 1)
        later = pltpu.roll(jnp.where(lane < d, below, sessions), LANES - d, 1)
        weights += hot(earlier == sessions) + hot(later == sessions)
    held = jnp.zeros((ROWS, LANES), jnp.float32)
    item_row = iota((ROWS, LANES), 0)
    for r in range(SLAB_ROWS):
        held += jnp.where(items[r : r + 1] == item_row, weights[r : r + 1], 0.0)
    margin = jnp.sum(held.T, axis=0, keepdims=True).astype(jnp.int32)
    total = jnp.sum(weights, axis=0, keepdims=True).astype(jnp.int32)
    own_items = jnp.where(half == 0, items[:HALF_ROWS], items[HALF_ROWS:])
    own_sessions = jnp.where(half == 0, sessions[:HALF_ROWS], sessions[HALF_ROWS:])
    pairs = own_sessions[:8] + own_sessions[8:] * 65536
    slab, _ = where()
    word = bits_ref[...]
    one = jnp.sum(
        jnp.where(iota(word.shape, 0) == jnp.minimum(slab, WORDS - 1), word, 0),
        axis=0,
        keepdims=True,
    )
    extra = jnp.concatenate([margin, total, one, jnp.zeros((5, LANES), jnp.int32)], axis=0)
    message = jnp.concatenate([own_items, pairs, extra], axis=0)
    for s in range(SLABS):
        out_ref[s] = message


def sketch_kernel(
    where, own_ref, other_ref, bits_hbm, out_ref,
    sess, codes, mask, table, counts, words, signs, sem,
):
    slab, band = where()
    half = lax.rem(band, 2)
    copy = pltpu.make_async_copy(
        bits_hbm.at[:, pl.ds(pl.multiple_of(slab * OWNED, OWNED), OWNED)],
        words,
        sem,
    )
    copy.start()
    lane_s = iota((SLAB_ROWS, LANES), 1)
    block_id = band * SLABS + slab
    pair_id = jnp.where(band < 2, 2 * slab + half, -1)

    edge = jnp.full((PAD, LANES), -(ROWS + 1.0), jnp.float32)
    codes[pl.ds(0, PAD), :] = edge
    codes[pl.ds(PAD + EVENT_ROWS, PAD), :] = edge
    sess[pl.ds(0, PAD), :] = jnp.full((PAD, LANES), -1, jnp.int32)

    def halves(s):
        mine, its = own_ref[s], other_ref[s]
        return jnp.where(half == 0, mine, its), jnp.where(half == 0, its, mine)

    def unpack(s, carry):
        first, second = halves(s)
        items = jnp.concatenate([first[:16], second[:16]], axis=0)
        a, b = first[16:24], second[16:24]
        sessions = jnp.concatenate([a & 65535, a >> 16, b & 65535, b >> 16], axis=0)
        base = pl.multiple_of(s * SLAB_ROWS, SLAB_ROWS)
        sess[pl.ds(PAD + base, SLAB_ROWS), :] = sessions
        above = sess[pl.ds(PAD - 1 + base, SLAB_ROWS), :]
        before = pltpu.roll(jnp.where(lane_s == LANES - 1, above, sessions), 1, 1)
        value = jnp.minimum(items, ROWS) + 1
        codes[pl.ds(PAD + base, SLAB_ROWS), :] = jnp.where(
            before != sessions, -value, value
        ).astype(jnp.float32)
        is_row = items < ROWS
        owned = jnp.where(is_row, items >> 1, items >> 10) == jnp.where(is_row, pair_id, block_id)
        ident = jnp.where(is_row, OWNED + items, items & (OWNED - 1))
        rows = pl.ds(base, SLAB_ROWS)
        mask[rows, :] = hot(owned).astype(jnp.bfloat16)
        table[rows, pl.ds(LANES, LANES)] = (ident & 255).astype(jnp.float32).astype(jnp.bfloat16)
        table[rows, pl.ds(2 * LANES, LANES)] = (ident >> 8).astype(jnp.float32).astype(jnp.bfloat16)
        return carry

    lax.fori_loop(0, SLABS, unpack, 0, unroll=4)
    for r in range(0, EVENT_ROWS, 128):
        rows = pl.ds(r, 128)
        table[rows, pl.ds(3 * LANES, LANES)] = codes[pl.ds(PAD - 1 + r, 128), :].astype(jnp.bfloat16)
        table[rows, pl.ds(4 * LANES, LANES)] = codes[pl.ds(PAD + r, 128), :].astype(jnp.bfloat16)
        table[rows, pl.ds(5 * LANES, LANES)] = codes[pl.ds(PAD + 1 + r, 128), :].astype(jnp.bfloat16)

    upto = hot(iota((LANES, LANES), 0) <= iota((LANES, LANES), 1)).astype(jnp.bfloat16)
    owned = mask[...]
    rank = jnp.dot(owned, upto, preferred_element_type=jnp.float32)
    table[:, pl.ds(0, LANES)] = (rank * owned.astype(jnp.float32)).astype(jnp.bfloat16)
    per_row = nt_dot(jnp.ones((8, LANES), jnp.bfloat16), owned)
    groups = EVENT_ROWS // LANES
    grouped = jnp.concatenate(
        [per_row[:1, g * LANES : (g + 1) * LANES] for g in range(groups)], axis=0
    )
    inside = jnp.dot(grouped.astype(jnp.bfloat16), upto, preferred_element_type=jnp.float32)
    ends, starts, base = [], [], jnp.zeros((1, 1), jnp.float32)
    for g in range(groups):
        ends.append(inside[g : g + 1] + base)
        starts.append(ends[g] - grouped[g : g + 1])
        base = base + inside[g : g + 1, LANES - 1 :]
    owned_events = jnp.max(base).astype(jnp.int32)

    counts[...] = jnp.zeros(counts.shape, jnp.float32)
    lane_f = iota((SLOTS, LANES), 1, jnp.float32)
    row32, col32 = iota((32, 32), 0), iota((32, 32), 1)
    ahead = (row32 > WINDOW) & (col32 > WINDOW) & (col32 <= row32)
    behind = (row32 < WINDOW) & (col32 > row32) & (col32 <= WINDOW)
    between = hot(ahead | behind).astype(jnp.bfloat16)
    place = iota((32, SLOTS), 0)
    in_window = (place != WINDOW) & (place <= 2 * WINDOW)
    row_ids = iota((ROWS, SLOTS), 0, jnp.float32)
    col_ids = iota((SLOTS, COLS), 1, jnp.float32)

    def chunk(step, carry):
        slot = (step * SLOTS + iota((SLOTS, LANES), 0)).astype(jnp.float32)
        picks, first = [], jnp.zeros((SLOTS, LANES), jnp.float32)
        for g in range(groups):
            here = (slot >= starts[g]) & (slot < ends[g])
            first += jnp.where(here, starts[g], 0.0)
            picks.append(hot(here).astype(jnp.bfloat16))
        pick = jnp.concatenate(picks, axis=1)
        got = jnp.dot(pick, table[...], preferred_element_type=jnp.float32)
        ordinal = slot[:, :1] + 1.0 - jnp.sum(first, axis=1, keepdims=True)
        chosen = got[:, :LANES] == ordinal
        ident = got[:, LANES : 2 * LANES] + 256.0 * got[:, 2 * LANES : 3 * LANES]
        column = jnp.sum(jnp.where(chosen, ident + 1.0, 0.0), axis=1, keepdims=True) - 1.0
        at_lane = jnp.sum(jnp.where(chosen, lane_f, 0.0), axis=1, keepdims=True)
        source = at_lane.astype(jnp.int32) + (iota((SLOTS, LANES), 1) - WINDOW)
        index = source & (LANES - 1)
        parts = [
            jnp.take_along_axis(got[:, k * LANES : (k + 1) * LANES], index, axis=1, mode="promise_in_bounds")
            for k in (3, 4, 5)
        ]
        window = jnp.where(source < 0, parts[0], jnp.where(source < LANES, parts[1], parts[2]))
        window = window.T[:32]
        breaks = hot(window < 0.0).astype(jnp.bfloat16)
        crossed = jnp.dot(between, breaks, preferred_element_type=jnp.float32)
        linked = (crossed == 0.0) & in_window
        near = jnp.where(linked, jnp.abs(window) - 1.0, 255.0)
        weight = jnp.sum(hot(linked), axis=0, keepdims=True)
        pairs = jnp.zeros((ROWS, SLOTS), jnp.float32)
        for d in range(2 * WINDOW + 1):
            if d != WINDOW:
                pairs += hot(near[d : d + 1] == row_ids)
        pairs = jnp.concatenate([pairs, jnp.broadcast_to(weight, (16, SLOTS))], axis=0)
        column_hot = hot(column == col_ids).astype(jnp.bfloat16)
        counts[...] += jnp.dot(
            pairs.astype(jnp.bfloat16), column_hot, preferred_element_type=jnp.float32
        )
        return carry

    lax.fori_loop(0, (owned_events + SLOTS - 1) // SLOTS, chunk, 0)

    def both(row_first, row_second):
        mine_f, its_f = own_ref[:, row_first, :], other_ref[:, row_first, :]
        mine_s, its_s = own_ref[:, row_second, :], other_ref[:, row_second, :]
        return jnp.where(half == 0, mine_f, its_f), jnp.where(half == 0, its_s, mine_s)

    start_items, end_items = both(0, 15)
    start_sess, end_sess = both(16, 23)
    start_sess, end_sess = start_sess & 65535, end_sess >> 16
    slab_row = iota((SLABS, LANES), 0)
    end_items = pltpu.roll(end_items, 1, 0)
    end_sess = jnp.where(slab_row == 0, -1, pltpu.roll(end_sess, 1, 0))
    cross = jnp.zeros((SLABS, LANES), jnp.float32)
    lane = iota((SLABS, LANES), 1)
    for d in range(1, WINDOW + 1):
        before = pltpu.roll(end_sess, d, 1)
        after = pltpu.roll(start_sess, LANES - d, 1)
        cross += hot((lane < d) & (before == start_sess))
        cross += hot((lane >= LANES - d) & (after == end_sess))
    cross_items = jnp.where(lane < LANES // 2, start_items, end_items)
    margins = jnp.sum(own_ref[:, MARGIN_ROW, :], axis=0, keepdims=True).astype(jnp.float32)
    item_row = iota((ROWS, LANES), 0)
    held = jnp.where(item_row == iota((ROWS, LANES), 1), margins, 0.0)
    for s in range(SLABS):
        held += jnp.where(cross_items[s : s + 1] == item_row, cross[s : s + 1], 0.0)
    row_margin = jnp.sum(held, axis=1, keepdims=True)
    totals = jnp.sum(own_ref[:, TOTAL_ROW, :], axis=0, keepdims=True).astype(jnp.float32)
    totals = totals + jnp.sum(cross, axis=0, keepdims=True)
    pair_total = jnp.sum(totals, axis=1, keepdims=True)

    count = counts[pl.ds(0, ROWS), :]
    col_margin = counts[pl.ds(ROWS, 1), :]
    log_ratio = (
        jnp.log(jnp.maximum(count, 1.0))
        + jnp.log(pair_total)
        - jnp.log(jnp.maximum(row_margin, 1.0))
        - jnp.log(jnp.maximum(col_margin, 1.0))
    )
    positive = jnp.where(count > 0, jnp.maximum(log_ratio, 0.0), 0.0)
    high = positive.astype(jnp.bfloat16)
    rest = positive - high.astype(jnp.float32)
    mid = rest.astype(jnp.bfloat16)
    low = (rest - mid.astype(jnp.float32)).astype(jnp.bfloat16)
    parts = jnp.concatenate([high, mid, low], axis=0)

    copy.wait()
    row_words = jnp.where(half == 0, own_ref[:WORDS, BITS_ROW, :], other_ref[:WORDS, BITS_ROW, :])
    held_words = jnp.concatenate([words[...], row_words], axis=1)
    held_words = jnp.concatenate([held_words, jnp.zeros((1, COLS), jnp.int32)], axis=0)
    for b in range(WORD_BITS):
        signs[pl.ds(b * 16, 16), :] = jnp.where((held_words >> b) & 1 == 1, 1.0, -1.0).astype(jnp.bfloat16)
    by_bit = nt_dot(parts, signs[...])
    by_bit = by_bit[:ROWS] + (by_bit[ROWS : 2 * ROWS] + by_bit[2 * ROWS :])
    have = iota((16 * WORD_BITS, SKETCH), 0)
    want = iota((16 * WORD_BITS, SKETCH), 1)
    order = hot((have & 15) * WORD_BITS + (have >> 4) == want).astype(jnp.bfloat16)
    high = by_bit.astype(jnp.bfloat16)
    rest = by_bit - high.astype(jnp.float32)
    mid = rest.astype(jnp.bfloat16)
    low = (rest - mid.astype(jnp.float32)).astype(jnp.bfloat16)
    moved = jnp.dot(
        jnp.concatenate([high, mid, low], axis=0), order, preferred_element_type=jnp.float32
    )
    result = moved[:ROWS] + (moved[ROWS : 2 * ROWS] + moved[2 * ROWS :])
    for s in range(SLABS):
        out_ref[s] = result[s * ROWS_DEV : (s + 1) * ROWS_DEV]


def pack(where, items, sessions, bits, interpret=False):
    return pl.pallas_call(
        lambda *refs: pack_kernel(where, *refs),
        out_shape=jax.ShapeDtypeStruct((SLABS, PAYLOAD, LANES), jnp.int32),
        grid=(1,),
        in_specs=[
            pl.BlockSpec((SLAB_ROWS, LANES), lambda i: (0, 0)),
            pl.BlockSpec((SLAB_ROWS, LANES), lambda i: (0, 0)),
            pl.BlockSpec((WORDS, LANES), lambda i: (0, 0)),
        ],
        out_specs=pl.BlockSpec((SLABS, PAYLOAD, LANES), lambda i: (0, 0, 0)),
        compiler_params=pltpu.CompilerParams(vmem_limit_bytes=VMEM_BYTES),
        interpret=interpret,
        name="pack_events",
    )(items, sessions, bits)


def sketch_part(where, own, other, bits, interpret=False):
    return pl.pallas_call(
        lambda *refs: sketch_kernel(where, *refs),
        out_shape=jax.ShapeDtypeStruct((SLABS, ROWS_DEV, SKETCH), jnp.float32),
        in_specs=[
            pl.BlockSpec(memory_space=pltpu.VMEM),
            pl.BlockSpec(memory_space=pltpu.VMEM),
            pl.BlockSpec(memory_space=pl.ANY),
        ],
        out_specs=pl.BlockSpec(memory_space=pltpu.VMEM),
        scratch_shapes=[
            pltpu.VMEM((PAD + EVENT_ROWS, LANES), jnp.int32),
            pltpu.VMEM((2 * PAD + EVENT_ROWS, LANES), jnp.float32),
            pltpu.VMEM((EVENT_ROWS, LANES), jnp.bfloat16),
            pltpu.VMEM((EVENT_ROWS, 6 * LANES), jnp.bfloat16),
            pltpu.VMEM((ROWS + 16, COLS), jnp.float32),
            pltpu.VMEM((WORDS, OWNED), jnp.int32),
            pltpu.VMEM((16 * WORD_BITS, COLS), jnp.bfloat16),
            pltpu.SemaphoreType.DMA,
        ],
        compiler_params=pltpu.CompilerParams(vmem_limit_bytes=VMEM_BYTES),
        interpret=interpret,
        name="sketch_part",
    )(own, other, bits)


def local(event_items, event_sessions, sketch_bits):
    def where():
        return lax.axis_index("stream"), lax.axis_index("item")

    message = pack(
        where,
        event_items.reshape(SLAB_ROWS, LANES),
        event_sessions.reshape(SLAB_ROWS, LANES),
        sketch_bits,
    )
    own = lax.all_to_all(message, "stream", 0, 0, tiled=True)
    other = lax.ppermute(own, "item", [(i, i ^ 1) for i in range(BANDS)])
    part = sketch_part(where, own, other, sketch_bits)
    rows = jnp.sum(lax.all_to_all(part, "stream", 0, 0, tiled=True), axis=0)
    spread = jnp.broadcast_to(rows[None], (BANDS,) + rows.shape)
    summed = jnp.sum(lax.all_to_all(spread, "item", 0, 0, tiled=True), axis=0)
    return summed / math.sqrt(EVENT_ROWS * LANES)


def solution(mesh):
    placed = (P("stream"), P("stream"), P(None, "item"))
    return jax.shard_map(
        local, mesh=mesh, in_specs=placed, out_specs=P("stream", None), check_vma=False
    )
```

```python
import math

import jax
import jax.numpy as jnp
from jax import lax
from jax.experimental import pallas as pl
from jax.experimental.pallas import tpu as pltpu
from jax.sharding import PartitionSpec as P

SKETCH = 256
WINDOW = 15
ROWS = 128
ROWS_DEV = 4
LANES = 128
SLABS = 32
BANDS = 8
SLAB_ROWS = 32
HALF_ROWS = SLAB_ROWS // 2
PAYLOAD = 32
EVENT_ROWS = SLABS * SLAB_ROWS
OWNED = 1024
COLS = OWNED + ROWS
WORD_BITS = 18
WORDS = 15
SLOTS = 384
PAD = 8
MARGIN_ROW, TOTAL_ROW, BITS_ROW = 24, 25, 26
QUOTA = 32
MESSAGE = 16
NONE = 255.0
VMEM_BYTES = 48 << 20


def iota(shape, axis, dtype=jnp.int32):
    out = lax.broadcasted_iota(jnp.int32, shape, axis)
    return out if dtype == jnp.int32 else out.astype(dtype)


def nt_dot(left, right):
    return lax.dot_general(
        left, right, (((1,), (1,)), ((), ())), preferred_element_type=jnp.float32
    )


def hot(mask):
    return jnp.where(mask, 1.0, 0.0)


def ppmi(count, row_margin, col_margin, pair_total):
    log_ratio = (
        jnp.log(jnp.maximum(count, 1.0))
        + jnp.log(pair_total)
        - jnp.log(jnp.maximum(row_margin, 1.0))
        - jnp.log(jnp.maximum(col_margin, 1.0))
    )
    return jnp.where(count > 0, jnp.maximum(log_ratio, 0.0), 0.0)


def split(values):
    high = values.astype(jnp.bfloat16)
    rest = values - high.astype(jnp.float32)
    mid = rest.astype(jnp.bfloat16)
    low = (rest - mid.astype(jnp.float32)).astype(jnp.bfloat16)
    return jnp.concatenate([high, mid, low], axis=0)


def joined(parts):
    third = parts.shape[0] // 3
    return parts[:third] + (parts[third : 2 * third] + parts[2 * third :])


def fill_signs(held_words, signs):
    held_words = jnp.concatenate([held_words, jnp.zeros((1, COLS), jnp.int32)], axis=0)
    for b in range(WORD_BITS):
        signs[pl.ds(b * 16, 16), :] = jnp.where((held_words >> b) & 1 == 1, 1.0, -1.0).astype(jnp.bfloat16)


def project(positive, signs):
    by_bit = joined(nt_dot(split(positive), signs[...]))
    have = iota((16 * WORD_BITS, SKETCH), 0)
    want = iota((16 * WORD_BITS, SKETCH), 1)
    order = hot((have & 15) * WORD_BITS + (have >> 4) == want).astype(jnp.bfloat16)
    return joined(jnp.dot(split(by_bit), order, preferred_element_type=jnp.float32))


def all_events_kernel(where, items_ref, sessions_ref, bits_ref, out_ref):
    _, band = where()
    half = lax.rem(band, 2)
    items, sessions = items_ref[...], sessions_ref[...]
    shape = items.shape
    row, lane = iota(shape, 0), iota(shape, 1)
    above = jnp.where(row == 0, -1, pltpu.roll(sessions, 1, 0))
    below = jnp.where(row == SLAB_ROWS - 1, -1, pltpu.roll(sessions, SLAB_ROWS - 1, 0))
    weights = jnp.zeros(shape, jnp.float32)
    for d in range(1, WINDOW + 1):
        earlier = pltpu.roll(jnp.where(lane >= LANES - d, above, sessions), d, 1)
        later = pltpu.roll(jnp.where(lane < d, below, sessions), LANES - d, 1)
        weights += hot(earlier == sessions) + hot(later == sessions)
    held = jnp.zeros((ROWS, LANES), jnp.float32)
    item_row = iota((ROWS, LANES), 0)
    for r in range(SLAB_ROWS):
        held += jnp.where(items[r : r + 1] == item_row, weights[r : r + 1], 0.0)
    margin = jnp.sum(held.T, axis=0, keepdims=True).astype(jnp.int32)
    total = jnp.sum(weights, axis=0, keepdims=True).astype(jnp.int32)
    own_items = jnp.where(half == 0, items[:HALF_ROWS], items[HALF_ROWS:])
    own_sessions = jnp.where(half == 0, sessions[:HALF_ROWS], sessions[HALF_ROWS:])
    pairs = own_sessions[:8] + own_sessions[8:] * 65536
    slab, _ = where()
    word = bits_ref[...]
    one = jnp.sum(
        jnp.where(iota(word.shape, 0) == jnp.minimum(slab, WORDS - 1), word, 0),
        axis=0,
        keepdims=True,
    )
    extra = jnp.concatenate([margin, total, one, jnp.zeros((5, LANES), jnp.int32)], axis=0)
    message = jnp.concatenate([own_items, pairs, extra], axis=0)
    for s in range(SLABS):
        out_ref[s] = message


def from_all_kernel(
    where, own_ref, other_ref, bits_hbm, out_ref,
    sess, codes, mask, table, counts, words, signs, sem,
):
    slab, band = where()
    half = lax.rem(band, 2)
    copy = pltpu.make_async_copy(
        bits_hbm.at[:, pl.ds(pl.multiple_of(slab * OWNED, OWNED), OWNED)],
        words,
        sem,
    )
    copy.start()
    lane_s = iota((SLAB_ROWS, LANES), 1)
    block_id = band * SLABS + slab
    pair_id = jnp.where(band < 2, 2 * slab + half, -1)

    edge = jnp.full((PAD, LANES), -(ROWS + 1.0), jnp.float32)
    codes[pl.ds(0, PAD), :] = edge
    codes[pl.ds(PAD + EVENT_ROWS, PAD), :] = edge
    sess[pl.ds(0, PAD), :] = jnp.full((PAD, LANES), -1, jnp.int32)

    def halves(s):
        mine, its = own_ref[s], other_ref[s]
        return jnp.where(half == 0, mine, its), jnp.where(half == 0, its, mine)

    def unpack(s, carry):
        first, second = halves(s)
        items = jnp.concatenate([first[:16], second[:16]], axis=0)
        a, b = first[16:24], second[16:24]
        sessions = jnp.concatenate([a & 65535, a >> 16, b & 65535, b >> 16], axis=0)
        base = pl.multiple_of(s * SLAB_ROWS, SLAB_ROWS)
        sess[pl.ds(PAD + base, SLAB_ROWS), :] = sessions
        above = sess[pl.ds(PAD - 1 + base, SLAB_ROWS), :]
        before = pltpu.roll(jnp.where(lane_s == LANES - 1, above, sessions), 1, 1)
        value = jnp.minimum(items, ROWS) + 1
        codes[pl.ds(PAD + base, SLAB_ROWS), :] = jnp.where(
            before != sessions, -value, value
        ).astype(jnp.float32)
        is_row = items < ROWS
        owned = jnp.where(is_row, items >> 1, items >> 10) == jnp.where(is_row, pair_id, block_id)
        ident = jnp.where(is_row, OWNED + items, items & (OWNED - 1))
        rows = pl.ds(base, SLAB_ROWS)
        mask[rows, :] = hot(owned).astype(jnp.bfloat16)
        table[rows, pl.ds(LANES, LANES)] = (ident & 255).astype(jnp.float32).astype(jnp.bfloat16)
        table[rows, pl.ds(2 * LANES, LANES)] = (ident >> 8).astype(jnp.float32).astype(jnp.bfloat16)
        return carry

    lax.fori_loop(0, SLABS, unpack, 0, unroll=4)
    for r in range(0, EVENT_ROWS, 128):
        rows = pl.ds(r, 128)
        table[rows, pl.ds(3 * LANES, LANES)] = codes[pl.ds(PAD - 1 + r, 128), :].astype(jnp.bfloat16)
        table[rows, pl.ds(4 * LANES, LANES)] = codes[pl.ds(PAD + r, 128), :].astype(jnp.bfloat16)
        table[rows, pl.ds(5 * LANES, LANES)] = codes[pl.ds(PAD + 1 + r, 128), :].astype(jnp.bfloat16)

    upto = hot(iota((LANES, LANES), 0) <= iota((LANES, LANES), 1)).astype(jnp.bfloat16)
    owned = mask[...]
    rank = jnp.dot(owned, upto, preferred_element_type=jnp.float32)
    table[:, pl.ds(0, LANES)] = (rank * owned.astype(jnp.float32)).astype(jnp.bfloat16)
    per_row = nt_dot(jnp.ones((8, LANES), jnp.bfloat16), owned)
    groups = EVENT_ROWS // LANES
    grouped = jnp.concatenate(
        [per_row[:1, g * LANES : (g + 1) * LANES] for g in range(groups)], axis=0
    )
    inside = jnp.dot(grouped.astype(jnp.bfloat16), upto, preferred_element_type=jnp.float32)
    ends, starts, base = [], [], jnp.zeros((1, 1), jnp.float32)
    for g in range(groups):
        ends.append(inside[g : g + 1] + base)
        starts.append(ends[g] - grouped[g : g + 1])
        base = base + inside[g : g + 1, LANES - 1 :]
    owned_events = jnp.max(base).astype(jnp.int32)

    counts[...] = jnp.zeros(counts.shape, jnp.float32)
    lane_f = iota((SLOTS, LANES), 1, jnp.float32)
    row32, col32 = iota((32, 32), 0), iota((32, 32), 1)
    ahead = (row32 > WINDOW) & (col32 > WINDOW) & (col32 <= row32)
    behind = (row32 < WINDOW) & (col32 > row32) & (col32 <= WINDOW)
    between = hot(ahead | behind).astype(jnp.bfloat16)
    place = iota((32, SLOTS), 0)
    in_window = (place != WINDOW) & (place <= 2 * WINDOW)
    row_ids = iota((ROWS, SLOTS), 0, jnp.float32)
    col_ids = iota((SLOTS, COLS), 1, jnp.float32)

    def chunk(step, carry):
        slot = (step * SLOTS + iota((SLOTS, LANES), 0)).astype(jnp.float32)
        picks, first = [], jnp.zeros((SLOTS, LANES), jnp.float32)
        for g in range(groups):
            here = (slot >= starts[g]) & (slot < ends[g])
            first += jnp.where(here, starts[g], 0.0)
            picks.append(hot(here).astype(jnp.bfloat16))
        pick = jnp.concatenate(picks, axis=1)
        got = jnp.dot(pick, table[...], preferred_element_type=jnp.float32)
        ordinal = slot[:, :1] + 1.0 - jnp.sum(first, axis=1, keepdims=True)
        chosen = got[:, :LANES] == ordinal
        ident = got[:, LANES : 2 * LANES] + 256.0 * got[:, 2 * LANES : 3 * LANES]
        column = jnp.sum(jnp.where(chosen, ident + 1.0, 0.0), axis=1, keepdims=True) - 1.0
        at_lane = jnp.sum(jnp.where(chosen, lane_f, 0.0), axis=1, keepdims=True)
        source = at_lane.astype(jnp.int32) + (iota((SLOTS, LANES), 1) - WINDOW)
        index = source & (LANES - 1)
        parts = [
            jnp.take_along_axis(got[:, k * LANES : (k + 1) * LANES], index, axis=1, mode="promise_in_bounds")
            for k in (3, 4, 5)
        ]
        window = jnp.where(source < 0, parts[0], jnp.where(source < LANES, parts[1], parts[2]))
        window = window.T[:32]
        breaks = hot(window < 0.0).astype(jnp.bfloat16)
        crossed = jnp.dot(between, breaks, preferred_element_type=jnp.float32)
        linked = (crossed == 0.0) & in_window
        near = jnp.where(linked, jnp.abs(window) - 1.0, 255.0)
        weight = jnp.sum(hot(linked), axis=0, keepdims=True)
        pairs = jnp.zeros((ROWS, SLOTS), jnp.float32)
        for d in range(2 * WINDOW + 1):
            if d != WINDOW:
                pairs += hot(near[d : d + 1] == row_ids)
        pairs = jnp.concatenate([pairs, jnp.broadcast_to(weight, (16, SLOTS))], axis=0)
        column_hot = hot(column == col_ids).astype(jnp.bfloat16)
        counts[...] += jnp.dot(
            pairs.astype(jnp.bfloat16), column_hot, preferred_element_type=jnp.float32
        )
        return carry

    lax.fori_loop(0, (owned_events + SLOTS - 1) // SLOTS, chunk, 0)

    def both(row_first, row_second):
        mine_f, its_f = own_ref[:, row_first, :], other_ref[:, row_first, :]
        mine_s, its_s = own_ref[:, row_second, :], other_ref[:, row_second, :]
        return jnp.where(half == 0, mine_f, its_f), jnp.where(half == 0, its_s, mine_s)

    start_items, end_items = both(0, 15)
    start_sess, end_sess = both(16, 23)
    start_sess, end_sess = start_sess & 65535, end_sess >> 16
    slab_row = iota((SLABS, LANES), 0)
    end_items = pltpu.roll(end_items, 1, 0)
    end_sess = jnp.where(slab_row == 0, -1, pltpu.roll(end_sess, 1, 0))
    cross = jnp.zeros((SLABS, LANES), jnp.float32)
    lane = iota((SLABS, LANES), 1)
    for d in range(1, WINDOW + 1):
        before = pltpu.roll(end_sess, d, 1)
        after = pltpu.roll(start_sess, LANES - d, 1)
        cross += hot((lane < d) & (before == start_sess))
        cross += hot((lane >= LANES - d) & (after == end_sess))
    cross_items = jnp.where(lane < LANES // 2, start_items, end_items)
    margins = jnp.sum(own_ref[:, MARGIN_ROW, :], axis=0, keepdims=True).astype(jnp.float32)
    item_row = iota((ROWS, LANES), 0)
    held = jnp.where(item_row == iota((ROWS, LANES), 1), margins, 0.0)
    for s in range(SLABS):
        held += jnp.where(cross_items[s : s + 1] == item_row, cross[s : s + 1], 0.0)
    row_margin = jnp.sum(held, axis=1, keepdims=True)
    totals = jnp.sum(own_ref[:, TOTAL_ROW, :], axis=0, keepdims=True).astype(jnp.float32)
    totals = totals + jnp.sum(cross, axis=0, keepdims=True)
    pair_total = jnp.sum(totals, axis=1, keepdims=True)

    positive = ppmi(
        counts[pl.ds(0, ROWS), :], row_margin, counts[pl.ds(ROWS, 1), :], pair_total
    )
    copy.wait()
    row_words = jnp.where(half == 0, own_ref[:WORDS, BITS_ROW, :], other_ref[:WORDS, BITS_ROW, :])
    fill_signs(jnp.concatenate([words[...], row_words], axis=1), signs)
    result = project(positive, signs)
    for s in range(SLABS):
        out_ref[s] = result[s * ROWS_DEV : (s + 1) * ROWS_DEV]


def all_events(where, items, sessions, bits, interpret=False):
    return pl.pallas_call(
        lambda *refs: all_events_kernel(where, *refs),
        out_shape=jax.ShapeDtypeStruct((SLABS, PAYLOAD, LANES), jnp.int32),
        grid=(1,),
        in_specs=[
            pl.BlockSpec((SLAB_ROWS, LANES), lambda i: (0, 0)),
            pl.BlockSpec((SLAB_ROWS, LANES), lambda i: (0, 0)),
            pl.BlockSpec((WORDS, LANES), lambda i: (0, 0)),
        ],
        out_specs=pl.BlockSpec((SLABS, PAYLOAD, LANES), lambda i: (0, 0, 0)),
        compiler_params=pltpu.CompilerParams(vmem_limit_bytes=VMEM_BYTES),
        interpret=interpret,
        name="all_events",
    )(items, sessions, bits)


def from_all(where, own, other, bits, interpret=False):
    return pl.pallas_call(
        lambda *refs: from_all_kernel(where, *refs),
        out_shape=jax.ShapeDtypeStruct((SLABS, ROWS_DEV, SKETCH), jnp.float32),
        in_specs=[
            pl.BlockSpec(memory_space=pltpu.VMEM),
            pl.BlockSpec(memory_space=pltpu.VMEM),
            pl.BlockSpec(memory_space=pl.ANY),
        ],
        out_specs=pl.BlockSpec(memory_space=pltpu.VMEM),
        scratch_shapes=[
            pltpu.VMEM((PAD + EVENT_ROWS, LANES), jnp.int32),
            pltpu.VMEM((2 * PAD + EVENT_ROWS, LANES), jnp.float32),
            pltpu.VMEM((EVENT_ROWS, LANES), jnp.bfloat16),
            pltpu.VMEM((EVENT_ROWS, 6 * LANES), jnp.bfloat16),
            pltpu.VMEM((ROWS + 16, COLS), jnp.float32),
            pltpu.VMEM((WORDS, OWNED), jnp.int32),
            pltpu.VMEM((16 * WORD_BITS, COLS), jnp.bfloat16),
            pltpu.SemaphoreType.DMA,
        ],
        compiler_params=pltpu.CompilerParams(vmem_limit_bytes=VMEM_BYTES),
        interpret=interpret,
        name="from_all",
    )(own, other, bits)


def route_kernel(where, items_hbm, sessions_hbm, out_ref, items_v, sessions_v, codes, table, near_rows, one_hots, pair_rows, sems):
    slab, band = where()
    get_items = pltpu.make_async_copy(items_hbm, items_v, sems.at[0])
    get_sessions = pltpu.make_async_copy(sessions_hbm, sessions_v, sems.at[1])
    get_items.start()
    get_sessions.start()
    get_items.wait()
    get_sessions.wait()
    items, sessions = items_v[...], sessions_v[...]
    shape = items.shape
    row, lane = iota(shape, 0), iota(shape, 1)
    above = jnp.where(row == 0, -1, pltpu.roll(sessions, 1, 0))
    below = jnp.where(row == SLAB_ROWS - 1, -1, pltpu.roll(sessions, SLAB_ROWS - 1, 0))
    earlier_links = jnp.zeros(shape, jnp.float32)
    later_links = jnp.zeros(shape, jnp.float32)
    for d in range(1, WINDOW + 1):
        earlier = pltpu.roll(jnp.where(lane >= LANES - d, above, sessions), d, 1)
        later = pltpu.roll(jnp.where(lane < d, below, sessions), LANES - d, 1)
        earlier_links += hot(earlier == sessions)
        later_links += hot(later == sessions)
    weights = earlier_links + later_links

    held = jnp.zeros((ROWS, LANES), jnp.float32)
    item_row = iota((ROWS, LANES), 0)
    for r in range(SLAB_ROWS):
        same = items[r : r + 1] == item_row
        held += jnp.where(same, weights[r : r + 1], 0.0)
        one_hots[:, pl.ds(r * LANES, LANES)] = hot(same).astype(jnp.bfloat16)
    margin = jnp.sum(held.T, axis=0, keepdims=True)
    total = jnp.sum(weights, axis=0, keepdims=True)
    first_link = iota(shape, 1, jnp.float32) - earlier_links
    place = iota((2 * LANES, LANES), 0, jnp.float32) - LANES
    self_place = iota((2 * LANES, LANES), 1, jnp.float32)
    sooner = place < self_place
    for r in range(SLAB_ROWS):
        links = hot(sooner & (place >= first_link[r : r + 1])).astype(jnp.bfloat16)
        if r == 0:
            pairs = jnp.dot(one_hots[:, pl.ds(0, LANES)], links[LANES:], preferred_element_type=jnp.float32)
        else:
            pairs = jnp.dot(
                one_hots[:, pl.ds((r - 1) * LANES, 2 * LANES)], links, preferred_element_type=jnp.float32
            )
        pair_rows[:, pl.ds(r * LANES, LANES)] = pairs.astype(jnp.bfloat16)
    ordered = nt_dot(pair_rows[...], one_hots[...])
    row_pairs = ordered + ordered.T

    before = pltpu.roll(jnp.where(lane == LANES - 1, above, sessions), 1, 1)
    value = jnp.minimum(items, ROWS) + 1
    edge = jnp.full((PAD, LANES), -(ROWS + 1.0), jnp.float32)
    codes[pl.ds(0, PAD), :] = edge
    codes[pl.ds(PAD + SLAB_ROWS, PAD), :] = edge
    codes[pl.ds(PAD, SLAB_ROWS), :] = jnp.where(before != sessions, -value, value).astype(jnp.float32)
    inside = items - band * (SLABS * OWNED)
    wide = (items >= ROWS) & (inside >= 0) & (inside < SLABS * OWNED)
    inside = jnp.where(wide, inside, 0)
    owner = jnp.where(wide, inside >> 10, -1)
    owner_row = iota((SLABS, LANES), 0)
    marks = [hot(owner[r : r + 1] == owner_row) for r in range(SLAB_ROWS)]
    upto = hot(iota((LANES, LANES), 0) <= iota((LANES, LANES), 1)).astype(jnp.bfloat16)
    ranks = jnp.dot(
        jnp.concatenate(marks, axis=0).astype(jnp.bfloat16), upto, preferred_element_type=jnp.float32
    )
    ranks = [ranks[r * SLABS : (r + 1) * SLABS] for r in range(SLAB_ROWS)]
    per_row = jnp.zeros((SLABS, LANES), jnp.float32)
    for r in range(SLAB_ROWS):
        per_row = jnp.where(lane == r, ranks[r][:, LANES - 1 :], per_row)
    ends = jnp.dot(per_row.astype(jnp.bfloat16), upto, preferred_element_type=jnp.float32)
    starts = ends - per_row
    most = jnp.max(ends[:, LANES - 1 :], axis=0, keepdims=True)
    orders = [
        jnp.sum(marks[r] * (ranks[r] + starts[:, r : r + 1]), axis=0, keepdims=True)
        for r in range(SLAB_ROWS)
    ]
    table[pl.ds(SLAB_ROWS, LANES - SLAB_ROWS), :] = jnp.zeros((LANES - SLAB_ROWS, 6 * LANES), jnp.bfloat16)
    fields = [
        jnp.minimum(jnp.concatenate(orders, axis=0), 255.0),
        (inside & 255).astype(jnp.float32),
        (inside >> 8).astype(jnp.float32),
        codes[pl.ds(PAD - 1, SLAB_ROWS), :],
        codes[pl.ds(PAD, SLAB_ROWS), :],
        codes[pl.ds(PAD + 1, SLAB_ROWS), :],
    ]
    for k, field in enumerate(fields):
        table[pl.ds(0, SLAB_ROWS), pl.ds(k * LANES, LANES)] = field.astype(jnp.bfloat16)
    slot = iota((QUOTA, LANES), 0, jnp.float32)
    picks = [
        hot((slot >= starts[s : s + 1]) & (slot < ends[s : s + 1])).astype(jnp.bfloat16)
        for s in range(SLABS)
    ]
    got = jnp.dot(jnp.concatenate(picks, axis=0), table[...], preferred_element_type=jnp.float32)
    big = (SLABS * QUOTA, LANES)
    number, lanes = iota(big, 0), iota(big, 1)
    target = (number >> 5).astype(jnp.float32) * 4.0
    high = got[:, 2 * LANES : 3 * LANES] - target
    ordinal = ((number & (QUOTA - 1)) + 1).astype(jnp.float32)
    chosen = (got[:, :LANES] == ordinal) & (high >= 0.0) & (high < 4.0)
    ident = got[:, LANES : 2 * LANES] + 256.0 * high
    column = jnp.sum(jnp.where(chosen, ident + 1.0, 0.0), axis=1, keepdims=True) - 1.0
    at_lane = jnp.sum(jnp.where(chosen, lanes.astype(jnp.float32), 0.0), axis=1, keepdims=True)
    source = at_lane.astype(jnp.int32) + (lanes - WINDOW)
    index = source & (LANES - 1)
    parts = [
        jnp.take_along_axis(got[:, k * LANES : (k + 1) * LANES], index, axis=1, mode="promise_in_bounds")
        for k in (3, 4, 5)
    ]
    window = jnp.where(source < 0, parts[0], jnp.where(source < LANES, parts[1], parts[2]))
    from_lane, to_lane = iota((LANES, LANES), 0), iota((LANES, LANES), 1)
    ahead = (to_lane > WINDOW) & (from_lane > WINDOW) & (from_lane <= to_lane)
    behind = (to_lane < WINDOW) & (from_lane > to_lane) & (from_lane <= WINDOW)
    between = hot(ahead | behind).astype(jnp.bfloat16)
    crossed = jnp.dot(
        hot(window < 0.0).astype(jnp.bfloat16), between, preferred_element_type=jnp.float32
    )
    linked = (crossed == 0.0) & (lanes <= 2 * WINDOW)
    near = jnp.where(linked, jnp.abs(window) - 1.0, NONE)
    near_rows[...] = jnp.where(lanes == WINDOW, column, near)

    ends_lane = iota((1, LANES), 1)
    spare = jnp.where(most > QUOTA, 1.0, 0.0)
    edge_items = jnp.where(ends_lane < LANES // 2, items[:1], items[SLAB_ROWS - 1 :]).astype(jnp.float32)
    edge_items = jnp.where(ends_lane == LANES // 2, spare, edge_items)
    edge_sessions = jnp.where(
        ends_lane < LANES // 2, sessions[:1], sessions[SLAB_ROWS - 1 :]
    ).astype(jnp.float32)
    common = jnp.concatenate([margin, total, edge_items, edge_sessions], axis=0)
    quarter = iota((8, LANES), 1) >> 5
    for s in range(SLABS):
        rows = near_rows[pl.ds(s * QUOTA, 8), :]
        for g in range(1, QUOTA // 8):
            part = pltpu.roll(near_rows[pl.ds(s * QUOTA + 8 * g, 8), :], 32 * g, 1)
            rows = jnp.where(quarter == g, part, rows)
        out_ref[s, pl.ds(0, 8), :] = rows
        out_ref[s, pl.ds(8, 8), :] = jnp.concatenate(
            [row_pairs[s * ROWS_DEV : (s + 1) * ROWS_DEV], common], axis=0
        )


def count_pairs(near, skip):
    slots = near.shape[1]
    row_ids = iota((ROWS, slots), 0, jnp.float32)
    pairs = jnp.zeros((ROWS, slots), jnp.float32)
    for d in range(near.shape[0]):
        if d not in skip:
            pairs += hot(near[d : d + 1] == row_ids)
    place = iota(near.shape, 0)
    real = near < NONE
    for d in skip:
        real = real & (place != d)
    weight = jnp.sum(hot(real), axis=0, keepdims=True)
    return jnp.concatenate([pairs, jnp.broadcast_to(weight, (16, slots))], axis=0).astype(jnp.bfloat16)


def sketch_kernel(where, got_ref, row_bits_ref, bits_hbm, out_ref, counts, table, words, signs, sem):
    slab, band = where()
    copy = pltpu.make_async_copy(
        bits_hbm.at[:, pl.ds(pl.multiple_of(slab * OWNED, OWNED), OWNED)], words, sem
    )
    copy.start()

    windows = got_ref[:, :8, :].reshape(SLABS * 8, LANES).T
    blocks, idents = [], []
    for g in range(QUOTA // 8):
        near = windows[32 * g : 32 * g + 32]
        idents.append(near[WINDOW : WINDOW + 1])
        blocks.append(count_pairs(near, (WINDOW, 31)))
    ident = jnp.concatenate(idents, axis=1)
    pairs = jnp.concatenate(blocks, axis=1)
    column_hot = hot(ident == iota((OWNED, ident.shape[1]), 0, jnp.float32)).astype(jnp.bfloat16)
    counts[:, pl.ds(0, OWNED)] = nt_dot(pairs, column_hot)

    edge_items, edge_sessions = got_ref[:, 14, :], got_ref[:, 15, :]
    overflow = jnp.max(edge_items[:, LANES // 2 : LANES // 2 + 1], axis=0, keepdims=True)
    slab_row, lane = iota((SLABS, LANES), 0), iota((SLABS, LANES), 1)
    end_items = pltpu.roll(edge_items, 1, 0)
    end_sess = jnp.where(slab_row == 0, -1.0, pltpu.roll(edge_sessions, 1, 0))
    cross = jnp.zeros((SLABS, LANES), jnp.float32)
    for d in range(1, WINDOW + 1):
        before = pltpu.roll(end_sess, d, 1)
        after = pltpu.roll(edge_sessions, LANES - d, 1)
        cross += hot((lane < d) & (before == edge_sessions))
        cross += hot((lane >= LANES - d) & (after == end_sess))
    items = jnp.where(lane < LANES // 2, edge_items, end_items)
    over = jnp.where(
        lane < LANES // 2,
        hot((edge_sessions == end_sess[:, LANES - 1 :]) & (lane < WINDOW)),
        hot((end_sess == edge_sessions[:, :1]) & (lane >= LANES - WINDOW)),
    )
    partner = jnp.where(over > 0.0, jnp.minimum(items, float(ROWS)), NONE)
    whole = items.astype(jnp.int32)
    is_row = whole < ROWS
    row_owner = jnp.where(band == 0, slab, -1)
    owned = jnp.where(is_row, whole >> 2, whole >> 10) == jnp.where(is_row, row_owner, band * SLABS + slab)
    owned = hot(owned & (cross > 0.0))
    local_id = jnp.where(is_row, OWNED + whole, whole & (OWNED - 1))
    upto = hot(iota((LANES, LANES), 0) <= iota((LANES, LANES), 1)).astype(jnp.bfloat16)
    blank = jnp.zeros((LANES - SLABS, LANES), jnp.float32)
    marks = jnp.concatenate([owned, blank], axis=0).astype(jnp.bfloat16)
    rank = jnp.dot(marks, upto, preferred_element_type=jnp.float32)
    per_row = nt_dot(jnp.ones((8, LANES), jnp.bfloat16), marks)
    ends = jnp.dot(per_row.astype(jnp.bfloat16), upto, preferred_element_type=jnp.float32)
    starts = (ends - per_row)[:1]
    ends = ends[:1]
    crossing = jnp.max(ends).astype(jnp.int32)
    table[...] = jnp.zeros(table.shape, jnp.bfloat16)
    fields = [
        rank[:SLABS] * owned,
        (local_id & 255).astype(jnp.float32),
        (local_id >> 8).astype(jnp.float32),
        partner,
    ]
    for k, field in enumerate(fields):
        table[pl.ds(0, SLABS), pl.ds(k * LANES, LANES)] = field.astype(jnp.bfloat16)

    mine = jnp.sum(got_ref[:, 8:12, :], axis=0)
    item_row, item_lane = iota((ROWS, LANES), 0), iota((ROWS, LANES), 1)
    placed = jnp.zeros((ROWS, LANES), jnp.float32)
    for q in range(ROWS_DEV):
        placed = jnp.where(item_row == row_owner * ROWS_DEV + q, mine[q : q + 1], placed)
    counts[pl.ds(0, ROWS), pl.ds(OWNED, ROWS)] = placed.T
    counts[pl.ds(ROWS, 16), pl.ds(OWNED, ROWS)] = jnp.zeros((16, ROWS), jnp.float32)

    slot_lane = iota((LANES, LANES), 1)
    col_ids = iota((LANES, COLS), 1, jnp.float32)

    def chunk(step, carry):
        slot = (step * LANES + iota((LANES, LANES), 0)).astype(jnp.float32)
        here = (slot >= starts) & (slot < ends)
        first = jnp.sum(jnp.where(here, starts, 0.0), axis=1, keepdims=True)
        got = jnp.dot(hot(here).astype(jnp.bfloat16), table[...], preferred_element_type=jnp.float32)
        chosen = got[:, :LANES] == slot[:, :1] + 1.0 - first
        ident = got[:, LANES : 2 * LANES] + 256.0 * got[:, 2 * LANES : 3 * LANES]
        column = jnp.sum(jnp.where(chosen, ident + 1.0, 0.0), axis=1, keepdims=True) - 1.0
        at = jnp.sum(jnp.where(chosen, slot_lane, 0), axis=1, keepdims=True)
        reach = LANES - WINDOW
        other_side = jnp.where(
            at < LANES // 2, hot(slot_lane >= reach + at), hot(slot_lane <= at - reach)
        )
        near = jnp.where(other_side > 0.0, got[:, 3 * LANES :], NONE).T
        near = jnp.concatenate([near[:16], near[LANES - 16 :]], axis=0)
        pairs = count_pairs(near, (15, 16))
        column_hot = hot(column == col_ids).astype(jnp.bfloat16)
        counts[...] += jnp.dot(pairs, column_hot, preferred_element_type=jnp.float32)
        return carry

    lax.fori_loop(0, (crossing + LANES - 1) // LANES, chunk, 0)

    margins = jnp.sum(got_ref[:, 12, :], axis=0, keepdims=True)
    held = jnp.where(item_row == item_lane, margins, 0.0)
    item_rows = item_row.astype(jnp.float32)
    for s in range(SLABS):
        held += jnp.where(items[s : s + 1] == item_rows, cross[s : s + 1], 0.0)
    row_margin = jnp.sum(held, axis=1, keepdims=True)
    totals = jnp.sum(got_ref[:, 13, :], axis=0, keepdims=True) + jnp.sum(cross, axis=0, keepdims=True)
    pair_total = jnp.sum(totals, axis=1, keepdims=True)
    col_margin = jnp.concatenate(
        [counts[pl.ds(ROWS, 1), pl.ds(0, OWNED)], jnp.sum(held.T, axis=0, keepdims=True)], axis=1
    )
    positive = ppmi(counts[pl.ds(0, ROWS), :], row_margin, col_margin, pair_total)
    copy.wait()
    fill_signs(jnp.concatenate([words[...], row_bits_ref[...]], axis=1), signs)
    result = project(positive, signs)
    result = jnp.where(overflow > 0.0, jnp.nan, result)
    for s in range(SLABS):
        out_ref[s] = result[s * ROWS_DEV : (s + 1) * ROWS_DEV]


def route(where, items, sessions, interpret=False):
    return pl.pallas_call(
        lambda *refs: route_kernel(where, *refs),
        out_shape=jax.ShapeDtypeStruct((SLABS, MESSAGE, LANES), jnp.float32),
        in_specs=[pl.BlockSpec(memory_space=pltpu.HBM)] * 2,
        out_specs=pl.BlockSpec(memory_space=pltpu.VMEM),
        scratch_shapes=[
            pltpu.VMEM((SLAB_ROWS, LANES), jnp.int32),
            pltpu.VMEM((SLAB_ROWS, LANES), jnp.int32),
            pltpu.VMEM((2 * PAD + SLAB_ROWS, LANES), jnp.float32),
            pltpu.VMEM((LANES, 6 * LANES), jnp.bfloat16),
            pltpu.VMEM((SLABS * QUOTA, LANES), jnp.float32),
            pltpu.VMEM((ROWS, SLAB_ROWS * LANES), jnp.bfloat16),
            pltpu.VMEM((ROWS, SLAB_ROWS * LANES), jnp.bfloat16),
            pltpu.SemaphoreType.DMA((2,)),
        ],
        compiler_params=pltpu.CompilerParams(vmem_limit_bytes=VMEM_BYTES),
        interpret=interpret,
        name="route_events",
    )(items, sessions)


def sketch_part(where, got, bits, interpret=False):
    return pl.pallas_call(
        lambda *refs: sketch_kernel(where, *refs),
        out_shape=jax.ShapeDtypeStruct((SLABS, ROWS_DEV, SKETCH), jnp.float32),
        grid=(1,),
        in_specs=[
            pl.BlockSpec((SLABS, MESSAGE, LANES), lambda i: (0, 0, 0)),
            pl.BlockSpec((WORDS, LANES), lambda i: (0, 0)),
            pl.BlockSpec(memory_space=pltpu.HBM),
        ],
        out_specs=pl.BlockSpec((SLABS, ROWS_DEV, SKETCH), lambda i: (0, 0, 0)),
        scratch_shapes=[
            pltpu.VMEM((ROWS + 16, COLS), jnp.float32),
            pltpu.VMEM((LANES, 4 * LANES), jnp.bfloat16),
            pltpu.VMEM((WORDS, OWNED), jnp.int32),
            pltpu.VMEM((16 * WORD_BITS, COLS), jnp.bfloat16),
            pltpu.SemaphoreType.DMA,
        ],
        compiler_params=pltpu.CompilerParams(vmem_limit_bytes=VMEM_BYTES),
        interpret=interpret,
        name="sketch_part",
    )(got, bits, bits)


def reduced(part):
    rows = jnp.sum(lax.all_to_all(part, "stream", 0, 0, tiled=True), axis=0)
    spread = jnp.broadcast_to(rows[None], (BANDS,) + rows.shape)
    summed = jnp.sum(lax.all_to_all(spread, "item", 0, 0, tiled=True), axis=0)
    return summed / math.sqrt(EVENT_ROWS * LANES)


def local(event_items, event_sessions, sketch_bits):
    def where():
        return lax.axis_index("stream"), lax.axis_index("item")

    items = event_items.reshape(SLAB_ROWS, LANES)
    sessions = event_sessions.reshape(SLAB_ROWS, LANES)

    def from_every_event(_):
        message = all_events(where, items, sessions, sketch_bits)
        own = lax.all_to_all(message, "stream", 0, 0, tiled=True)
        other = lax.ppermute(own, "item", [(i, i ^ 1) for i in range(BANDS)])
        return reduced(from_all(where, own, other, sketch_bits))

    routed = lax.all_to_all(route(where, items, sessions), "stream", 0, 0, tiled=True)
    result = reduced(sketch_part(where, routed, sketch_bits))
    return lax.cond(jnp.isnan(result[0, 0]), from_every_event, lambda kept: kept, result)


def solution(mesh):
    placed = (P("stream"), P("stream"), P(None, "item"))
    return jax.shard_map(
        local, mesh=mesh, in_specs=placed, out_specs=P("stream", None), check_vma=False
    )
```

```python
import math

import jax
import jax.numpy as jnp
from jax import lax
from jax.experimental import pallas as pl
from jax.experimental.pallas import tpu as pltpu
from jax.sharding import PartitionSpec as P

SKETCH = 256
WINDOW = 15
ROWS = 128
ROWS_DEV = 4
LANES = 128
SLABS = 32
BANDS = 8
SLAB_ROWS = 32
HALF_ROWS = SLAB_ROWS // 2
PAYLOAD = 32
EVENT_ROWS = SLABS * SLAB_ROWS
OWNED = 1024
COLS = OWNED + ROWS
WORD_BITS = 18
WORDS = 15
SLOTS = 384
PAD = 8
MARGIN_ROW, TOTAL_ROW, BITS_ROW = 24, 25, 26
QUOTA = 32
MESSAGE = 8
HALF = LANES // 2
NONE = 255.0
NOBODY = 4095.0
SPOT = HALF + 16
VMEM_BYTES = 48 << 20
COUNT = jnp.bfloat16


def iota(shape, axis, dtype=jnp.int32):
    out = lax.broadcasted_iota(jnp.int32, shape, axis)
    return out if dtype == jnp.int32 else out.astype(dtype)


def nt_dot(left, right):
    return lax.dot_general(
        left, right, (((1,), (1,)), ((), ())), preferred_element_type=jnp.float32
    )


def hot(mask):
    return jnp.where(mask, 1.0, 0.0)


def ppmi(count, row_margin, col_margin, pair_total):
    log_ratio = (
        jnp.log(jnp.maximum(count, 1.0))
        + jnp.log(pair_total)
        - jnp.log(jnp.maximum(row_margin, 1.0))
        - jnp.log(jnp.maximum(col_margin, 1.0))
    )
    return jnp.where(count > 0, jnp.maximum(log_ratio, 0.0), 0.0)


def split(values):
    high = values.astype(jnp.bfloat16)
    rest = values - high.astype(jnp.float32)
    mid = rest.astype(jnp.bfloat16)
    low = (rest - mid.astype(jnp.float32)).astype(jnp.bfloat16)
    return jnp.concatenate([high, mid, low], axis=0)


def two_parts(values):
    high = values.astype(jnp.bfloat16)
    low = (values - high.astype(jnp.float32)).astype(jnp.bfloat16)
    return jnp.concatenate([high, low], axis=0)


def joined(parts):
    third = parts.shape[0] // 3
    return parts[:third] + (parts[third : 2 * third] + parts[2 * third :])


def fill_signs(held_words, signs):
    held_words = jnp.concatenate([held_words, jnp.zeros((1, COLS), jnp.int32)], axis=0)
    for b in range(WORD_BITS):
        signs[pl.ds(b * 16, 16), :] = jnp.where((held_words >> b) & 1 == 1, 1.0, -1.0).astype(jnp.bfloat16)


def project(positive, signs):
    by_bit = joined(nt_dot(split(positive), signs[...]))
    have = iota((16 * WORD_BITS, SKETCH), 0)
    want = iota((16 * WORD_BITS, SKETCH), 1)
    order = hot((have & 15) * WORD_BITS + (have >> 4) == want).astype(jnp.bfloat16)
    return joined(jnp.dot(split(by_bit), order, preferred_element_type=jnp.float32))


def all_events_kernel(where, items_ref, sessions_ref, bits_ref, out_ref):
    _, band = where()
    half = lax.rem(band, 2)
    items, sessions = items_ref[...], sessions_ref[...]
    shape = items.shape
    row, lane = iota(shape, 0), iota(shape, 1)
    above = jnp.where(row == 0, -1, pltpu.roll(sessions, 1, 0))
    below = jnp.where(row == SLAB_ROWS - 1, -1, pltpu.roll(sessions, SLAB_ROWS - 1, 0))
    weights = jnp.zeros(shape, jnp.float32)
    for d in range(1, WINDOW + 1):
        earlier = pltpu.roll(jnp.where(lane >= LANES - d, above, sessions), d, 1)
        later = pltpu.roll(jnp.where(lane < d, below, sessions), LANES - d, 1)
        weights += hot(earlier == sessions) + hot(later == sessions)
    held = jnp.zeros((ROWS, LANES), jnp.float32)
    item_row = iota((ROWS, LANES), 0)
    for r in range(SLAB_ROWS):
        held += jnp.where(items[r : r + 1] == item_row, weights[r : r + 1], 0.0)
    margin = jnp.sum(held.T, axis=0, keepdims=True).astype(jnp.int32)
    total = jnp.sum(weights, axis=0, keepdims=True).astype(jnp.int32)
    own_items = jnp.where(half == 0, items[:HALF_ROWS], items[HALF_ROWS:])
    own_sessions = jnp.where(half == 0, sessions[:HALF_ROWS], sessions[HALF_ROWS:])
    pairs = own_sessions[:8] + own_sessions[8:] * 65536
    slab, _ = where()
    word = bits_ref[...]
    one = jnp.sum(
        jnp.where(iota(word.shape, 0) == jnp.minimum(slab, WORDS - 1), word, 0),
        axis=0,
        keepdims=True,
    )
    extra = jnp.concatenate([margin, total, one, jnp.zeros((5, LANES), jnp.int32)], axis=0)
    message = jnp.concatenate([own_items, pairs, extra], axis=0)
    for s in range(SLABS):
        out_ref[s] = message


def from_all_kernel(
    where, own_ref, other_ref, bits_hbm, out_ref,
    sess, codes, mask, table, counts, words, signs, sem,
):
    slab, band = where()
    half = lax.rem(band, 2)
    copy = pltpu.make_async_copy(
        bits_hbm.at[:, pl.ds(pl.multiple_of(slab * OWNED, OWNED), OWNED)],
        words,
        sem,
    )
    copy.start()
    lane_s = iota((SLAB_ROWS, LANES), 1)
    block_id = band * SLABS + slab
    pair_id = jnp.where(band < 2, 2 * slab + half, -1)

    edge = jnp.full((PAD, LANES), -(ROWS + 1.0), jnp.float32)
    codes[pl.ds(0, PAD), :] = edge
    codes[pl.ds(PAD + EVENT_ROWS, PAD), :] = edge
    sess[pl.ds(0, PAD), :] = jnp.full((PAD, LANES), -1, jnp.int32)

    def halves(s):
        mine, its = own_ref[s], other_ref[s]
        return jnp.where(half == 0, mine, its), jnp.where(half == 0, its, mine)

    def unpack(s, carry):
        first, second = halves(s)
        items = jnp.concatenate([first[:16], second[:16]], axis=0)
        a, b = first[16:24], second[16:24]
        sessions = jnp.concatenate([a & 65535, a >> 16, b & 65535, b >> 16], axis=0)
        base = pl.multiple_of(s * SLAB_ROWS, SLAB_ROWS)
        sess[pl.ds(PAD + base, SLAB_ROWS), :] = sessions
        above = sess[pl.ds(PAD - 1 + base, SLAB_ROWS), :]
        before = pltpu.roll(jnp.where(lane_s == LANES - 1, above, sessions), 1, 1)
        value = jnp.minimum(items, ROWS) + 1
        codes[pl.ds(PAD + base, SLAB_ROWS), :] = jnp.where(
            before != sessions, -value, value
        ).astype(jnp.float32)
        is_row = items < ROWS
        owned = jnp.where(is_row, items >> 1, items >> 10) == jnp.where(is_row, pair_id, block_id)
        ident = jnp.where(is_row, OWNED + items, items & (OWNED - 1))
        rows = pl.ds(base, SLAB_ROWS)
        mask[rows, :] = hot(owned).astype(jnp.bfloat16)
        table[rows, pl.ds(LANES, LANES)] = (ident & 255).astype(jnp.float32).astype(jnp.bfloat16)
        table[rows, pl.ds(2 * LANES, LANES)] = (ident >> 8).astype(jnp.float32).astype(jnp.bfloat16)
        return carry

    lax.fori_loop(0, SLABS, unpack, 0, unroll=4)
    for r in range(0, EVENT_ROWS, 128):
        rows = pl.ds(r, 128)
        table[rows, pl.ds(3 * LANES, LANES)] = codes[pl.ds(PAD - 1 + r, 128), :].astype(jnp.bfloat16)
        table[rows, pl.ds(4 * LANES, LANES)] = codes[pl.ds(PAD + r, 128), :].astype(jnp.bfloat16)
        table[rows, pl.ds(5 * LANES, LANES)] = codes[pl.ds(PAD + 1 + r, 128), :].astype(jnp.bfloat16)

    upto = hot(iota((LANES, LANES), 0) <= iota((LANES, LANES), 1)).astype(jnp.bfloat16)
    owned = mask[...]
    rank = jnp.dot(owned, upto, preferred_element_type=jnp.float32)
    table[:, pl.ds(0, LANES)] = (rank * owned.astype(jnp.float32)).astype(jnp.bfloat16)
    per_row = nt_dot(jnp.ones((8, LANES), jnp.bfloat16), owned)
    groups = EVENT_ROWS // LANES
    grouped = jnp.concatenate(
        [per_row[:1, g * LANES : (g + 1) * LANES] for g in range(groups)], axis=0
    )
    inside = jnp.dot(grouped.astype(jnp.bfloat16), upto, preferred_element_type=jnp.float32)
    ends, starts, base = [], [], jnp.zeros((1, 1), jnp.float32)
    for g in range(groups):
        ends.append(inside[g : g + 1] + base)
        starts.append(ends[g] - grouped[g : g + 1])
        base = base + inside[g : g + 1, LANES - 1 :]
    owned_events = jnp.max(base).astype(jnp.int32)

    counts[...] = jnp.zeros(counts.shape, jnp.float32)
    lane_f = iota((SLOTS, LANES), 1, jnp.float32)
    row32, col32 = iota((32, 32), 0), iota((32, 32), 1)
    ahead = (row32 > WINDOW) & (col32 > WINDOW) & (col32 <= row32)
    behind = (row32 < WINDOW) & (col32 > row32) & (col32 <= WINDOW)
    between = hot(ahead | behind).astype(jnp.bfloat16)
    place = iota((32, SLOTS), 0)
    in_window = (place != WINDOW) & (place <= 2 * WINDOW)
    row_ids = iota((ROWS, SLOTS), 0, jnp.float32)
    col_ids = iota((SLOTS, COLS), 1, jnp.float32)

    def chunk(step, carry):
        slot = (step * SLOTS + iota((SLOTS, LANES), 0)).astype(jnp.float32)
        picks, first = [], jnp.zeros((SLOTS, LANES), jnp.float32)
        for g in range(groups):
            here = (slot >= starts[g]) & (slot < ends[g])
            first += jnp.where(here, starts[g], 0.0)
            picks.append(hot(here).astype(jnp.bfloat16))
        pick = jnp.concatenate(picks, axis=1)
        got = jnp.dot(pick, table[...], preferred_element_type=jnp.float32)
        ordinal = slot[:, :1] + 1.0 - jnp.sum(first, axis=1, keepdims=True)
        chosen = got[:, :LANES] == ordinal
        ident = got[:, LANES : 2 * LANES] + 256.0 * got[:, 2 * LANES : 3 * LANES]
        column = jnp.sum(jnp.where(chosen, ident + 1.0, 0.0), axis=1, keepdims=True) - 1.0
        at_lane = jnp.sum(jnp.where(chosen, lane_f, 0.0), axis=1, keepdims=True)
        source = at_lane.astype(jnp.int32) + (iota((SLOTS, LANES), 1) - WINDOW)
        index = source & (LANES - 1)
        parts = [
            jnp.take_along_axis(got[:, k * LANES : (k + 1) * LANES], index, axis=1, mode="promise_in_bounds")
            for k in (3, 4, 5)
        ]
        window = jnp.where(source < 0, parts[0], jnp.where(source < LANES, parts[1], parts[2]))
        window = window.T[:32]
        breaks = hot(window < 0.0).astype(jnp.bfloat16)
        crossed = jnp.dot(between, breaks, preferred_element_type=jnp.float32)
        linked = (crossed == 0.0) & in_window
        near = jnp.where(linked, jnp.abs(window) - 1.0, 255.0)
        weight = jnp.sum(hot(linked), axis=0, keepdims=True)
        pairs = jnp.zeros((ROWS, SLOTS), jnp.float32)
        for d in range(2 * WINDOW + 1):
            if d != WINDOW:
                pairs += hot(near[d : d + 1] == row_ids)
        pairs = jnp.concatenate([pairs, jnp.broadcast_to(weight, (16, SLOTS))], axis=0)
        column_hot = hot(column == col_ids).astype(jnp.bfloat16)
        counts[...] += jnp.dot(
            pairs.astype(jnp.bfloat16), column_hot, preferred_element_type=jnp.float32
        )
        return carry

    lax.fori_loop(0, (owned_events + SLOTS - 1) // SLOTS, chunk, 0)

    def both(row_first, row_second):
        mine_f, its_f = own_ref[:, row_first, :], other_ref[:, row_first, :]
        mine_s, its_s = own_ref[:, row_second, :], other_ref[:, row_second, :]
        return jnp.where(half == 0, mine_f, its_f), jnp.where(half == 0, its_s, mine_s)

    start_items, end_items = both(0, 15)
    start_sess, end_sess = both(16, 23)
    start_sess, end_sess = start_sess & 65535, end_sess >> 16
    slab_row = iota((SLABS, LANES), 0)
    end_items = pltpu.roll(end_items, 1, 0)
    end_sess = jnp.where(slab_row == 0, -1, pltpu.roll(end_sess, 1, 0))
    cross = jnp.zeros((SLABS, LANES), jnp.float32)
    lane = iota((SLABS, LANES), 1)
    for d in range(1, WINDOW + 1):
        before = pltpu.roll(end_sess, d, 1)
        after = pltpu.roll(start_sess, LANES - d, 1)
        cross += hot((lane < d) & (before == start_sess))
        cross += hot((lane >= LANES - d) & (after == end_sess))
    cross_items = jnp.where(lane < LANES // 2, start_items, end_items)
    margins = jnp.sum(own_ref[:, MARGIN_ROW, :], axis=0, keepdims=True).astype(jnp.float32)
    item_row = iota((ROWS, LANES), 0)
    held = jnp.where(item_row == iota((ROWS, LANES), 1), margins, 0.0)
    for s in range(SLABS):
        held += jnp.where(cross_items[s : s + 1] == item_row, cross[s : s + 1], 0.0)
    row_margin = jnp.sum(held, axis=1, keepdims=True)
    totals = jnp.sum(own_ref[:, TOTAL_ROW, :], axis=0, keepdims=True).astype(jnp.float32)
    totals = totals + jnp.sum(cross, axis=0, keepdims=True)
    pair_total = jnp.sum(totals, axis=1, keepdims=True)

    positive = ppmi(
        counts[pl.ds(0, ROWS), :], row_margin, counts[pl.ds(ROWS, 1), :], pair_total
    )
    copy.wait()
    row_words = jnp.where(half == 0, own_ref[:WORDS, BITS_ROW, :], other_ref[:WORDS, BITS_ROW, :])
    fill_signs(jnp.concatenate([words[...], row_words], axis=1), signs)
    result = project(positive, signs)
    for s in range(SLABS):
        out_ref[s] = result[s * ROWS_DEV : (s + 1) * ROWS_DEV]


def all_events(where, items, sessions, bits, interpret=False):
    return pl.pallas_call(
        lambda *refs: all_events_kernel(where, *refs),
        out_shape=jax.ShapeDtypeStruct((SLABS, PAYLOAD, LANES), jnp.int32),
        grid=(1,),
        in_specs=[
            pl.BlockSpec((SLAB_ROWS, LANES), lambda i: (0, 0)),
            pl.BlockSpec((SLAB_ROWS, LANES), lambda i: (0, 0)),
            pl.BlockSpec((WORDS, LANES), lambda i: (0, 0)),
        ],
        out_specs=pl.BlockSpec((SLABS, PAYLOAD, LANES), lambda i: (0, 0, 0)),
        compiler_params=pltpu.CompilerParams(vmem_limit_bytes=VMEM_BYTES),
        interpret=interpret,
        name="all_events",
    )(items, sessions, bits)


def from_all(where, own, other, bits, interpret=False):
    return pl.pallas_call(
        lambda *refs: from_all_kernel(where, *refs),
        out_shape=jax.ShapeDtypeStruct((SLABS, ROWS_DEV, SKETCH), jnp.float32),
        in_specs=[
            pl.BlockSpec(memory_space=pltpu.VMEM),
            pl.BlockSpec(memory_space=pltpu.VMEM),
            pl.BlockSpec(memory_space=pl.ANY),
        ],
        out_specs=pl.BlockSpec(memory_space=pltpu.VMEM),
        scratch_shapes=[
            pltpu.VMEM((PAD + EVENT_ROWS, LANES), jnp.int32),
            pltpu.VMEM((2 * PAD + EVENT_ROWS, LANES), jnp.float32),
            pltpu.VMEM((EVENT_ROWS, LANES), jnp.bfloat16),
            pltpu.VMEM((EVENT_ROWS, 6 * LANES), jnp.bfloat16),
            pltpu.VMEM((ROWS + 16, COLS), jnp.float32),
            pltpu.VMEM((WORDS, OWNED), jnp.int32),
            pltpu.VMEM((16 * WORD_BITS, COLS), jnp.bfloat16),
            pltpu.SemaphoreType.DMA,
        ],
        compiler_params=pltpu.CompilerParams(vmem_limit_bytes=VMEM_BYTES),
        interpret=interpret,
        name="from_all",
    )(own, other, bits)


def route_kernel(where, items_hbm, sessions_hbm, out_ref, items_v, sessions_v, codes, table, near_rows, one_hots, pair_rows, sems):
    slab, band = where()
    get_items = pltpu.make_async_copy(items_hbm, items_v, sems.at[0])
    get_sessions = pltpu.make_async_copy(sessions_hbm, sessions_v, sems.at[1])
    get_items.start()
    get_sessions.start()
    get_items.wait()
    get_sessions.wait()
    items, sessions = items_v[...], sessions_v[...]
    shape = items.shape
    row, lane = iota(shape, 0), iota(shape, 1)
    above = jnp.where(row == 0, -1, pltpu.roll(sessions, 1, 0))
    below = jnp.where(row == SLAB_ROWS - 1, -1, pltpu.roll(sessions, SLAB_ROWS - 1, 0))
    earlier_links = jnp.zeros(shape, jnp.float32)
    later_links = jnp.zeros(shape, jnp.float32)
    for d in range(1, WINDOW + 1):
        earlier = pltpu.roll(jnp.where(lane >= LANES - d, above, sessions), d, 1)
        later = pltpu.roll(jnp.where(lane < d, below, sessions), LANES - d, 1)
        earlier_links += hot(earlier == sessions)
        later_links += hot(later == sessions)
    weights = earlier_links + later_links

    held = jnp.zeros((ROWS, LANES), jnp.float32)
    item_row = iota((ROWS, LANES), 0)
    for r in range(SLAB_ROWS):
        same = items[r : r + 1] == item_row
        held += jnp.where(same, weights[r : r + 1], 0.0)
        one_hots[:, pl.ds(r * LANES, LANES)] = hot(same).astype(jnp.bfloat16)
    margin = jnp.sum(held.T, axis=0, keepdims=True)
    total = jnp.sum(weights, axis=0, keepdims=True)
    first_link = iota(shape, 1, jnp.float32) - earlier_links
    place = iota((2 * LANES, LANES), 0, jnp.float32) - LANES
    self_place = iota((2 * LANES, LANES), 1, jnp.float32)
    sooner = place < self_place
    for r in range(SLAB_ROWS):
        links = hot(sooner & (place >= first_link[r : r + 1])).astype(jnp.bfloat16)
        if r == 0:
            pairs = jnp.dot(one_hots[:, pl.ds(0, LANES)], links[LANES:], preferred_element_type=jnp.float32)
        else:
            pairs = jnp.dot(
                one_hots[:, pl.ds((r - 1) * LANES, 2 * LANES)], links, preferred_element_type=jnp.float32
            )
        pair_rows[:, pl.ds(r * LANES, LANES)] = pairs.astype(jnp.bfloat16)
    ordered = nt_dot(pair_rows[...], one_hots[...])
    row_pairs = ordered + ordered.T

    before = pltpu.roll(jnp.where(lane == LANES - 1, above, sessions), 1, 1)
    value = jnp.minimum(items, ROWS) + 1
    edge = jnp.full((PAD, LANES), -(ROWS + 1.0), jnp.float32)
    codes[pl.ds(0, PAD), :] = edge
    codes[pl.ds(PAD + SLAB_ROWS, PAD), :] = edge
    codes[pl.ds(PAD, SLAB_ROWS), :] = jnp.where(before != sessions, -value, value).astype(jnp.float32)
    inside = items - band * (SLABS * OWNED)
    wide = (items >= ROWS) & (inside >= 0) & (inside < SLABS * OWNED)
    inside = jnp.where(wide, inside, 0)
    owner = jnp.where(wide, inside >> 10, -1)
    owner_row = iota((SLABS, LANES), 0)
    marks = [hot(owner[r : r + 1] == owner_row) for r in range(SLAB_ROWS)]
    upto = hot(iota((LANES, LANES), 0) <= iota((LANES, LANES), 1)).astype(jnp.bfloat16)
    ranks = jnp.dot(
        jnp.concatenate(marks, axis=0).astype(jnp.bfloat16), upto, preferred_element_type=jnp.float32
    )
    ranks = [ranks[r * SLABS : (r + 1) * SLABS] for r in range(SLAB_ROWS)]
    per_row = jnp.zeros((SLABS, LANES), jnp.float32)
    for r in range(SLAB_ROWS):
        per_row = jnp.where(lane == r, ranks[r][:, LANES - 1 :], per_row)
    ends = jnp.dot(per_row.astype(jnp.bfloat16), upto, preferred_element_type=jnp.float32)
    starts = ends - per_row
    block = jnp.where(items >= ROWS, items >> 10, -1)
    sixteen = iota((16, LANES), 0)
    upper = [hot((block[r : r + 1] >> 4) == sixteen) for r in range(SLAB_ROWS)]
    lower = [hot((block[r : r + 1] & 15) == sixteen) for r in range(SLAB_ROWS)]
    loads = nt_dot(
        jnp.concatenate(upper, axis=1).astype(jnp.bfloat16),
        jnp.concatenate(lower, axis=1).astype(jnp.bfloat16),
    )
    most = jnp.max(jnp.max(loads, axis=0, keepdims=True), axis=1, keepdims=True)
    orders = [
        jnp.sum(marks[r] * (ranks[r] + starts[:, r : r + 1]), axis=0, keepdims=True)
        for r in range(SLAB_ROWS)
    ]
    table[pl.ds(SLAB_ROWS, LANES - SLAB_ROWS), :] = jnp.zeros((LANES - SLAB_ROWS, 5 * LANES), jnp.bfloat16)
    row_codes = codes[pl.ds(PAD, SLAB_ROWS), :]
    left = jnp.where(lane >= LANES - 32, codes[pl.ds(PAD - 1, SLAB_ROWS), :], row_codes)
    right = jnp.where(lane < 32, codes[pl.ds(PAD + 1, SLAB_ROWS), :], row_codes)
    fields = [
        jnp.minimum(jnp.concatenate(orders, axis=0), 255.0),
        (inside & 255).astype(jnp.float32),
        (inside >> 8).astype(jnp.float32),
        pltpu.roll(left, 32, 1),
        pltpu.roll(right, LANES - 32, 1),
    ]
    for k, field in enumerate(fields):
        table[pl.ds(0, SLAB_ROWS), pl.ds(k * LANES, LANES)] = field.astype(jnp.bfloat16)
    slot = iota((QUOTA, LANES), 0, jnp.float32)
    picks = [
        hot((slot >= starts[s : s + 1]) & (slot < ends[s : s + 1])).astype(jnp.bfloat16)
        for s in range(SLABS)
    ]
    got = jnp.dot(jnp.concatenate(picks, axis=0), table[...], preferred_element_type=jnp.float32)
    big = (SLABS * QUOTA, LANES)
    number, lanes = iota(big, 0), iota(big, 1)
    target = (number >> 5).astype(jnp.float32) * 4.0
    high = got[:, 2 * LANES : 3 * LANES] - target
    ordinal = ((number & (QUOTA - 1)) + 1).astype(jnp.float32)
    chosen = (got[:, :LANES] == ordinal) & (high >= 0.0) & (high < 4.0)
    ident = got[:, LANES : 2 * LANES] + 256.0 * high
    column = NOBODY + jnp.sum(jnp.where(chosen, ident - NOBODY, 0.0), axis=1, keepdims=True)
    at_lane = jnp.sum(jnp.where(chosen, lanes, 0), axis=1, keepdims=True)
    in_left = at_lane < HALF
    index = (at_lane + jnp.where(in_left, 32 - WINDOW, -32 - WINDOW) + lanes) & (LANES - 1)
    reach = jnp.where(in_left, got[:, 3 * LANES : 4 * LANES], got[:, 4 * LANES :])
    window = jnp.take_along_axis(reach, index, axis=1, mode="promise_in_bounds")
    from_lane, to_lane = iota((LANES, LANES), 0), iota((LANES, LANES), 1)
    ahead = (to_lane > WINDOW) & (from_lane > WINDOW) & (from_lane <= to_lane)
    behind = (to_lane < WINDOW) & (from_lane > to_lane) & (from_lane <= WINDOW)
    between = hot(ahead | behind).astype(jnp.bfloat16)
    crossed = jnp.dot(
        hot(window < 0.0).astype(jnp.bfloat16), between, preferred_element_type=jnp.float32
    )
    linked = (crossed == 0.0) & (lanes <= 2 * WINDOW)
    near = jnp.where(linked, jnp.abs(window) - 1.0, NONE)
    near = jnp.where(lanes == WINDOW, column, near)
    near_rows[...] = (near + 4096.0 * pltpu.roll(near, LANES - 16, 1)).astype(jnp.int32)

    whole = jnp.where(item_row == iota((ROWS, LANES), 1), ordered, row_pairs).astype(jnp.int32)
    packed = pltpu.roll(whole, HALF, 1) + jnp.where(iota((ROWS, LANES), 1) >= HALF, whole * 65536, 0)
    ends_lane = iota((1, LANES), 1)
    spare = jnp.where(most > QUOTA, 1, 0)
    total = jnp.sum(total, axis=1, keepdims=True).astype(jnp.int32)
    margin = margin.astype(jnp.int32)

    def edges(values, single):
        both = jnp.where(ends_lane < LANES - 32, pltpu.roll(values[:1], HALF, 1), values[SLAB_ROWS - 1 :])
        return jnp.where(ends_lane == SPOT, single, both)

    common = jnp.concatenate(
        [pltpu.roll(margin, HALF, 1), margin, edges(items, total), edges(sessions, spare)], axis=0
    )
    sixteenth = iota((8, LANES), 1) >> 4
    for s in range(SLABS):
        rows = jnp.concatenate([packed[s * ROWS_DEV : (s + 1) * ROWS_DEV], common], axis=0)
        for g in range(QUOTA // 8):
            part = near_rows[pl.ds(s * QUOTA + 8 * g, 8), :]
            rows = jnp.where(sixteenth == g, pltpu.roll(part, 16 * g, 1) if g else part, rows)
        out_ref[s] = rows


def count_pairs(near, skip):
    slots = near.shape[1]
    place = iota(near.shape, 0)
    real = near < NONE
    for d in skip:
        real = real & (place != d)
    weight = jnp.sum(hot(real), axis=0, keepdims=True)
    row_ids = iota((ROWS, slots), 0, jnp.float32).astype(COUNT)
    one, none = jnp.ones((), COUNT), jnp.zeros((), COUNT)
    pairs = jnp.zeros((ROWS, slots), COUNT)
    near = near.astype(COUNT)
    for d in range(near.shape[0]):
        if d not in skip:
            pairs += jnp.where(near[d : d + 1] == row_ids, one, none)
    weight = jnp.broadcast_to(weight, (16, slots)).astype(jnp.bfloat16)
    return jnp.concatenate([pairs.astype(jnp.bfloat16), weight], axis=0)


def sketch_kernel(
    where, got_ref, row_bits_ref, bits_hbm, out_ref, spoilt_ref, counts, table, words, wide_signs, sem
):
    slab, band = where()
    copy = pltpu.make_async_copy(
        bits_hbm.at[:, pl.ds(pl.multiple_of(slab * OWNED, OWNED), OWNED)], words, sem
    )
    copy.start()

    slab_row, lane = iota((SLABS, LANES), 0), iota((SLABS, LANES), 1)
    raw_items, raw_sessions = got_ref[:, 6, :], got_ref[:, 7, :]
    edge_items = jnp.where(lane < HALF, pltpu.roll(raw_items, HALF, 1), raw_items)
    edge_sessions = jnp.where(lane < HALF, pltpu.roll(raw_sessions, HALF, 1), raw_sessions)
    spoilt_ref[0, 0] = jnp.max(jnp.where(lane == SPOT, raw_sessions, 0))
    end_items = pltpu.roll(edge_items, 1, 0)
    end_sess = jnp.where(slab_row == 0, -1, pltpu.roll(edge_sessions, 1, 0))
    cross = jnp.zeros((SLABS, LANES), jnp.float32)
    for d in range(1, WINDOW + 1):
        before = pltpu.roll(end_sess, d, 1)
        after = pltpu.roll(edge_sessions, LANES - d, 1)
        cross += hot((lane < d) & (before == edge_sessions))
        cross += hot((lane >= LANES - d) & (after == end_sess))
    items = jnp.where(lane < HALF, edge_items, end_items)
    over = jnp.where(
        lane < HALF,
        hot((edge_sessions == end_sess[:, LANES - 1 :]) & (lane < WINDOW)),
        hot((end_sess == edge_sessions[:, :1]) & (lane >= LANES - WINDOW)),
    )
    partner = jnp.where(over > 0.0, jnp.minimum(items, ROWS).astype(jnp.float32), NONE)
    is_row = items < ROWS
    row_owner = jnp.where(band == 0, slab, -1)
    owned = jnp.where(is_row, items >> 2, items >> 10) == jnp.where(is_row, row_owner, band * SLABS + slab)
    owned = hot(owned & (cross > 0.0))
    local_id = jnp.where(is_row, OWNED + items, items & (OWNED - 1))
    upto = hot(iota((LANES, LANES), 0) <= iota((LANES, LANES), 1)).astype(jnp.bfloat16)
    blank = jnp.zeros((LANES - SLABS, LANES), jnp.float32)
    marks = jnp.concatenate([owned, blank], axis=0).astype(jnp.bfloat16)
    rank = jnp.dot(marks, upto, preferred_element_type=jnp.float32)
    per_row = nt_dot(jnp.ones((8, LANES), jnp.bfloat16), marks)
    ends = jnp.dot(per_row.astype(jnp.bfloat16), upto, preferred_element_type=jnp.float32)
    starts = (ends - per_row)[:1]
    ends = ends[:1]
    crossing = jnp.max(ends).astype(jnp.int32)
    fields = [
        rank[:SLABS] * owned,
        (local_id & 255).astype(jnp.float32),
        (local_id >> 8).astype(jnp.float32),
        partner,
    ]
    for k, field in enumerate(fields):
        table[:, pl.ds(k * LANES, LANES)] = jnp.concatenate([field, blank], axis=0).astype(jnp.bfloat16)
    slot_lane = iota((LANES, LANES), 1)
    col_ids = iota((LANES, COLS), 1, jnp.float32)

    def crossed(step):
        slot = (step * LANES + iota((LANES, LANES), 0)).astype(jnp.float32)
        here = (slot >= starts) & (slot < ends)
        first = jnp.sum(jnp.where(here, starts, 0.0), axis=1, keepdims=True)
        got = jnp.dot(hot(here).astype(jnp.bfloat16), table[...], preferred_element_type=jnp.float32)
        chosen = got[:, :LANES] == slot[:, :1] + 1.0 - first
        ident = got[:, LANES : 2 * LANES] + 256.0 * got[:, 2 * LANES : 3 * LANES]
        column = jnp.sum(jnp.where(chosen, ident + 1.0, 0.0), axis=1, keepdims=True) - 1.0
        at = jnp.sum(jnp.where(chosen, slot_lane, 0), axis=1, keepdims=True)
        reach = LANES - WINDOW
        other_side = jnp.where(at < HALF, hot(slot_lane >= reach + at), hot(slot_lane <= at - reach))
        near = jnp.where(other_side > 0.0, got[:, 3 * LANES :], NONE).T
        near = jnp.concatenate([near[:16], near[LANES - 16 :]], axis=0)
        pairs = count_pairs(near, (15, 16))
        column_hot = hot(column == col_ids).astype(jnp.bfloat16)
        return jnp.dot(pairs, column_hot, preferred_element_type=jnp.float32)

    first_crossed = crossed(0)

    windows = got_ref[...].reshape(SLABS * MESSAGE, LANES).T[:HALF]
    low, high = (windows & 4095).astype(jnp.float32), (windows >> 12).astype(jnp.float32)
    blocks, idents = [], []
    for g in range(QUOTA // 8):
        near = jnp.concatenate([low[16 * g : 16 * g + 16], high[16 * g : 16 * g + 16]], axis=0)
        idents.append(near[WINDOW : WINDOW + 1])
        blocks.append(count_pairs(near, (WINDOW, 31)))
    ident = jnp.concatenate(idents, axis=1)
    pairs = jnp.concatenate(blocks, axis=1)
    column_hot = hot(ident == iota((OWNED, ident.shape[1]), 0, jnp.float32)).astype(jnp.bfloat16)
    counts[:, pl.ds(0, OWNED)] = nt_dot(pairs, column_hot) + first_crossed[:, :OWNED]

    low_sum = jnp.zeros((MESSAGE, LANES), jnp.int32)
    high_sum = jnp.zeros((MESSAGE, LANES), jnp.int32)
    for s in range(SLABS):
        word = got_ref[s]
        low_sum += word & 65535
        high_sum += (word >> 16) & 65535
    mine = jnp.where(iota((MESSAGE, LANES), 1) < HALF, pltpu.roll(low_sum, HALF, 1), high_sum)
    item_row, item_lane = iota((ROWS, LANES), 0), iota((ROWS, LANES), 1)
    placed = jnp.zeros((ROWS, LANES), jnp.int32)
    for q in range(ROWS_DEV):
        placed = jnp.where(item_row == row_owner * ROWS_DEV + q, mine[q : q + 1], placed)
    placed = jnp.where(item_row == item_lane, 2 * placed, placed).astype(jnp.float32)
    counts[pl.ds(0, ROWS), pl.ds(OWNED, ROWS)] = placed.T + first_crossed[:ROWS, OWNED:]

    def chunk(step, carry):
        counts[...] += crossed(step)
        return carry

    lax.fori_loop(1, (crossing + LANES - 1) // LANES, chunk, 0)

    margin_low = jnp.sum(got_ref[:, 4, :], axis=0, keepdims=True)
    margin_high = jnp.sum(got_ref[:, 5, :], axis=0, keepdims=True)
    margins = jnp.where(item_lane[:1] < HALF, pltpu.roll(margin_low, HALF, 1), margin_high)
    held = jnp.where(item_row == item_lane, margins.astype(jnp.float32), 0.0)
    for s in range(SLABS):
        held += jnp.where(items[s : s + 1] == item_row, cross[s : s + 1], 0.0)
    row_margin = jnp.sum(held, axis=1, keepdims=True)
    totals = jnp.where(lane == SPOT, raw_items, 0).astype(jnp.float32) + cross
    pair_total = jnp.sum(jnp.sum(totals, axis=0, keepdims=True), axis=1, keepdims=True)
    col_margin = jnp.concatenate(
        [counts[pl.ds(ROWS, 1), pl.ds(0, OWNED)], jnp.sum(held.T, axis=0, keepdims=True)], axis=1
    )
    positive = ppmi(counts[pl.ds(0, ROWS), :], row_margin, col_margin, pair_total)
    copy.wait()
    held_words = jnp.concatenate([words[...], row_bits_ref[...]], axis=1)
    for b in range(WORD_BITS):
        sign = jnp.where((held_words >> b) & 1 == 1, 1.0, -1.0)
        for j in range(COLS // LANES):
            wide_signs[j, pl.ds(b, WORDS, stride=WORD_BITS), :] = sign[:, j * LANES : (j + 1) * LANES]
    parts = two_parts(positive)
    signs = [wide_signs[j, pl.ds(0, SKETCH), :].astype(jnp.bfloat16) for j in range(COLS // LANES)]
    result = nt_dot(parts, jnp.concatenate(signs, axis=1))
    result = result[:ROWS] + result[ROWS:]
    for s in range(SLABS):
        out_ref[s] = result[s * ROWS_DEV : (s + 1) * ROWS_DEV]


def route(where, items, sessions, interpret=False):
    return pl.pallas_call(
        lambda *refs: route_kernel(where, *refs),
        out_shape=jax.ShapeDtypeStruct((SLABS, MESSAGE, LANES), jnp.int32),
        in_specs=[pl.BlockSpec(memory_space=pltpu.HBM)] * 2,
        out_specs=pl.BlockSpec(memory_space=pltpu.VMEM),
        scratch_shapes=[
            pltpu.VMEM((SLAB_ROWS, LANES), jnp.int32),
            pltpu.VMEM((SLAB_ROWS, LANES), jnp.int32),
            pltpu.VMEM((2 * PAD + SLAB_ROWS, LANES), jnp.float32),
            pltpu.VMEM((LANES, 5 * LANES), jnp.bfloat16),
            pltpu.VMEM((SLABS * QUOTA, LANES), jnp.int32),
            pltpu.VMEM((ROWS, SLAB_ROWS * LANES), jnp.bfloat16),
            pltpu.VMEM((ROWS, SLAB_ROWS * LANES), jnp.bfloat16),
            pltpu.SemaphoreType.DMA((2,)),
        ],
        compiler_params=pltpu.CompilerParams(vmem_limit_bytes=VMEM_BYTES),
        interpret=interpret,
        name="route_events",
    )(items, sessions)


def sketch_part(where, got, bits, interpret=False):
    return pl.pallas_call(
        lambda *refs: sketch_kernel(where, *refs),
        out_shape=(
            jax.ShapeDtypeStruct((SLABS, ROWS_DEV, SKETCH), jnp.float32),
            jax.ShapeDtypeStruct((1, 1), jnp.int32),
        ),
        grid=(1,),
        in_specs=[
            pl.BlockSpec((SLABS, MESSAGE, LANES), lambda i: (0, 0, 0)),
            pl.BlockSpec((WORDS, LANES), lambda i: (0, 0)),
            pl.BlockSpec(memory_space=pltpu.HBM),
        ],
        out_specs=(
            pl.BlockSpec((SLABS, ROWS_DEV, SKETCH), lambda i: (0, 0, 0)),
            pl.BlockSpec(memory_space=pltpu.SMEM),
        ),
        scratch_shapes=[
            pltpu.VMEM((ROWS + 16, COLS), jnp.float32),
            pltpu.VMEM((LANES, 4 * LANES), jnp.bfloat16),
            pltpu.VMEM((WORDS, OWNED), jnp.int32),
            pltpu.VMEM((COLS // LANES, 16 * WORD_BITS, LANES), jnp.float32),
            pltpu.SemaphoreType.DMA,
        ],
        compiler_params=pltpu.CompilerParams(vmem_limit_bytes=VMEM_BYTES),
        interpret=interpret,
        name="sketch_part",
    )(got, bits, bits)


def shares(part):
    rows = jnp.sum(lax.all_to_all(part, "stream", 0, 0, tiled=True), axis=0)
    spread = jnp.broadcast_to(rows[None], (BANDS,) + rows.shape)
    return lax.all_to_all(spread, "item", 0, 0, tiled=True)


def local(event_items, event_sessions, sketch_bits):
    def where():
        return lax.axis_index("stream"), lax.axis_index("item")

    items = event_items.reshape(SLAB_ROWS, LANES)
    sessions = event_sessions.reshape(SLAB_ROWS, LANES)

    def from_every_event(_):
        message = all_events(where, items, sessions, sketch_bits)
        own = lax.all_to_all(message, "stream", 0, 0, tiled=True)
        other = lax.ppermute(own, "item", [(i, i ^ 1) for i in range(BANDS)])
        return shares(from_all(where, own, other, sketch_bits))

    routed = lax.all_to_all(route(where, items, sessions), "stream", 0, 0, tiled=True)
    part, spoilt = sketch_part(where, routed, sketch_bits)
    gathered = lax.cond(spoilt[0, 0] > 0, from_every_event, lambda kept: kept, shares(part))
    return jnp.sum(gathered, axis=0) / math.sqrt(EVENT_ROWS * LANES)


def solution(mesh):
    placed = (P("stream"), P("stream"), P(None, "item"))
    return jax.shard_map(
        local, mesh=mesh, in_specs=placed, out_specs=P("stream", None), check_vma=False
    )
```

```python
import math

import jax
import jax.numpy as jnp
from jax import lax
from jax.experimental import pallas as pl
from jax.experimental.pallas import tpu as pltpu
from jax.sharding import PartitionSpec as P

SKETCH = 256
WINDOW = 15
ROWS = 128
ROWS_DEV = 4
LANES = 128
SLABS = 32
BANDS = 8
SLAB_ROWS = 32
HALF_ROWS = SLAB_ROWS // 2
PAYLOAD = 32
EVENT_ROWS = SLABS * SLAB_ROWS
OWNED = 1024
COLS = OWNED + ROWS
WORD_BITS = 18
WORDS = 15
SLOTS = 384
PAD = 8
MARGIN_ROW, TOTAL_ROW, BITS_ROW = 24, 25, 26
QUOTA = 32
MESSAGE = 8
HALF = LANES // 2
NONE = 255.0
SPOT = HALF + 16
VMEM_BYTES = 48 << 20
COUNT = jnp.bfloat16


def iota(shape, axis, dtype=jnp.int32):
    out = lax.broadcasted_iota(jnp.int32, shape, axis)
    return out if dtype == jnp.int32 else out.astype(dtype)


def nt_dot(left, right):
    return lax.dot_general(
        left, right, (((1,), (1,)), ((), ())), preferred_element_type=jnp.float32
    )


def hot(mask):
    return jnp.where(mask, 1.0, 0.0)


def ppmi(count, row_margin, col_margin, pair_total):
    log_ratio = (
        jnp.log(jnp.maximum(count, 1.0))
        + jnp.log(pair_total)
        - jnp.log(jnp.maximum(row_margin, 1.0))
        - jnp.log(jnp.maximum(col_margin, 1.0))
    )
    return jnp.where(count > 0, jnp.maximum(log_ratio, 0.0), 0.0)


def split(values):
    high = values.astype(jnp.bfloat16)
    rest = values - high.astype(jnp.float32)
    mid = rest.astype(jnp.bfloat16)
    low = (rest - mid.astype(jnp.float32)).astype(jnp.bfloat16)
    return jnp.concatenate([high, mid, low], axis=0)


def two_parts(values):
    high = values.astype(jnp.bfloat16)
    low = (values - high.astype(jnp.float32)).astype(jnp.bfloat16)
    return jnp.concatenate([high, low], axis=0)


def joined(parts):
    third = parts.shape[0] // 3
    return parts[:third] + (parts[third : 2 * third] + parts[2 * third :])


def fill_signs(held_words, signs):
    held_words = jnp.concatenate([held_words, jnp.zeros((1, COLS), jnp.int32)], axis=0)
    for b in range(WORD_BITS):
        signs[pl.ds(b * 16, 16), :] = jnp.where((held_words >> b) & 1 == 1, 1.0, -1.0).astype(jnp.bfloat16)


def project(positive, signs):
    by_bit = joined(nt_dot(split(positive), signs[...]))
    have = iota((16 * WORD_BITS, SKETCH), 0)
    want = iota((16 * WORD_BITS, SKETCH), 1)
    order = hot((have & 15) * WORD_BITS + (have >> 4) == want).astype(jnp.bfloat16)
    return joined(jnp.dot(split(by_bit), order, preferred_element_type=jnp.float32))


def all_events_kernel(where, items_ref, sessions_ref, bits_ref, out_ref):
    _, band = where()
    half = lax.rem(band, 2)
    items, sessions = items_ref[...], sessions_ref[...]
    shape = items.shape
    row, lane = iota(shape, 0), iota(shape, 1)
    above = jnp.where(row == 0, -1, pltpu.roll(sessions, 1, 0))
    below = jnp.where(row == SLAB_ROWS - 1, -1, pltpu.roll(sessions, SLAB_ROWS - 1, 0))
    weights = jnp.zeros(shape, jnp.float32)
    for d in range(1, WINDOW + 1):
        earlier = pltpu.roll(jnp.where(lane >= LANES - d, above, sessions), d, 1)
        later = pltpu.roll(jnp.where(lane < d, below, sessions), LANES - d, 1)
        weights += hot(earlier == sessions) + hot(later == sessions)
    held = jnp.zeros((ROWS, LANES), jnp.float32)
    item_row = iota((ROWS, LANES), 0)
    for r in range(SLAB_ROWS):
        held += jnp.where(items[r : r + 1] == item_row, weights[r : r + 1], 0.0)
    margin = jnp.sum(held.T, axis=0, keepdims=True).astype(jnp.int32)
    total = jnp.sum(weights, axis=0, keepdims=True).astype(jnp.int32)
    own_items = jnp.where(half == 0, items[:HALF_ROWS], items[HALF_ROWS:])
    own_sessions = jnp.where(half == 0, sessions[:HALF_ROWS], sessions[HALF_ROWS:])
    pairs = own_sessions[:8] + own_sessions[8:] * 65536
    slab, _ = where()
    word = bits_ref[...]
    one = jnp.sum(
        jnp.where(iota(word.shape, 0) == jnp.minimum(slab, WORDS - 1), word, 0),
        axis=0,
        keepdims=True,
    )
    extra = jnp.concatenate([margin, total, one, jnp.zeros((5, LANES), jnp.int32)], axis=0)
    message = jnp.concatenate([own_items, pairs, extra], axis=0)
    for s in range(SLABS):
        out_ref[s] = message


def from_all_kernel(
    where, own_ref, other_ref, bits_hbm, out_ref,
    sess, codes, mask, table, counts, words, signs, sem,
):
    slab, band = where()
    half = lax.rem(band, 2)
    copy = pltpu.make_async_copy(
        bits_hbm.at[:, pl.ds(pl.multiple_of(slab * OWNED, OWNED), OWNED)],
        words,
        sem,
    )
    copy.start()
    lane_s = iota((SLAB_ROWS, LANES), 1)
    block_id = band * SLABS + slab
    pair_id = jnp.where(band < 2, 2 * slab + half, -1)

    edge = jnp.full((PAD, LANES), -(ROWS + 1.0), jnp.float32)
    codes[pl.ds(0, PAD), :] = edge
    codes[pl.ds(PAD + EVENT_ROWS, PAD), :] = edge
    sess[pl.ds(0, PAD), :] = jnp.full((PAD, LANES), -1, jnp.int32)

    def halves(s):
        mine, its = own_ref[s], other_ref[s]
        return jnp.where(half == 0, mine, its), jnp.where(half == 0, its, mine)

    def unpack(s, carry):
        first, second = halves(s)
        items = jnp.concatenate([first[:16], second[:16]], axis=0)
        a, b = first[16:24], second[16:24]
        sessions = jnp.concatenate([a & 65535, a >> 16, b & 65535, b >> 16], axis=0)
        base = pl.multiple_of(s * SLAB_ROWS, SLAB_ROWS)
        sess[pl.ds(PAD + base, SLAB_ROWS), :] = sessions
        above = sess[pl.ds(PAD - 1 + base, SLAB_ROWS), :]
        before = pltpu.roll(jnp.where(lane_s == LANES - 1, above, sessions), 1, 1)
        value = jnp.minimum(items, ROWS) + 1
        codes[pl.ds(PAD + base, SLAB_ROWS), :] = jnp.where(
            before != sessions, -value, value
        ).astype(jnp.float32)
        is_row = items < ROWS
        owned = jnp.where(is_row, items >> 1, items >> 10) == jnp.where(is_row, pair_id, block_id)
        ident = jnp.where(is_row, OWNED + items, items & (OWNED - 1))
        rows = pl.ds(base, SLAB_ROWS)
        mask[rows, :] = hot(owned).astype(jnp.bfloat16)
        table[rows, pl.ds(LANES, LANES)] = (ident & 255).astype(jnp.float32).astype(jnp.bfloat16)
        table[rows, pl.ds(2 * LANES, LANES)] = (ident >> 8).astype(jnp.float32).astype(jnp.bfloat16)
        return carry

    lax.fori_loop(0, SLABS, unpack, 0, unroll=4)
    for r in range(0, EVENT_ROWS, 128):
        rows = pl.ds(r, 128)
        table[rows, pl.ds(3 * LANES, LANES)] = codes[pl.ds(PAD - 1 + r, 128), :].astype(jnp.bfloat16)
        table[rows, pl.ds(4 * LANES, LANES)] = codes[pl.ds(PAD + r, 128), :].astype(jnp.bfloat16)
        table[rows, pl.ds(5 * LANES, LANES)] = codes[pl.ds(PAD + 1 + r, 128), :].astype(jnp.bfloat16)

    upto = hot(iota((LANES, LANES), 0) <= iota((LANES, LANES), 1)).astype(jnp.bfloat16)
    owned = mask[...]
    rank = jnp.dot(owned, upto, preferred_element_type=jnp.float32)
    table[:, pl.ds(0, LANES)] = (rank * owned.astype(jnp.float32)).astype(jnp.bfloat16)
    per_row = nt_dot(jnp.ones((8, LANES), jnp.bfloat16), owned)
    groups = EVENT_ROWS // LANES
    grouped = jnp.concatenate(
        [per_row[:1, g * LANES : (g + 1) * LANES] for g in range(groups)], axis=0
    )
    inside = jnp.dot(grouped.astype(jnp.bfloat16), upto, preferred_element_type=jnp.float32)
    ends, starts, base = [], [], jnp.zeros((1, 1), jnp.float32)
    for g in range(groups):
        ends.append(inside[g : g + 1] + base)
        starts.append(ends[g] - grouped[g : g + 1])
        base = base + inside[g : g + 1, LANES - 1 :]
    owned_events = jnp.max(base).astype(jnp.int32)

    counts[...] = jnp.zeros(counts.shape, jnp.float32)
    lane_f = iota((SLOTS, LANES), 1, jnp.float32)
    row32, col32 = iota((32, 32), 0), iota((32, 32), 1)
    ahead = (row32 > WINDOW) & (col32 > WINDOW) & (col32 <= row32)
    behind = (row32 < WINDOW) & (col32 > row32) & (col32 <= WINDOW)
    between = hot(ahead | behind).astype(jnp.bfloat16)
    place = iota((32, SLOTS), 0)
    in_window = (place != WINDOW) & (place <= 2 * WINDOW)
    row_ids = iota((ROWS, SLOTS), 0, jnp.float32)
    col_ids = iota((SLOTS, COLS), 1, jnp.float32)

    def chunk(step, carry):
        slot = (step * SLOTS + iota((SLOTS, LANES), 0)).astype(jnp.float32)
        picks, first = [], jnp.zeros((SLOTS, LANES), jnp.float32)
        for g in range(groups):
            here = (slot >= starts[g]) & (slot < ends[g])
            first += jnp.where(here, starts[g], 0.0)
            picks.append(hot(here).astype(jnp.bfloat16))
        pick = jnp.concatenate(picks, axis=1)
        got = jnp.dot(pick, table[...], preferred_element_type=jnp.float32)
        ordinal = slot[:, :1] + 1.0 - jnp.sum(first, axis=1, keepdims=True)
        chosen = got[:, :LANES] == ordinal
        ident = got[:, LANES : 2 * LANES] + 256.0 * got[:, 2 * LANES : 3 * LANES]
        column = jnp.sum(jnp.where(chosen, ident + 1.0, 0.0), axis=1, keepdims=True) - 1.0
        at_lane = jnp.sum(jnp.where(chosen, lane_f, 0.0), axis=1, keepdims=True)
        source = at_lane.astype(jnp.int32) + (iota((SLOTS, LANES), 1) - WINDOW)
        index = source & (LANES - 1)
        parts = [
            jnp.take_along_axis(got[:, k * LANES : (k + 1) * LANES], index, axis=1, mode="promise_in_bounds")
            for k in (3, 4, 5)
        ]
        window = jnp.where(source < 0, parts[0], jnp.where(source < LANES, parts[1], parts[2]))
        window = window.T[:32]
        breaks = hot(window < 0.0).astype(jnp.bfloat16)
        crossed = jnp.dot(between, breaks, preferred_element_type=jnp.float32)
        linked = (crossed == 0.0) & in_window
        near = jnp.where(linked, jnp.abs(window) - 1.0, 255.0)
        weight = jnp.sum(hot(linked), axis=0, keepdims=True)
        pairs = jnp.zeros((ROWS, SLOTS), jnp.float32)
        for d in range(2 * WINDOW + 1):
            if d != WINDOW:
                pairs += hot(near[d : d + 1] == row_ids)
        pairs = jnp.concatenate([pairs, jnp.broadcast_to(weight, (16, SLOTS))], axis=0)
        column_hot = hot(column == col_ids).astype(jnp.bfloat16)
        counts[...] += jnp.dot(
            pairs.astype(jnp.bfloat16), column_hot, preferred_element_type=jnp.float32
        )
        return carry

    lax.fori_loop(0, (owned_events + SLOTS - 1) // SLOTS, chunk, 0)

    def both(row_first, row_second):
        mine_f, its_f = own_ref[:, row_first, :], other_ref[:, row_first, :]
        mine_s, its_s = own_ref[:, row_second, :], other_ref[:, row_second, :]
        return jnp.where(half == 0, mine_f, its_f), jnp.where(half == 0, its_s, mine_s)

    start_items, end_items = both(0, 15)
    start_sess, end_sess = both(16, 23)
    start_sess, end_sess = start_sess & 65535, end_sess >> 16
    slab_row = iota((SLABS, LANES), 0)
    end_items = pltpu.roll(end_items, 1, 0)
    end_sess = jnp.where(slab_row == 0, -1, pltpu.roll(end_sess, 1, 0))
    cross = jnp.zeros((SLABS, LANES), jnp.float32)
    lane = iota((SLABS, LANES), 1)
    for d in range(1, WINDOW + 1):
        before = pltpu.roll(end_sess, d, 1)
        after = pltpu.roll(start_sess, LANES - d, 1)
        cross += hot((lane < d) & (before == start_sess))
        cross += hot((lane >= LANES - d) & (after == end_sess))
    cross_items = jnp.where(lane < LANES // 2, start_items, end_items)
    margins = jnp.sum(own_ref[:, MARGIN_ROW, :], axis=0, keepdims=True).astype(jnp.float32)
    item_row = iota((ROWS, LANES), 0)
    held = jnp.where(item_row == iota((ROWS, LANES), 1), margins, 0.0)
    for s in range(SLABS):
        held += jnp.where(cross_items[s : s + 1] == item_row, cross[s : s + 1], 0.0)
    row_margin = jnp.sum(held, axis=1, keepdims=True)
    totals = jnp.sum(own_ref[:, TOTAL_ROW, :], axis=0, keepdims=True).astype(jnp.float32)
    totals = totals + jnp.sum(cross, axis=0, keepdims=True)
    pair_total = jnp.sum(totals, axis=1, keepdims=True)

    positive = ppmi(
        counts[pl.ds(0, ROWS), :], row_margin, counts[pl.ds(ROWS, 1), :], pair_total
    )
    copy.wait()
    row_words = jnp.where(half == 0, own_ref[:WORDS, BITS_ROW, :], other_ref[:WORDS, BITS_ROW, :])
    fill_signs(jnp.concatenate([words[...], row_words], axis=1), signs)
    result = project(positive, signs)
    for s in range(SLABS):
        out_ref[s] = result[s * ROWS_DEV : (s + 1) * ROWS_DEV]


def all_events(where, items, sessions, bits, interpret=False):
    return pl.pallas_call(
        lambda *refs: all_events_kernel(where, *refs),
        out_shape=jax.ShapeDtypeStruct((SLABS, PAYLOAD, LANES), jnp.int32),
        grid=(1,),
        in_specs=[
            pl.BlockSpec((SLAB_ROWS, LANES), lambda i: (0, 0)),
            pl.BlockSpec((SLAB_ROWS, LANES), lambda i: (0, 0)),
            pl.BlockSpec((WORDS, LANES), lambda i: (0, 0)),
        ],
        out_specs=pl.BlockSpec((SLABS, PAYLOAD, LANES), lambda i: (0, 0, 0)),
        compiler_params=pltpu.CompilerParams(vmem_limit_bytes=VMEM_BYTES),
        interpret=interpret,
        name="all_events",
    )(items, sessions, bits)


def from_all(where, own, other, bits, interpret=False):
    return pl.pallas_call(
        lambda *refs: from_all_kernel(where, *refs),
        out_shape=jax.ShapeDtypeStruct((SLABS, ROWS_DEV, SKETCH), jnp.float32),
        in_specs=[
            pl.BlockSpec(memory_space=pltpu.VMEM),
            pl.BlockSpec(memory_space=pltpu.VMEM),
            pl.BlockSpec(memory_space=pl.ANY),
        ],
        out_specs=pl.BlockSpec(memory_space=pltpu.VMEM),
        scratch_shapes=[
            pltpu.VMEM((PAD + EVENT_ROWS, LANES), jnp.int32),
            pltpu.VMEM((2 * PAD + EVENT_ROWS, LANES), jnp.float32),
            pltpu.VMEM((EVENT_ROWS, LANES), jnp.bfloat16),
            pltpu.VMEM((EVENT_ROWS, 6 * LANES), jnp.bfloat16),
            pltpu.VMEM((ROWS + 16, COLS), jnp.float32),
            pltpu.VMEM((WORDS, OWNED), jnp.int32),
            pltpu.VMEM((16 * WORD_BITS, COLS), jnp.bfloat16),
            pltpu.SemaphoreType.DMA,
        ],
        compiler_params=pltpu.CompilerParams(vmem_limit_bytes=VMEM_BYTES),
        interpret=interpret,
        name="from_all",
    )(own, other, bits)


def route_kernel(where, items_hbm, sessions_hbm, out_ref, items_v, sessions_v, codes, table, near_rows, one_hots, pair_rows, sems):
    slab, band = where()
    get_items = pltpu.make_async_copy(items_hbm, items_v, sems.at[0])
    get_sessions = pltpu.make_async_copy(sessions_hbm, sessions_v, sems.at[1])
    get_items.start()
    get_sessions.start()
    get_items.wait()
    get_sessions.wait()
    items, sessions = items_v[...], sessions_v[...]
    shape = items.shape
    row, lane = iota(shape, 0), iota(shape, 1)
    above = jnp.where(row == 0, -1, pltpu.roll(sessions, 1, 0))
    below = jnp.where(row == SLAB_ROWS - 1, -1, pltpu.roll(sessions, SLAB_ROWS - 1, 0))
    earlier_links = jnp.zeros(shape, jnp.float32)
    later_links = jnp.zeros(shape, jnp.float32)
    for d in range(1, WINDOW + 1):
        earlier = pltpu.roll(jnp.where(lane >= LANES - d, above, sessions), d, 1)
        later = pltpu.roll(jnp.where(lane < d, below, sessions), LANES - d, 1)
        earlier_links += hot(earlier == sessions)
        later_links += hot(later == sessions)
    weights = earlier_links + later_links

    one, none = jnp.ones((), jnp.bfloat16), jnp.zeros((), jnp.bfloat16)
    item_codes = jnp.minimum(items, 255).astype(jnp.float32).astype(jnp.bfloat16)
    row_ids = iota((ROWS, LANES), 0, jnp.float32).astype(jnp.bfloat16)
    for r in range(SLAB_ROWS):
        same = item_codes[r : r + 1] == row_ids
        one_hots[:, pl.ds(r * LANES, LANES)] = jnp.where(same, one, none)
        pair_rows[pl.ds(ROWS, 16), pl.ds(r * LANES, LANES)] = jnp.broadcast_to(
            weights[r : r + 1], (16, LANES)
        ).astype(jnp.bfloat16)
    total = jnp.sum(weights, axis=0, keepdims=True)
    first_link = (iota(shape, 1, jnp.float32) - earlier_links).astype(jnp.bfloat16)
    place = iota((LANES, LANES), 0, jnp.float32).astype(jnp.bfloat16)
    sooner = iota((LANES, LANES), 0) < iota((LANES, LANES), 1)
    sooner = jnp.where(sooner, place, jnp.full((), -64.0, jnp.bfloat16))
    last = (iota((16, LANES), 0, jnp.float32) - 16.0).astype(jnp.bfloat16)
    no_links = jnp.zeros((LANES - 16, LANES), jnp.bfloat16)
    for r in range(SLAB_ROWS):
        begin = first_link[r : r + 1]
        links = jnp.where(sooner >= begin, one, none)
        if r == 0:
            pairs = jnp.dot(one_hots[:, pl.ds(0, LANES)], links, preferred_element_type=jnp.float32)
        else:
            links = jnp.concatenate([no_links, jnp.where(last >= begin, one, none), links], axis=0)
            pairs = jnp.dot(
                one_hots[:, pl.ds((r - 1) * LANES, 2 * LANES)], links, preferred_element_type=jnp.float32
            )
        pair_rows[pl.ds(0, ROWS), pl.ds(r * LANES, LANES)] = pairs.astype(jnp.bfloat16)
    ordered = nt_dot(pair_rows[...], one_hots[...])
    margin = ordered[ROWS : ROWS + 1]
    ordered = ordered[:ROWS]
    row_pairs = ordered + ordered.T
    item_row = iota((ROWS, LANES), 0)

    before = pltpu.roll(jnp.where(lane == LANES - 1, above, sessions), 1, 1)
    value = jnp.minimum(items, ROWS) + 1
    edge = jnp.full((PAD, LANES), -(ROWS + 1.0), jnp.float32)
    codes[pl.ds(0, PAD), :] = edge
    codes[pl.ds(PAD + SLAB_ROWS, PAD), :] = edge
    codes[pl.ds(PAD, SLAB_ROWS), :] = jnp.where(before != sessions, -value, value).astype(jnp.float32)
    inside = items - band * (SLABS * OWNED)
    wide = (items >= ROWS) & (inside >= 0) & (inside < SLABS * OWNED)
    inside = jnp.where(wide, inside, 0)
    owner = jnp.where(wide, inside >> 10, -1)
    owner_row = iota((SLABS, LANES), 0)
    marks = [hot(owner[r : r + 1] == owner_row) for r in range(SLAB_ROWS)]
    upto = hot(iota((LANES, LANES), 0) <= iota((LANES, LANES), 1)).astype(jnp.bfloat16)
    ranks = jnp.dot(
        jnp.concatenate(marks, axis=0).astype(jnp.bfloat16), upto, preferred_element_type=jnp.float32
    )
    ranks = [ranks[r * SLABS : (r + 1) * SLABS] for r in range(SLAB_ROWS)]
    per_row = jnp.zeros((SLABS, LANES), jnp.float32)
    for r in range(SLAB_ROWS):
        per_row = jnp.where(lane == r, ranks[r][:, LANES - 1 :], per_row)
    ends = jnp.dot(per_row.astype(jnp.bfloat16), upto, preferred_element_type=jnp.float32)
    starts = ends - per_row
    block = jnp.where(items >= ROWS, items >> 10, -1)
    sixteen = iota((16, LANES), 0)
    upper = [hot((block[r : r + 1] >> 4) == sixteen) for r in range(SLAB_ROWS)]
    lower = [hot((block[r : r + 1] & 15) == sixteen) for r in range(SLAB_ROWS)]
    loads = nt_dot(
        jnp.concatenate(upper, axis=1).astype(jnp.bfloat16),
        jnp.concatenate(lower, axis=1).astype(jnp.bfloat16),
    )
    most = jnp.max(jnp.max(loads, axis=0, keepdims=True), axis=1, keepdims=True)
    orders = [
        jnp.sum(marks[r] * (ranks[r] + starts[:, r : r + 1]), axis=0, keepdims=True)
        for r in range(SLAB_ROWS)
    ]
    table[pl.ds(SLAB_ROWS, LANES - SLAB_ROWS), :] = jnp.zeros((LANES - SLAB_ROWS, 5 * LANES), jnp.bfloat16)
    row_codes = codes[pl.ds(PAD, SLAB_ROWS), :]
    left = jnp.where(lane >= LANES - 32, codes[pl.ds(PAD - 1, SLAB_ROWS), :], row_codes)
    right = jnp.where(lane < 32, codes[pl.ds(PAD + 1, SLAB_ROWS), :], row_codes)
    fields = [
        jnp.minimum(jnp.concatenate(orders, axis=0), 255.0),
        (inside & 255).astype(jnp.float32),
        (inside >> 8).astype(jnp.float32),
        pltpu.roll(left, 32, 1),
        pltpu.roll(right, LANES - 32, 1),
    ]
    for k, field in enumerate(fields):
        table[pl.ds(0, SLAB_ROWS), pl.ds(k * LANES, LANES)] = field.astype(jnp.bfloat16)
    slot = iota((QUOTA, LANES), 0, jnp.float32)
    picks = [
        hot((slot >= starts[s : s + 1]) & (slot < ends[s : s + 1])).astype(jnp.bfloat16)
        for s in range(SLABS)
    ]
    got = jnp.dot(jnp.concatenate(picks, axis=0), table[...], preferred_element_type=jnp.float32)
    big = (SLABS * QUOTA, LANES)
    number, lanes = iota(big, 0), iota(big, 1)
    target = (number >> 5).astype(jnp.float32) * 4.0
    high = got[:, 2 * LANES : 3 * LANES] - target
    ordinal = ((number & (QUOTA - 1)) + 1).astype(jnp.float32)
    chosen = (got[:, :LANES] == ordinal) & (high >= 0.0) & (high < 4.0)
    ident = got[:, LANES : 2 * LANES] + 256.0 * high + 1.0
    found = jnp.sum(
        jnp.where(chosen, ident * LANES + lanes.astype(jnp.float32), 0.0), axis=1, keepdims=True
    ).astype(jnp.int32)
    column = (((found >> 7) - 1) & 4095).astype(jnp.float32)
    at_lane = found & (LANES - 1)
    index = ((at_lane & (HALF - 1)) + (32 - WINDOW) + lanes) & (LANES - 1)
    reach = jnp.where(at_lane < HALF, got[:, 3 * LANES : 4 * LANES], got[:, 4 * LANES :])
    window = jnp.take_along_axis(reach, index, axis=1, mode="promise_in_bounds")
    from_lane, to_lane = iota((LANES, LANES), 0), iota((LANES, LANES), 1)
    ahead = (to_lane > WINDOW) & (from_lane > WINDOW) & (from_lane <= to_lane)
    behind = (to_lane < WINDOW) & (from_lane > to_lane) & (from_lane <= WINDOW)
    between = hot(ahead | behind).astype(jnp.bfloat16)
    crossed = jnp.dot(
        hot(window < 0.0).astype(jnp.bfloat16), between, preferred_element_type=jnp.float32
    )
    linked = (crossed == 0.0) & (lanes <= 2 * WINDOW)
    near = jnp.where(linked, jnp.abs(window) - 1.0, NONE)
    near = jnp.where(lanes == WINDOW, column, near)
    near_rows[...] = (near + 4096.0 * pltpu.roll(near, LANES - 16, 1)).astype(jnp.int32)

    whole = jnp.where(item_row == iota((ROWS, LANES), 1), ordered, row_pairs).astype(jnp.int32)
    packed = pltpu.roll(whole, HALF, 1) + jnp.where(iota((ROWS, LANES), 1) >= HALF, whole * 65536, 0)
    ends_lane = iota((1, LANES), 1)
    spare = jnp.where(most > QUOTA, 1, 0)
    total = jnp.sum(total, axis=1, keepdims=True).astype(jnp.int32)
    margin = margin.astype(jnp.int32)

    def edges(values, single):
        both = jnp.where(ends_lane < LANES - 32, pltpu.roll(values[:1], HALF, 1), values[SLAB_ROWS - 1 :])
        return jnp.where(ends_lane == SPOT, single, both)

    common = jnp.concatenate(
        [pltpu.roll(margin, HALF, 1), margin, edges(items, total), edges(sessions, spare)], axis=0
    )
    sixteenth = iota((8, LANES), 1) >> 4
    for s in range(SLABS):
        rows = jnp.concatenate([packed[s * ROWS_DEV : (s + 1) * ROWS_DEV], common], axis=0)
        for g in range(QUOTA // 8):
            part = near_rows[pl.ds(s * QUOTA + 8 * g, 8), :]
            rows = jnp.where(sixteenth == g, pltpu.roll(part, 16 * g, 1) if g else part, rows)
        out_ref[s] = rows


def count_pairs(near, skip):
    slots = near.shape[1]
    place = iota(near.shape, 0)
    real = near < NONE
    for d in skip:
        real = real & (place != d)
    weight = jnp.sum(hot(real), axis=0, keepdims=True)
    row_ids = iota((ROWS, slots), 0, jnp.float32).astype(COUNT)
    one, none = jnp.ones((), COUNT), jnp.zeros((), COUNT)
    pairs = jnp.zeros((ROWS, slots), COUNT)
    near = near.astype(COUNT)
    for d in range(near.shape[0]):
        if d not in skip:
            pairs += jnp.where(near[d : d + 1] == row_ids, one, none)
    weight = jnp.broadcast_to(weight, (16, slots)).astype(jnp.bfloat16)
    return jnp.concatenate([pairs.astype(jnp.bfloat16), weight], axis=0)


def sketch_kernel(
    where, got_ref, row_bits_ref, bits_hbm, out_ref, spoilt_ref, counts, table, words, wide_signs, sem
):
    slab, band = where()
    copy = pltpu.make_async_copy(
        bits_hbm.at[:, pl.ds(pl.multiple_of(slab * OWNED, OWNED), OWNED)], words, sem
    )
    copy.start()

    slab_row, lane = iota((SLABS, LANES), 0), iota((SLABS, LANES), 1)
    raw_items, raw_sessions = got_ref[:, 6, :], got_ref[:, 7, :]
    edge_items = jnp.where(lane < HALF, pltpu.roll(raw_items, HALF, 1), raw_items)
    edge_sessions = jnp.where(lane < HALF, pltpu.roll(raw_sessions, HALF, 1), raw_sessions)
    spoilt_ref[0, 0] = jnp.max(jnp.where(lane == SPOT, raw_sessions, 0))
    end_items = pltpu.roll(edge_items, 1, 0)
    end_sess = jnp.where(slab_row == 0, -1, pltpu.roll(edge_sessions, 1, 0))
    cross = jnp.zeros((SLABS, LANES), jnp.float32)
    for d in range(1, WINDOW + 1):
        before = pltpu.roll(end_sess, d, 1)
        after = pltpu.roll(edge_sessions, LANES - d, 1)
        cross += hot((lane < d) & (before == edge_sessions))
        cross += hot((lane >= LANES - d) & (after == end_sess))
    items = jnp.where(lane < HALF, edge_items, end_items)
    over = jnp.where(
        lane < HALF,
        hot((edge_sessions == end_sess[:, LANES - 1 :]) & (lane < WINDOW)),
        hot((end_sess == edge_sessions[:, :1]) & (lane >= LANES - WINDOW)),
    )
    partner = jnp.where(over > 0.0, jnp.minimum(items, ROWS).astype(jnp.float32), NONE)
    is_row = items < ROWS
    row_owner = jnp.where(band == 0, slab, -1)
    owned = jnp.where(is_row, items >> 2, items >> 10) == jnp.where(is_row, row_owner, band * SLABS + slab)
    owned = hot(owned & (cross > 0.0))
    local_id = jnp.where(is_row, OWNED + items, items & (OWNED - 1))
    upto = hot(iota((LANES, LANES), 0) <= iota((LANES, LANES), 1)).astype(jnp.bfloat16)
    blank = jnp.zeros((LANES - SLABS, LANES), jnp.float32)
    marks = jnp.concatenate([owned, blank], axis=0).astype(jnp.bfloat16)
    rank = jnp.dot(marks, upto, preferred_element_type=jnp.float32)
    per_row = nt_dot(jnp.ones((8, LANES), jnp.bfloat16), marks)
    ends = jnp.dot(per_row.astype(jnp.bfloat16), upto, preferred_element_type=jnp.float32)
    starts = (ends - per_row)[:1]
    ends = ends[:1]
    crossing = jnp.max(ends).astype(jnp.int32)
    fields = [
        rank[:SLABS] * owned,
        (local_id & 255).astype(jnp.float32),
        (local_id >> 8).astype(jnp.float32),
        partner,
    ]
    for k, field in enumerate(fields):
        table[:, pl.ds(k * LANES, LANES)] = jnp.concatenate([field, blank], axis=0).astype(jnp.bfloat16)
    slot_lane = iota((LANES, LANES), 1)
    col_ids = iota((LANES, COLS), 1, jnp.float32)

    def crossed(step):
        slot = (step * LANES + iota((LANES, LANES), 0)).astype(jnp.float32)
        here = (slot >= starts) & (slot < ends)
        first = jnp.sum(jnp.where(here, starts, 0.0), axis=1, keepdims=True)
        got = jnp.dot(hot(here).astype(jnp.bfloat16), table[...], preferred_element_type=jnp.float32)
        chosen = got[:, :LANES] == slot[:, :1] + 1.0 - first
        ident = got[:, LANES : 2 * LANES] + 256.0 * got[:, 2 * LANES : 3 * LANES]
        column = jnp.sum(jnp.where(chosen, ident + 1.0, 0.0), axis=1, keepdims=True) - 1.0
        at = jnp.sum(jnp.where(chosen, slot_lane, 0), axis=1, keepdims=True)
        reach = LANES - WINDOW
        other_side = jnp.where(at < HALF, hot(slot_lane >= reach + at), hot(slot_lane <= at - reach))
        near = jnp.where(other_side > 0.0, got[:, 3 * LANES :], NONE).T
        near = jnp.concatenate([near[:16], near[LANES - 16 :]], axis=0)
        pairs = count_pairs(near, (15, 16))
        column_hot = hot(column == col_ids).astype(jnp.bfloat16)
        return jnp.dot(pairs, column_hot, preferred_element_type=jnp.float32)

    first_crossed = crossed(0)

    windows = got_ref[...].reshape(SLABS * MESSAGE, LANES).T[:HALF]
    low, high = (windows & 4095).astype(jnp.float32), (windows >> 12).astype(jnp.float32)
    blocks, idents = [], []
    for g in range(QUOTA // 8):
        near = jnp.concatenate([low[16 * g : 16 * g + 16], high[16 * g : 16 * g + 16]], axis=0)
        idents.append(near[WINDOW : WINDOW + 1])
        blocks.append(count_pairs(near, (WINDOW, 31)))
    ident = jnp.concatenate(idents, axis=1)
    pairs = jnp.concatenate(blocks, axis=1)
    column_hot = hot(ident == iota((OWNED, ident.shape[1]), 0, jnp.float32)).astype(jnp.bfloat16)
    counts[:, pl.ds(0, OWNED)] = nt_dot(pairs, column_hot) + first_crossed[:, :OWNED]

    low_sum = jnp.zeros((MESSAGE, LANES), jnp.int32)
    high_sum = jnp.zeros((MESSAGE, LANES), jnp.int32)
    for s in range(SLABS):
        word = got_ref[s]
        low_sum += word & 65535
        high_sum += (word >> 16) & 65535
    mine = jnp.where(iota((MESSAGE, LANES), 1) < HALF, pltpu.roll(low_sum, HALF, 1), high_sum)
    item_row, item_lane = iota((ROWS, LANES), 0), iota((ROWS, LANES), 1)
    placed = jnp.zeros((ROWS, LANES), jnp.int32)
    for q in range(ROWS_DEV):
        placed = jnp.where(item_row == row_owner * ROWS_DEV + q, mine[q : q + 1], placed)
    placed = jnp.where(item_row == item_lane, 2 * placed, placed).astype(jnp.float32)
    counts[pl.ds(0, ROWS), pl.ds(OWNED, ROWS)] = placed.T + first_crossed[:ROWS, OWNED:]

    def chunk(step, carry):
        counts[...] += crossed(step)
        return carry

    lax.fori_loop(1, (crossing + LANES - 1) // LANES, chunk, 0)

    margin_low = jnp.sum(got_ref[:, 4, :], axis=0, keepdims=True)
    margin_high = jnp.sum(got_ref[:, 5, :], axis=0, keepdims=True)
    margins = jnp.where(item_lane[:1] < HALF, pltpu.roll(margin_low, HALF, 1), margin_high)
    held = jnp.where(item_row == item_lane, margins.astype(jnp.float32), 0.0)
    for s in range(SLABS):
        held += jnp.where(items[s : s + 1] == item_row, cross[s : s + 1], 0.0)
    row_margin = jnp.sum(held, axis=1, keepdims=True)
    totals = jnp.where(lane == SPOT, raw_items, 0).astype(jnp.float32) + cross
    pair_total = jnp.sum(jnp.sum(totals, axis=0, keepdims=True), axis=1, keepdims=True)
    col_margin = jnp.concatenate(
        [counts[pl.ds(ROWS, 1), pl.ds(0, OWNED)], jnp.sum(held.T, axis=0, keepdims=True)], axis=1
    )
    positive = ppmi(counts[pl.ds(0, ROWS), :], row_margin, col_margin, pair_total)
    copy.wait()
    held_words = jnp.concatenate([words[...], row_bits_ref[...]], axis=1)
    for b in range(WORD_BITS):
        sign = jnp.where((held_words >> b) & 1 == 1, 1.0, -1.0)
        for j in range(COLS // LANES):
            wide_signs[j, pl.ds(b, WORDS, stride=WORD_BITS), :] = sign[:, j * LANES : (j + 1) * LANES]
    parts = two_parts(positive)
    signs = [wide_signs[j, pl.ds(0, SKETCH), :].astype(jnp.bfloat16) for j in range(COLS // LANES)]
    result = nt_dot(parts, jnp.concatenate(signs, axis=1))
    result = result[:ROWS] + result[ROWS:]
    for s in range(SLABS):
        out_ref[s] = result[s * ROWS_DEV : (s + 1) * ROWS_DEV]


def route(where, items, sessions, interpret=False):
    return pl.pallas_call(
        lambda *refs: route_kernel(where, *refs),
        out_shape=jax.ShapeDtypeStruct((SLABS, MESSAGE, LANES), jnp.int32),
        in_specs=[pl.BlockSpec(memory_space=pltpu.HBM)] * 2,
        out_specs=pl.BlockSpec(memory_space=pltpu.VMEM),
        scratch_shapes=[
            pltpu.VMEM((SLAB_ROWS, LANES), jnp.int32),
            pltpu.VMEM((SLAB_ROWS, LANES), jnp.int32),
            pltpu.VMEM((2 * PAD + SLAB_ROWS, LANES), jnp.float32),
            pltpu.VMEM((LANES, 5 * LANES), jnp.bfloat16),
            pltpu.VMEM((SLABS * QUOTA, LANES), jnp.int32),
            pltpu.VMEM((ROWS, SLAB_ROWS * LANES), jnp.bfloat16),
            pltpu.VMEM((ROWS + 16, SLAB_ROWS * LANES), jnp.bfloat16),
            pltpu.SemaphoreType.DMA((2,)),
        ],
        compiler_params=pltpu.CompilerParams(vmem_limit_bytes=VMEM_BYTES),
        interpret=interpret,
        name="route_events",
    )(items, sessions)


def sketch_part(where, got, bits, interpret=False):
    return pl.pallas_call(
        lambda *refs: sketch_kernel(where, *refs),
        out_shape=(
            jax.ShapeDtypeStruct((SLABS, ROWS_DEV, SKETCH), jnp.float32),
            jax.ShapeDtypeStruct((1, 1), jnp.int32),
        ),
        grid=(1,),
        in_specs=[
            pl.BlockSpec((SLABS, MESSAGE, LANES), lambda i: (0, 0, 0)),
            pl.BlockSpec((WORDS, LANES), lambda i: (0, 0)),
            pl.BlockSpec(memory_space=pltpu.HBM),
        ],
        out_specs=(
            pl.BlockSpec((SLABS, ROWS_DEV, SKETCH), lambda i: (0, 0, 0)),
            pl.BlockSpec(memory_space=pltpu.SMEM),
        ),
        scratch_shapes=[
            pltpu.VMEM((ROWS + 16, COLS), jnp.float32),
            pltpu.VMEM((LANES, 4 * LANES), jnp.bfloat16),
            pltpu.VMEM((WORDS, OWNED), jnp.int32),
            pltpu.VMEM((COLS // LANES, 16 * WORD_BITS, LANES), jnp.float32),
            pltpu.SemaphoreType.DMA,
        ],
        compiler_params=pltpu.CompilerParams(vmem_limit_bytes=VMEM_BYTES),
        interpret=interpret,
        name="sketch_part",
    )(got, bits, bits)


def shares(part):
    rows = jnp.sum(lax.all_to_all(part, "stream", 0, 0, tiled=True), axis=0)
    spread = jnp.broadcast_to(rows[None], (BANDS,) + rows.shape)
    return lax.all_to_all(spread, "item", 0, 0, tiled=True)


def local(event_items, event_sessions, sketch_bits):
    def where():
        return lax.axis_index("stream"), lax.axis_index("item")

    items = event_items.reshape(SLAB_ROWS, LANES)
    sessions = event_sessions.reshape(SLAB_ROWS, LANES)

    def from_every_event(_):
        message = all_events(where, items, sessions, sketch_bits)
        own = lax.all_to_all(message, "stream", 0, 0, tiled=True)
        other = lax.ppermute(own, "item", [(i, i ^ 1) for i in range(BANDS)])
        return shares(from_all(where, own, other, sketch_bits))

    routed = lax.all_to_all(route(where, items, sessions), "stream", 0, 0, tiled=True)
    part, spoilt = sketch_part(where, routed, sketch_bits)
    gathered = lax.cond(spoilt[0, 0] > 0, from_every_event, lambda kept: kept, shares(part))
    return jnp.sum(gathered, axis=0) / math.sqrt(EVENT_ROWS * LANES)


def solution(mesh):
    placed = (P("stream"), P("stream"), P(None, "item"))
    return jax.shard_map(
        local, mesh=mesh, in_specs=placed, out_specs=P("stream", None), check_vma=False
    )
```

```python
import math

import jax
import jax.numpy as jnp
from jax import lax
from jax.experimental import pallas as pl
from jax.experimental.pallas import tpu as pltpu
from jax.sharding import PartitionSpec as P

SKETCH = 256
WINDOW = 15
ROWS = 128
ROWS_DEV = 4
LANES = 128
SLABS = 32
BANDS = 8
SLAB_ROWS = 32
HALF_ROWS = SLAB_ROWS // 2
PAYLOAD = 32
EVENT_ROWS = SLABS * SLAB_ROWS
OWNED = 1024
COLS = OWNED + ROWS
WORD_BITS = 18
WORDS = 15
SLOTS = 384
PAD = 8
MARGIN_ROW, TOTAL_ROW, BITS_ROW = 24, 25, 26
QUOTA = 32
MESSAGE = 8
HALF = LANES // 2
NONE = 255.0
SPOT = HALF + 16
VMEM_BYTES = 48 << 20
COUNT = jnp.bfloat16


def iota(shape, axis, dtype=jnp.int32):
    out = lax.broadcasted_iota(jnp.int32, shape, axis)
    return out if dtype == jnp.int32 else out.astype(dtype)


def nt_dot(left, right):
    return lax.dot_general(
        left, right, (((1,), (1,)), ((), ())), preferred_element_type=jnp.float32
    )


def hot(mask):
    return jnp.where(mask, 1.0, 0.0)


def ppmi(count, row_margin, col_margin, pair_total):
    log_ratio = (
        jnp.log(jnp.maximum(count, 1.0))
        + jnp.log(pair_total)
        - jnp.log(jnp.maximum(row_margin, 1.0))
        - jnp.log(jnp.maximum(col_margin, 1.0))
    )
    return jnp.where(count > 0, jnp.maximum(log_ratio, 0.0), 0.0)


def split(values):
    high = values.astype(jnp.bfloat16)
    rest = values - high.astype(jnp.float32)
    mid = rest.astype(jnp.bfloat16)
    low = (rest - mid.astype(jnp.float32)).astype(jnp.bfloat16)
    return jnp.concatenate([high, mid, low], axis=0)


def two_parts(values):
    high = values.astype(jnp.bfloat16)
    low = (values - high.astype(jnp.float32)).astype(jnp.bfloat16)
    return jnp.concatenate([high, low], axis=0)


def joined(parts):
    third = parts.shape[0] // 3
    return parts[:third] + (parts[third : 2 * third] + parts[2 * third :])


def fill_signs(held_words, signs):
    held_words = jnp.concatenate([held_words, jnp.zeros((1, COLS), jnp.int32)], axis=0)
    for b in range(WORD_BITS):
        signs[pl.ds(b * 16, 16), :] = jnp.where((held_words >> b) & 1 == 1, 1.0, -1.0).astype(jnp.bfloat16)


def project(positive, signs):
    by_bit = joined(nt_dot(split(positive), signs[...]))
    have = iota((16 * WORD_BITS, SKETCH), 0)
    want = iota((16 * WORD_BITS, SKETCH), 1)
    order = hot((have & 15) * WORD_BITS + (have >> 4) == want).astype(jnp.bfloat16)
    return joined(jnp.dot(split(by_bit), order, preferred_element_type=jnp.float32))


def all_events_kernel(where, items_ref, sessions_ref, bits_ref, out_ref):
    _, band = where()
    half = lax.rem(band, 2)
    items, sessions = items_ref[...], sessions_ref[...]
    shape = items.shape
    row, lane = iota(shape, 0), iota(shape, 1)
    above = jnp.where(row == 0, -1, pltpu.roll(sessions, 1, 0))
    below = jnp.where(row == SLAB_ROWS - 1, -1, pltpu.roll(sessions, SLAB_ROWS - 1, 0))
    weights = jnp.zeros(shape, jnp.float32)
    for d in range(1, WINDOW + 1):
        earlier = pltpu.roll(jnp.where(lane >= LANES - d, above, sessions), d, 1)
        later = pltpu.roll(jnp.where(lane < d, below, sessions), LANES - d, 1)
        weights += hot(earlier == sessions) + hot(later == sessions)
    held = jnp.zeros((ROWS, LANES), jnp.float32)
    item_row = iota((ROWS, LANES), 0)
    for r in range(SLAB_ROWS):
        held += jnp.where(items[r : r + 1] == item_row, weights[r : r + 1], 0.0)
    margin = jnp.sum(held.T, axis=0, keepdims=True).astype(jnp.int32)
    total = jnp.sum(weights, axis=0, keepdims=True).astype(jnp.int32)
    own_items = jnp.where(half == 0, items[:HALF_ROWS], items[HALF_ROWS:])
    own_sessions = jnp.where(half == 0, sessions[:HALF_ROWS], sessions[HALF_ROWS:])
    pairs = own_sessions[:8] + own_sessions[8:] * 65536
    slab, _ = where()
    word = bits_ref[...]
    one = jnp.sum(
        jnp.where(iota(word.shape, 0) == jnp.minimum(slab, WORDS - 1), word, 0),
        axis=0,
        keepdims=True,
    )
    extra = jnp.concatenate([margin, total, one, jnp.zeros((5, LANES), jnp.int32)], axis=0)
    message = jnp.concatenate([own_items, pairs, extra], axis=0)
    for s in range(SLABS):
        out_ref[s] = message


def from_all_kernel(
    where, own_ref, other_ref, bits_hbm, out_ref,
    sess, codes, mask, table, counts, words, signs, sem,
):
    slab, band = where()
    half = lax.rem(band, 2)
    copy = pltpu.make_async_copy(
        bits_hbm.at[:, pl.ds(pl.multiple_of(slab * OWNED, OWNED), OWNED)],
        words,
        sem,
    )
    copy.start()
    lane_s = iota((SLAB_ROWS, LANES), 1)
    block_id = band * SLABS + slab
    pair_id = jnp.where(band < 2, 2 * slab + half, -1)

    edge = jnp.full((PAD, LANES), -(ROWS + 1.0), jnp.float32)
    codes[pl.ds(0, PAD), :] = edge
    codes[pl.ds(PAD + EVENT_ROWS, PAD), :] = edge
    sess[pl.ds(0, PAD), :] = jnp.full((PAD, LANES), -1, jnp.int32)

    def halves(s):
        mine, its = own_ref[s], other_ref[s]
        return jnp.where(half == 0, mine, its), jnp.where(half == 0, its, mine)

    def unpack(s, carry):
        first, second = halves(s)
        items = jnp.concatenate([first[:16], second[:16]], axis=0)
        a, b = first[16:24], second[16:24]
        sessions = jnp.concatenate([a & 65535, a >> 16, b & 65535, b >> 16], axis=0)
        base = pl.multiple_of(s * SLAB_ROWS, SLAB_ROWS)
        sess[pl.ds(PAD + base, SLAB_ROWS), :] = sessions
        above = sess[pl.ds(PAD - 1 + base, SLAB_ROWS), :]
        before = pltpu.roll(jnp.where(lane_s == LANES - 1, above, sessions), 1, 1)
        value = jnp.minimum(items, ROWS) + 1
        codes[pl.ds(PAD + base, SLAB_ROWS), :] = jnp.where(
            before != sessions, -value, value
        ).astype(jnp.float32)
        is_row = items < ROWS
        owned = jnp.where(is_row, items >> 1, items >> 10) == jnp.where(is_row, pair_id, block_id)
        ident = jnp.where(is_row, OWNED + items, items & (OWNED - 1))
        rows = pl.ds(base, SLAB_ROWS)
        mask[rows, :] = hot(owned).astype(jnp.bfloat16)
        table[rows, pl.ds(LANES, LANES)] = (ident & 255).astype(jnp.float32).astype(jnp.bfloat16)
        table[rows, pl.ds(2 * LANES, LANES)] = (ident >> 8).astype(jnp.float32).astype(jnp.bfloat16)
        return carry

    lax.fori_loop(0, SLABS, unpack, 0, unroll=4)
    for r in range(0, EVENT_ROWS, 128):
        rows = pl.ds(r, 128)
        table[rows, pl.ds(3 * LANES, LANES)] = codes[pl.ds(PAD - 1 + r, 128), :].astype(jnp.bfloat16)
        table[rows, pl.ds(4 * LANES, LANES)] = codes[pl.ds(PAD + r, 128), :].astype(jnp.bfloat16)
        table[rows, pl.ds(5 * LANES, LANES)] = codes[pl.ds(PAD + 1 + r, 128), :].astype(jnp.bfloat16)

    upto = hot(iota((LANES, LANES), 0) <= iota((LANES, LANES), 1)).astype(jnp.bfloat16)
    owned = mask[...]
    rank = jnp.dot(owned, upto, preferred_element_type=jnp.float32)
    table[:, pl.ds(0, LANES)] = (rank * owned.astype(jnp.float32)).astype(jnp.bfloat16)
    per_row = nt_dot(jnp.ones((8, LANES), jnp.bfloat16), owned)
    groups = EVENT_ROWS // LANES
    grouped = jnp.concatenate(
        [per_row[:1, g * LANES : (g + 1) * LANES] for g in range(groups)], axis=0
    )
    inside = jnp.dot(grouped.astype(jnp.bfloat16), upto, preferred_element_type=jnp.float32)
    ends, starts, base = [], [], jnp.zeros((1, 1), jnp.float32)
    for g in range(groups):
        ends.append(inside[g : g + 1] + base)
        starts.append(ends[g] - grouped[g : g + 1])
        base = base + inside[g : g + 1, LANES - 1 :]
    owned_events = jnp.max(base).astype(jnp.int32)

    counts[...] = jnp.zeros(counts.shape, jnp.float32)
    lane_f = iota((SLOTS, LANES), 1, jnp.float32)
    row32, col32 = iota((32, 32), 0), iota((32, 32), 1)
    ahead = (row32 > WINDOW) & (col32 > WINDOW) & (col32 <= row32)
    behind = (row32 < WINDOW) & (col32 > row32) & (col32 <= WINDOW)
    between = hot(ahead | behind).astype(jnp.bfloat16)
    place = iota((32, SLOTS), 0)
    in_window = (place != WINDOW) & (place <= 2 * WINDOW)
    row_ids = iota((ROWS, SLOTS), 0, jnp.float32)
    col_ids = iota((SLOTS, COLS), 1, jnp.float32)

    def chunk(step, carry):
        slot = (step * SLOTS + iota((SLOTS, LANES), 0)).astype(jnp.float32)
        picks, first = [], jnp.zeros((SLOTS, LANES), jnp.float32)
        for g in range(groups):
            here = (slot >= starts[g]) & (slot < ends[g])
            first += jnp.where(here, starts[g], 0.0)
            picks.append(hot(here).astype(jnp.bfloat16))
        pick = jnp.concatenate(picks, axis=1)
        got = jnp.dot(pick, table[...], preferred_element_type=jnp.float32)
        ordinal = slot[:, :1] + 1.0 - jnp.sum(first, axis=1, keepdims=True)
        chosen = got[:, :LANES] == ordinal
        ident = got[:, LANES : 2 * LANES] + 256.0 * got[:, 2 * LANES : 3 * LANES]
        column = jnp.sum(jnp.where(chosen, ident + 1.0, 0.0), axis=1, keepdims=True) - 1.0
        at_lane = jnp.sum(jnp.where(chosen, lane_f, 0.0), axis=1, keepdims=True)
        source = at_lane.astype(jnp.int32) + (iota((SLOTS, LANES), 1) - WINDOW)
        index = source & (LANES - 1)
        parts = [
            jnp.take_along_axis(got[:, k * LANES : (k + 1) * LANES], index, axis=1, mode="promise_in_bounds")
            for k in (3, 4, 5)
        ]
        window = jnp.where(source < 0, parts[0], jnp.where(source < LANES, parts[1], parts[2]))
        window = window.T[:32]
        breaks = hot(window < 0.0).astype(jnp.bfloat16)
        crossed = jnp.dot(between, breaks, preferred_element_type=jnp.float32)
        linked = (crossed == 0.0) & in_window
        near = jnp.where(linked, jnp.abs(window) - 1.0, 255.0)
        weight = jnp.sum(hot(linked), axis=0, keepdims=True)
        pairs = jnp.zeros((ROWS, SLOTS), jnp.float32)
        for d in range(2 * WINDOW + 1):
            if d != WINDOW:
                pairs += hot(near[d : d + 1] == row_ids)
        pairs = jnp.concatenate([pairs, jnp.broadcast_to(weight, (16, SLOTS))], axis=0)
        column_hot = hot(column == col_ids).astype(jnp.bfloat16)
        counts[...] += jnp.dot(
            pairs.astype(jnp.bfloat16), column_hot, preferred_element_type=jnp.float32
        )
        return carry

    lax.fori_loop(0, (owned_events + SLOTS - 1) // SLOTS, chunk, 0)

    def both(row_first, row_second):
        mine_f, its_f = own_ref[:, row_first, :], other_ref[:, row_first, :]
        mine_s, its_s = own_ref[:, row_second, :], other_ref[:, row_second, :]
        return jnp.where(half == 0, mine_f, its_f), jnp.where(half == 0, its_s, mine_s)

    start_items, end_items = both(0, 15)
    start_sess, end_sess = both(16, 23)
    start_sess, end_sess = start_sess & 65535, end_sess >> 16
    slab_row = iota((SLABS, LANES), 0)
    end_items = pltpu.roll(end_items, 1, 0)
    end_sess = jnp.where(slab_row == 0, -1, pltpu.roll(end_sess, 1, 0))
    cross = jnp.zeros((SLABS, LANES), jnp.float32)
    lane = iota((SLABS, LANES), 1)
    for d in range(1, WINDOW + 1):
        before = pltpu.roll(end_sess, d, 1)
        after = pltpu.roll(start_sess, LANES - d, 1)
        cross += hot((lane < d) & (before == start_sess))
        cross += hot((lane >= LANES - d) & (after == end_sess))
    cross_items = jnp.where(lane < LANES // 2, start_items, end_items)
    margins = jnp.sum(own_ref[:, MARGIN_ROW, :], axis=0, keepdims=True).astype(jnp.float32)
    item_row = iota((ROWS, LANES), 0)
    held = jnp.where(item_row == iota((ROWS, LANES), 1), margins, 0.0)
    for s in range(SLABS):
        held += jnp.where(cross_items[s : s + 1] == item_row, cross[s : s + 1], 0.0)
    row_margin = jnp.sum(held, axis=1, keepdims=True)
    totals = jnp.sum(own_ref[:, TOTAL_ROW, :], axis=0, keepdims=True).astype(jnp.float32)
    totals = totals + jnp.sum(cross, axis=0, keepdims=True)
    pair_total = jnp.sum(totals, axis=1, keepdims=True)

    positive = ppmi(
        counts[pl.ds(0, ROWS), :], row_margin, counts[pl.ds(ROWS, 1), :], pair_total
    )
    copy.wait()
    row_words = jnp.where(half == 0, own_ref[:WORDS, BITS_ROW, :], other_ref[:WORDS, BITS_ROW, :])
    fill_signs(jnp.concatenate([words[...], row_words], axis=1), signs)
    result = project(positive, signs)
    for s in range(SLABS):
        out_ref[s] = result[s * ROWS_DEV : (s + 1) * ROWS_DEV]


def all_events(where, items, sessions, bits, interpret=False):
    return pl.pallas_call(
        lambda *refs: all_events_kernel(where, *refs),
        out_shape=jax.ShapeDtypeStruct((SLABS, PAYLOAD, LANES), jnp.int32),
        grid=(1,),
        in_specs=[
            pl.BlockSpec((SLAB_ROWS, LANES), lambda i: (0, 0)),
            pl.BlockSpec((SLAB_ROWS, LANES), lambda i: (0, 0)),
            pl.BlockSpec((WORDS, LANES), lambda i: (0, 0)),
        ],
        out_specs=pl.BlockSpec((SLABS, PAYLOAD, LANES), lambda i: (0, 0, 0)),
        compiler_params=pltpu.CompilerParams(vmem_limit_bytes=VMEM_BYTES),
        interpret=interpret,
        name="all_events",
    )(items, sessions, bits)


def from_all(where, own, other, bits, interpret=False):
    return pl.pallas_call(
        lambda *refs: from_all_kernel(where, *refs),
        out_shape=jax.ShapeDtypeStruct((SLABS, ROWS_DEV, SKETCH), jnp.float32),
        in_specs=[
            pl.BlockSpec(memory_space=pltpu.VMEM),
            pl.BlockSpec(memory_space=pltpu.VMEM),
            pl.BlockSpec(memory_space=pl.ANY),
        ],
        out_specs=pl.BlockSpec(memory_space=pltpu.VMEM),
        scratch_shapes=[
            pltpu.VMEM((PAD + EVENT_ROWS, LANES), jnp.int32),
            pltpu.VMEM((2 * PAD + EVENT_ROWS, LANES), jnp.float32),
            pltpu.VMEM((EVENT_ROWS, LANES), jnp.bfloat16),
            pltpu.VMEM((EVENT_ROWS, 6 * LANES), jnp.bfloat16),
            pltpu.VMEM((ROWS + 16, COLS), jnp.float32),
            pltpu.VMEM((WORDS, OWNED), jnp.int32),
            pltpu.VMEM((16 * WORD_BITS, COLS), jnp.bfloat16),
            pltpu.SemaphoreType.DMA,
        ],
        compiler_params=pltpu.CompilerParams(vmem_limit_bytes=VMEM_BYTES),
        interpret=interpret,
        name="from_all",
    )(own, other, bits)


def route_kernel(where, items_hbm, sessions_hbm, out_ref, items_v, sessions_v, codes, table, near_rows, one_hots, pair_rows, sems):
    slab, band = where()
    get_items = pltpu.make_async_copy(items_hbm, items_v, sems.at[0])
    get_sessions = pltpu.make_async_copy(sessions_hbm, sessions_v, sems.at[1])
    get_items.start()
    get_sessions.start()
    get_items.wait()
    get_sessions.wait()
    items, sessions = items_v[...], sessions_v[...]
    shape = items.shape
    row, lane = iota(shape, 0), iota(shape, 1)
    above = jnp.where(row == 0, -1, pltpu.roll(sessions, 1, 0))
    below = jnp.where(row == SLAB_ROWS - 1, -1, pltpu.roll(sessions, SLAB_ROWS - 1, 0))
    earlier_links = jnp.zeros(shape, jnp.float32)
    later_links = jnp.zeros(shape, jnp.float32)
    for d in range(1, WINDOW + 1):
        earlier = pltpu.roll(jnp.where(lane >= LANES - d, above, sessions), d, 1)
        later = pltpu.roll(jnp.where(lane < d, below, sessions), LANES - d, 1)
        earlier_links += hot(earlier == sessions)
        later_links += hot(later == sessions)
    weights = earlier_links + later_links

    one, none = jnp.ones((), jnp.bfloat16), jnp.zeros((), jnp.bfloat16)
    item_codes = jnp.minimum(items, 255).astype(jnp.float32).astype(jnp.bfloat16)
    row_ids = iota((ROWS, LANES), 0, jnp.float32).astype(jnp.bfloat16)
    for r in range(SLAB_ROWS):
        same = item_codes[r : r + 1] == row_ids
        one_hots[:, pl.ds(r * LANES, LANES)] = jnp.where(same, one, none)
        pair_rows[pl.ds(ROWS, 16), pl.ds(r * LANES, LANES)] = jnp.broadcast_to(
            weights[r : r + 1], (16, LANES)
        ).astype(jnp.bfloat16)
    total = jnp.sum(weights, axis=0, keepdims=True)
    first_link = (iota(shape, 1, jnp.float32) - earlier_links).astype(jnp.bfloat16)
    place = iota((LANES, LANES), 0, jnp.float32).astype(jnp.bfloat16)
    sooner = iota((LANES, LANES), 0) < iota((LANES, LANES), 1)
    sooner = jnp.where(sooner, place, jnp.full((), -64.0, jnp.bfloat16))
    last = (iota((16, LANES), 0, jnp.float32) - 16.0).astype(jnp.bfloat16)
    ordered = jnp.zeros((ROWS + 16, ROWS), jnp.float32)
    no_links = jnp.zeros((LANES - 16, LANES), jnp.bfloat16)
    for r in range(SLAB_ROWS):
        begin = first_link[r : r + 1]
        links = jnp.where(sooner >= begin, one, none)
        if r == 0:
            pairs = jnp.dot(one_hots[:, pl.ds(0, LANES)], links, preferred_element_type=jnp.float32)
        else:
            links = jnp.concatenate([no_links, jnp.where(last >= begin, one, none), links], axis=0)
            pairs = jnp.dot(
                one_hots[:, pl.ds((r - 1) * LANES, 2 * LANES)], links, preferred_element_type=jnp.float32
            )
        pair_rows[pl.ds(0, ROWS), pl.ds(r * LANES, LANES)] = pairs.astype(jnp.bfloat16)
        if r % 4 == 3:
            ready = pl.ds((r - 3) * LANES, 4 * LANES)
            ordered += nt_dot(pair_rows[:, ready], one_hots[:, ready])
    margin = ordered[ROWS : ROWS + 1]
    ordered = ordered[:ROWS]
    row_pairs = ordered + ordered.T
    item_row = iota((ROWS, LANES), 0)

    before = pltpu.roll(jnp.where(lane == LANES - 1, above, sessions), 1, 1)
    value = jnp.minimum(items, ROWS) + 1
    edge = jnp.full((PAD, LANES), -(ROWS + 1.0), jnp.float32)
    codes[pl.ds(0, PAD), :] = edge
    codes[pl.ds(PAD + SLAB_ROWS, PAD), :] = edge
    codes[pl.ds(PAD, SLAB_ROWS), :] = jnp.where(before != sessions, -value, value).astype(jnp.float32)
    inside = items - band * (SLABS * OWNED)
    wide = (items >= ROWS) & (inside >= 0) & (inside < SLABS * OWNED)
    inside = jnp.where(wide, inside, 0)
    owner = jnp.where(wide, inside >> 10, -1)
    owner_row = iota((SLABS, LANES), 0)
    marks = [hot(owner[r : r + 1] == owner_row) for r in range(SLAB_ROWS)]
    upto = hot(iota((LANES, LANES), 0) <= iota((LANES, LANES), 1)).astype(jnp.bfloat16)
    ranks = jnp.dot(
        jnp.concatenate(marks, axis=0).astype(jnp.bfloat16), upto, preferred_element_type=jnp.float32
    )
    ranks = [ranks[r * SLABS : (r + 1) * SLABS] for r in range(SLAB_ROWS)]
    per_row = jnp.zeros((SLABS, LANES), jnp.float32)
    for r in range(SLAB_ROWS):
        per_row = jnp.where(lane == r, ranks[r][:, LANES - 1 :], per_row)
    ends = jnp.dot(per_row.astype(jnp.bfloat16), upto, preferred_element_type=jnp.float32)
    starts = ends - per_row
    block = jnp.where(items >= ROWS, items >> 10, -1)
    sixteen = iota((16, LANES), 0)
    upper = [hot((block[r : r + 1] >> 4) == sixteen) for r in range(SLAB_ROWS)]
    lower = [hot((block[r : r + 1] & 15) == sixteen) for r in range(SLAB_ROWS)]
    loads = nt_dot(
        jnp.concatenate(upper, axis=1).astype(jnp.bfloat16),
        jnp.concatenate(lower, axis=1).astype(jnp.bfloat16),
    )
    most = jnp.max(jnp.max(loads, axis=0, keepdims=True), axis=1, keepdims=True)
    orders = [
        jnp.sum(marks[r] * (ranks[r] + starts[:, r : r + 1]), axis=0, keepdims=True)
        for r in range(SLAB_ROWS)
    ]
    table[pl.ds(SLAB_ROWS, LANES - SLAB_ROWS), :] = jnp.zeros((LANES - SLAB_ROWS, 5 * LANES), jnp.bfloat16)
    row_codes = codes[pl.ds(PAD, SLAB_ROWS), :]
    left = jnp.where(lane >= LANES - 32, codes[pl.ds(PAD - 1, SLAB_ROWS), :], row_codes)
    right = jnp.where(lane < 32, codes[pl.ds(PAD + 1, SLAB_ROWS), :], row_codes)
    fields = [
        jnp.minimum(jnp.concatenate(orders, axis=0), 255.0),
        (inside & 255).astype(jnp.float32),
        (inside >> 8).astype(jnp.float32),
        pltpu.roll(left, 32, 1),
        pltpu.roll(right, LANES - 32, 1),
    ]
    for k, field in enumerate(fields):
        table[pl.ds(0, SLAB_ROWS), pl.ds(k * LANES, LANES)] = field.astype(jnp.bfloat16)
    slot = iota((QUOTA, LANES), 0, jnp.float32)
    picks = [
        hot((slot >= starts[s : s + 1]) & (slot < ends[s : s + 1])).astype(jnp.bfloat16)
        for s in range(SLABS)
    ]
    got = jnp.dot(jnp.concatenate(picks, axis=0), table[...], preferred_element_type=jnp.float32)
    big = (SLABS * QUOTA, LANES)
    number, lanes = iota(big, 0), iota(big, 1)
    target = (number >> 5).astype(jnp.float32) * 4.0
    high = got[:, 2 * LANES : 3 * LANES] - target
    ordinal = ((number & (QUOTA - 1)) + 1).astype(jnp.float32)
    chosen = (got[:, :LANES] == ordinal) & (high >= 0.0) & (high < 4.0)
    ident = got[:, LANES : 2 * LANES] + 256.0 * high + 1.0
    found = jnp.sum(
        jnp.where(chosen, ident * LANES + lanes.astype(jnp.float32), 0.0), axis=1, keepdims=True
    ).astype(jnp.int32)
    column = (((found >> 7) - 1) & 4095).astype(jnp.float32)
    at_lane = found & (LANES - 1)
    index = ((at_lane & (HALF - 1)) + (32 - WINDOW) + lanes) & (LANES - 1)
    reach = jnp.where(at_lane < HALF, got[:, 3 * LANES : 4 * LANES], got[:, 4 * LANES :])
    window = jnp.take_along_axis(reach, index, axis=1, mode="promise_in_bounds")
    from_lane, to_lane = iota((LANES, LANES), 0), iota((LANES, LANES), 1)
    ahead = (to_lane > WINDOW) & (from_lane > WINDOW) & (from_lane <= to_lane)
    behind = (to_lane < WINDOW) & (from_lane > to_lane) & (from_lane <= WINDOW)
    between = hot(ahead | behind).astype(jnp.bfloat16)
    crossed = jnp.dot(
        hot(window < 0.0).astype(jnp.bfloat16), between, preferred_element_type=jnp.float32
    )
    linked = (crossed == 0.0) & (lanes <= 2 * WINDOW)
    near = jnp.where(linked, jnp.abs(window) - 1.0, NONE)
    near = jnp.where(lanes == WINDOW, column, near)
    near_rows[...] = (near + 4096.0 * pltpu.roll(near, LANES - 16, 1)).astype(jnp.int32)

    whole = jnp.where(item_row == iota((ROWS, LANES), 1), ordered, row_pairs).astype(jnp.int32)
    packed = pltpu.roll(whole, HALF, 1) + jnp.where(iota((ROWS, LANES), 1) >= HALF, whole * 65536, 0)
    ends_lane = iota((1, LANES), 1)
    spare = jnp.where(most > QUOTA, 1, 0)
    total = jnp.sum(total, axis=1, keepdims=True).astype(jnp.int32)
    margin = margin.astype(jnp.int32)

    def edges(values, single):
        both = jnp.where(ends_lane < LANES - 32, pltpu.roll(values[:1], HALF, 1), values[SLAB_ROWS - 1 :])
        return jnp.where(ends_lane == SPOT, single, both)

    common = jnp.concatenate(
        [pltpu.roll(margin, HALF, 1), margin, edges(items, total), edges(sessions, spare)], axis=0
    )
    sixteenth = iota((8, LANES), 1) >> 4
    for s in range(SLABS):
        rows = jnp.concatenate([packed[s * ROWS_DEV : (s + 1) * ROWS_DEV], common], axis=0)
        for g in range(QUOTA // 8):
            part = near_rows[pl.ds(s * QUOTA + 8 * g, 8), :]
            rows = jnp.where(sixteenth == g, pltpu.roll(part, 16 * g, 1) if g else part, rows)
        out_ref[s] = rows


def count_pairs(near, skip):
    slots = near.shape[1]
    place = iota(near.shape, 0)
    real = near < NONE
    for d in skip:
        real = real & (place != d)
    weight = jnp.sum(hot(real), axis=0, keepdims=True)
    row_ids = iota((ROWS, slots), 0, jnp.float32).astype(COUNT)
    one, none = jnp.ones((), COUNT), jnp.zeros((), COUNT)
    pairs = jnp.zeros((ROWS, slots), COUNT)
    near = near.astype(COUNT)
    for d in range(near.shape[0]):
        if d not in skip:
            pairs += jnp.where(near[d : d + 1] == row_ids, one, none)
    weight = jnp.broadcast_to(weight, (16, slots)).astype(jnp.bfloat16)
    return jnp.concatenate([pairs.astype(jnp.bfloat16), weight], axis=0)


def sketch_kernel(
    where, got_ref, row_bits_ref, bits_hbm, out_ref, spoilt_ref, counts, table, words, wide_signs, sem
):
    slab, band = where()
    copy = pltpu.make_async_copy(
        bits_hbm.at[:, pl.ds(pl.multiple_of(slab * OWNED, OWNED), OWNED)], words, sem
    )
    copy.start()

    slab_row, lane = iota((SLABS, LANES), 0), iota((SLABS, LANES), 1)
    raw_items, raw_sessions = got_ref[:, 6, :], got_ref[:, 7, :]
    edge_items = jnp.where(lane < HALF, pltpu.roll(raw_items, HALF, 1), raw_items)
    edge_sessions = jnp.where(lane < HALF, pltpu.roll(raw_sessions, HALF, 1), raw_sessions)
    spoilt_ref[0, 0] = jnp.max(jnp.where(lane == SPOT, raw_sessions, 0))
    end_items = pltpu.roll(edge_items, 1, 0)
    end_sess = jnp.where(slab_row == 0, -1, pltpu.roll(edge_sessions, 1, 0))
    cross = jnp.zeros((SLABS, LANES), jnp.float32)
    for d in range(1, WINDOW + 1):
        before = pltpu.roll(end_sess, d, 1)
        after = pltpu.roll(edge_sessions, LANES - d, 1)
        cross += hot((lane < d) & (before == edge_sessions))
        cross += hot((lane >= LANES - d) & (after == end_sess))
    items = jnp.where(lane < HALF, edge_items, end_items)
    over = jnp.where(
        lane < HALF,
        hot((edge_sessions == end_sess[:, LANES - 1 :]) & (lane < WINDOW)),
        hot((end_sess == edge_sessions[:, :1]) & (lane >= LANES - WINDOW)),
    )
    partner = jnp.where(over > 0.0, jnp.minimum(items, ROWS).astype(jnp.float32), NONE)
    is_row = items < ROWS
    row_owner = jnp.where(band == 0, slab, -1)
    owned = jnp.where(is_row, items >> 2, items >> 10) == jnp.where(is_row, row_owner, band * SLABS + slab)
    owned = hot(owned & (cross > 0.0))
    local_id = jnp.where(is_row, OWNED + items, items & (OWNED - 1))
    upto = hot(iota((LANES, LANES), 0) <= iota((LANES, LANES), 1)).astype(jnp.bfloat16)
    blank = jnp.zeros((LANES - SLABS, LANES), jnp.float32)
    marks = jnp.concatenate([owned, blank], axis=0).astype(jnp.bfloat16)
    rank = jnp.dot(marks, upto, preferred_element_type=jnp.float32)
    per_row = nt_dot(jnp.ones((8, LANES), jnp.bfloat16), marks)
    ends = jnp.dot(per_row.astype(jnp.bfloat16), upto, preferred_element_type=jnp.float32)
    starts = (ends - per_row)[:1]
    ends = ends[:1]
    crossing = jnp.max(ends).astype(jnp.int32)
    fields = [
        rank[:SLABS] * owned,
        (local_id & 255).astype(jnp.float32),
        (local_id >> 8).astype(jnp.float32),
        partner,
    ]
    for k, field in enumerate(fields):
        table[:, pl.ds(k * LANES, LANES)] = jnp.concatenate([field, blank], axis=0).astype(jnp.bfloat16)
    slot_lane = iota((LANES, LANES), 1)
    col_ids = iota((LANES, COLS), 1, jnp.float32)

    def crossed(step):
        slot = (step * LANES + iota((LANES, LANES), 0)).astype(jnp.float32)
        here = (slot >= starts) & (slot < ends)
        first = jnp.sum(jnp.where(here, starts, 0.0), axis=1, keepdims=True)
        got = jnp.dot(hot(here).astype(jnp.bfloat16), table[...], preferred_element_type=jnp.float32)
        chosen = got[:, :LANES] == slot[:, :1] + 1.0 - first
        ident = got[:, LANES : 2 * LANES] + 256.0 * got[:, 2 * LANES : 3 * LANES]
        column = jnp.sum(jnp.where(chosen, ident + 1.0, 0.0), axis=1, keepdims=True) - 1.0
        at = jnp.sum(jnp.where(chosen, slot_lane, 0), axis=1, keepdims=True)
        reach = LANES - WINDOW
        other_side = jnp.where(at < HALF, hot(slot_lane >= reach + at), hot(slot_lane <= at - reach))
        near = jnp.where(other_side > 0.0, got[:, 3 * LANES :], NONE).T
        near = jnp.concatenate([near[:16], near[LANES - 16 :]], axis=0)
        pairs = count_pairs(near, (15, 16))
        column_hot = hot(column == col_ids).astype(jnp.bfloat16)
        return jnp.dot(pairs, column_hot, preferred_element_type=jnp.float32)

    first_crossed = crossed(0)

    windows = got_ref[...].reshape(SLABS * MESSAGE, LANES).T[:HALF]
    low, high = (windows & 4095).astype(jnp.float32), (windows >> 12).astype(jnp.float32)
    blocks, idents = [], []
    for g in range(QUOTA // 8):
        near = jnp.concatenate([low[16 * g : 16 * g + 16], high[16 * g : 16 * g + 16]], axis=0)
        idents.append(near[WINDOW : WINDOW + 1])
        blocks.append(count_pairs(near, (WINDOW, 31)))
    ident = jnp.concatenate(idents, axis=1)
    pairs = jnp.concatenate(blocks, axis=1)
    column_hot = hot(ident == iota((OWNED, ident.shape[1]), 0, jnp.float32)).astype(jnp.bfloat16)
    counts[:, pl.ds(0, OWNED)] = nt_dot(pairs, column_hot) + first_crossed[:, :OWNED]

    low_sum = jnp.zeros((MESSAGE, LANES), jnp.int32)
    high_sum = jnp.zeros((MESSAGE, LANES), jnp.int32)
    for s in range(SLABS):
        word = got_ref[s]
        low_sum += word & 65535
        high_sum += (word >> 16) & 65535
    mine = jnp.where(iota((MESSAGE, LANES), 1) < HALF, pltpu.roll(low_sum, HALF, 1), high_sum)
    item_row, item_lane = iota((ROWS, LANES), 0), iota((ROWS, LANES), 1)
    placed = jnp.zeros((ROWS, LANES), jnp.int32)
    for q in range(ROWS_DEV):
        placed = jnp.where(item_row == row_owner * ROWS_DEV + q, mine[q : q + 1], placed)
    placed = jnp.where(item_row == item_lane, 2 * placed, placed).astype(jnp.float32)
    counts[pl.ds(0, ROWS), pl.ds(OWNED, ROWS)] = placed.T + first_crossed[:ROWS, OWNED:]

    def chunk(step, carry):
        counts[...] += crossed(step)
        return carry

    lax.fori_loop(1, (crossing + LANES - 1) // LANES, chunk, 0)

    margin_low = jnp.sum(got_ref[:, 4, :], axis=0, keepdims=True)
    margin_high = jnp.sum(got_ref[:, 5, :], axis=0, keepdims=True)
    margins = jnp.where(item_lane[:1] < HALF, pltpu.roll(margin_low, HALF, 1), margin_high)
    held = jnp.where(item_row == item_lane, margins.astype(jnp.float32), 0.0)
    edge_codes = jnp.minimum(items, 255).astype(jnp.float32).astype(jnp.bfloat16)
    edge_rows = item_row.astype(jnp.float32).astype(jnp.bfloat16)
    edge_cross = cross.astype(jnp.bfloat16)
    for first in range(0, SLABS, 16):
        part = jnp.zeros((ROWS, LANES), jnp.bfloat16)
        for s in range(first, first + 16):
            same = edge_codes[s : s + 1] == edge_rows
            part += jnp.where(same, edge_cross[s : s + 1], jnp.zeros((), jnp.bfloat16))
        held += part.astype(jnp.float32)
    row_margin = jnp.sum(held, axis=1, keepdims=True)
    totals = jnp.where(lane == SPOT, raw_items, 0).astype(jnp.float32) + cross
    pair_total = jnp.sum(jnp.sum(totals, axis=0, keepdims=True), axis=1, keepdims=True)
    col_margin = jnp.concatenate(
        [counts[pl.ds(ROWS, 1), pl.ds(0, OWNED)], jnp.sum(held.T, axis=0, keepdims=True)], axis=1
    )
    positive = ppmi(counts[pl.ds(0, ROWS), :], row_margin, col_margin, pair_total)
    copy.wait()
    held_words = jnp.concatenate([words[...], row_bits_ref[...]], axis=1)
    for b in range(WORD_BITS):
        sign = jnp.where((held_words >> b) & 1 == 1, 1.0, -1.0)
        for j in range(COLS // LANES):
            wide_signs[j, pl.ds(b, WORDS, stride=WORD_BITS), :] = sign[:, j * LANES : (j + 1) * LANES]
    parts = two_parts(positive)
    signs = [wide_signs[j, pl.ds(0, SKETCH), :].astype(jnp.bfloat16) for j in range(COLS // LANES)]
    result = nt_dot(parts, jnp.concatenate(signs, axis=1))
    result = result[:ROWS] + result[ROWS:]
    for s in range(SLABS):
        out_ref[s] = result[s * ROWS_DEV : (s + 1) * ROWS_DEV]


def route(where, items, sessions, interpret=False):
    return pl.pallas_call(
        lambda *refs: route_kernel(where, *refs),
        out_shape=jax.ShapeDtypeStruct((SLABS, MESSAGE, LANES), jnp.int32),
        in_specs=[pl.BlockSpec(memory_space=pltpu.HBM)] * 2,
        out_specs=pl.BlockSpec(memory_space=pltpu.VMEM),
        scratch_shapes=[
            pltpu.VMEM((SLAB_ROWS, LANES), jnp.int32),
            pltpu.VMEM((SLAB_ROWS, LANES), jnp.int32),
            pltpu.VMEM((2 * PAD + SLAB_ROWS, LANES), jnp.float32),
            pltpu.VMEM((LANES, 5 * LANES), jnp.bfloat16),
            pltpu.VMEM((SLABS * QUOTA, LANES), jnp.int32),
            pltpu.VMEM((ROWS, SLAB_ROWS * LANES), jnp.bfloat16),
            pltpu.VMEM((ROWS + 16, SLAB_ROWS * LANES), jnp.bfloat16),
            pltpu.SemaphoreType.DMA((2,)),
        ],
        compiler_params=pltpu.CompilerParams(vmem_limit_bytes=VMEM_BYTES),
        interpret=interpret,
        name="route_events",
    )(items, sessions)


def sketch_part(where, got, bits, interpret=False):
    return pl.pallas_call(
        lambda *refs: sketch_kernel(where, *refs),
        out_shape=(
            jax.ShapeDtypeStruct((SLABS, ROWS_DEV, SKETCH), jnp.float32),
            jax.ShapeDtypeStruct((1, 1), jnp.int32),
        ),
        grid=(1,),
        in_specs=[
            pl.BlockSpec((SLABS, MESSAGE, LANES), lambda i: (0, 0, 0)),
            pl.BlockSpec((WORDS, LANES), lambda i: (0, 0)),
            pl.BlockSpec(memory_space=pltpu.HBM),
        ],
        out_specs=(
            pl.BlockSpec((SLABS, ROWS_DEV, SKETCH), lambda i: (0, 0, 0)),
            pl.BlockSpec(memory_space=pltpu.SMEM),
        ),
        scratch_shapes=[
            pltpu.VMEM((ROWS + 16, COLS), jnp.float32),
            pltpu.VMEM((LANES, 4 * LANES), jnp.bfloat16),
            pltpu.VMEM((WORDS, OWNED), jnp.int32),
            pltpu.VMEM((COLS // LANES, 16 * WORD_BITS, LANES), jnp.float32),
            pltpu.SemaphoreType.DMA,
        ],
        compiler_params=pltpu.CompilerParams(vmem_limit_bytes=VMEM_BYTES),
        interpret=interpret,
        name="sketch_part",
    )(got, bits, bits)


def shares(part):
    rows = jnp.sum(lax.all_to_all(part, "stream", 0, 0, tiled=True), axis=0)
    spread = jnp.broadcast_to(rows[None], (BANDS,) + rows.shape)
    return lax.all_to_all(spread, "item", 0, 0, tiled=True)


def local(event_items, event_sessions, sketch_bits):
    def where():
        return lax.axis_index("stream"), lax.axis_index("item")

    items = event_items.reshape(SLAB_ROWS, LANES)
    sessions = event_sessions.reshape(SLAB_ROWS, LANES)

    def from_every_event(_):
        message = all_events(where, items, sessions, sketch_bits)
        own = lax.all_to_all(message, "stream", 0, 0, tiled=True)
        other = lax.ppermute(own, "item", [(i, i ^ 1) for i in range(BANDS)])
        return shares(from_all(where, own, other, sketch_bits))

    routed = lax.all_to_all(route(where, items, sessions), "stream", 0, 0, tiled=True)
    part, spoilt = sketch_part(where, routed, sketch_bits)
    gathered = lax.cond(spoilt[0, 0] > 0, from_every_event, lambda kept: kept, shares(part))
    return jnp.sum(gathered, axis=0) / math.sqrt(EVENT_ROWS * LANES)


def solution(mesh):
    placed = (P("stream"), P("stream"), P(None, "item"))
    return jax.shard_map(
        local, mesh=mesh, in_specs=placed, out_specs=P("stream", None), check_vma=False
    )
```

```python
import math

import jax
import jax.numpy as jnp
from jax import lax
from jax.experimental import pallas as pl
from jax.experimental.pallas import tpu as pltpu
from jax.sharding import PartitionSpec as P

SKETCH = 256
WINDOW = 15
ROWS = 128
ROWS_DEV = 4
LANES = 128
SLABS = 32
BANDS = 8
SLAB_ROWS = 32
HALF_ROWS = SLAB_ROWS // 2
PAYLOAD = 32
EVENT_ROWS = SLABS * SLAB_ROWS
OWNED = 1024
COLS = OWNED + ROWS
WORD_BITS = 18
WORDS = 15
SLOTS = 384
PAD = 8
MARGIN_ROW, TOTAL_ROW, BITS_ROW = 24, 25, 26
QUOTA = 32
MESSAGE = 8
HALF = LANES // 2
NONE = 255.0
SPOT = HALF + 16
VMEM_BYTES = 48 << 20
COUNT = jnp.bfloat16


def iota(shape, axis, dtype=jnp.int32):
    out = lax.broadcasted_iota(jnp.int32, shape, axis)
    return out if dtype == jnp.int32 else out.astype(dtype)


def nt_dot(left, right):
    return lax.dot_general(
        left, right, (((1,), (1,)), ((), ())), preferred_element_type=jnp.float32
    )


def hot(mask):
    return jnp.where(mask, 1.0, 0.0)


def ppmi(count, row_margin, col_margin, pair_total):
    log_ratio = (
        jnp.log(jnp.maximum(count, 1.0))
        + jnp.log(pair_total)
        - jnp.log(jnp.maximum(row_margin, 1.0))
        - jnp.log(jnp.maximum(col_margin, 1.0))
    )
    return jnp.where(count > 0, jnp.maximum(log_ratio, 0.0), 0.0)


def split(values):
    high = values.astype(jnp.bfloat16)
    rest = values - high.astype(jnp.float32)
    mid = rest.astype(jnp.bfloat16)
    low = (rest - mid.astype(jnp.float32)).astype(jnp.bfloat16)
    return jnp.concatenate([high, mid, low], axis=0)


def two_parts(values):
    high = values.astype(jnp.bfloat16)
    low = (values - high.astype(jnp.float32)).astype(jnp.bfloat16)
    return jnp.concatenate([high, low], axis=0)


def joined(parts):
    third = parts.shape[0] // 3
    return parts[:third] + (parts[third : 2 * third] + parts[2 * third :])


def fill_signs(held_words, signs):
    held_words = jnp.concatenate([held_words, jnp.zeros((1, COLS), jnp.int32)], axis=0)
    for b in range(WORD_BITS):
        signs[pl.ds(b * 16, 16), :] = jnp.where((held_words >> b) & 1 == 1, 1.0, -1.0).astype(jnp.bfloat16)


def project(positive, signs):
    by_bit = joined(nt_dot(split(positive), signs[...]))
    have = iota((16 * WORD_BITS, SKETCH), 0)
    want = iota((16 * WORD_BITS, SKETCH), 1)
    order = hot((have & 15) * WORD_BITS + (have >> 4) == want).astype(jnp.bfloat16)
    return joined(jnp.dot(split(by_bit), order, preferred_element_type=jnp.float32))


def all_events_kernel(where, items_ref, sessions_ref, bits_ref, out_ref):
    _, band = where()
    half = lax.rem(band, 2)
    items, sessions = items_ref[...], sessions_ref[...]
    shape = items.shape
    row, lane = iota(shape, 0), iota(shape, 1)
    above = jnp.where(row == 0, -1, pltpu.roll(sessions, 1, 0))
    below = jnp.where(row == SLAB_ROWS - 1, -1, pltpu.roll(sessions, SLAB_ROWS - 1, 0))
    weights = jnp.zeros(shape, jnp.float32)
    for d in range(1, WINDOW + 1):
        earlier = pltpu.roll(jnp.where(lane >= LANES - d, above, sessions), d, 1)
        later = pltpu.roll(jnp.where(lane < d, below, sessions), LANES - d, 1)
        weights += hot(earlier == sessions) + hot(later == sessions)
    held = jnp.zeros((ROWS, LANES), jnp.float32)
    item_row = iota((ROWS, LANES), 0)
    for r in range(SLAB_ROWS):
        held += jnp.where(items[r : r + 1] == item_row, weights[r : r + 1], 0.0)
    margin = jnp.sum(held.T, axis=0, keepdims=True).astype(jnp.int32)
    total = jnp.sum(weights, axis=0, keepdims=True).astype(jnp.int32)
    own_items = jnp.where(half == 0, items[:HALF_ROWS], items[HALF_ROWS:])
    own_sessions = jnp.where(half == 0, sessions[:HALF_ROWS], sessions[HALF_ROWS:])
    pairs = own_sessions[:8] + own_sessions[8:] * 65536
    slab, _ = where()
    word = bits_ref[...]
    one = jnp.sum(
        jnp.where(iota(word.shape, 0) == jnp.minimum(slab, WORDS - 1), word, 0),
        axis=0,
        keepdims=True,
    )
    extra = jnp.concatenate([margin, total, one, jnp.zeros((5, LANES), jnp.int32)], axis=0)
    message = jnp.concatenate([own_items, pairs, extra], axis=0)
    for s in range(SLABS):
        out_ref[s] = message


def from_all_kernel(
    where, own_ref, other_ref, bits_hbm, out_ref,
    sess, codes, mask, table, counts, words, signs, sem,
):
    slab, band = where()
    half = lax.rem(band, 2)
    copy = pltpu.make_async_copy(
        bits_hbm.at[:, pl.ds(pl.multiple_of(slab * OWNED, OWNED), OWNED)],
        words,
        sem,
    )
    copy.start()
    lane_s = iota((SLAB_ROWS, LANES), 1)
    block_id = band * SLABS + slab
    pair_id = jnp.where(band < 2, 2 * slab + half, -1)

    edge = jnp.full((PAD, LANES), -(ROWS + 1.0), jnp.float32)
    codes[pl.ds(0, PAD), :] = edge
    codes[pl.ds(PAD + EVENT_ROWS, PAD), :] = edge
    sess[pl.ds(0, PAD), :] = jnp.full((PAD, LANES), -1, jnp.int32)

    def halves(s):
        mine, its = own_ref[s], other_ref[s]
        return jnp.where(half == 0, mine, its), jnp.where(half == 0, its, mine)

    def unpack(s, carry):
        first, second = halves(s)
        items = jnp.concatenate([first[:16], second[:16]], axis=0)
        a, b = first[16:24], second[16:24]
        sessions = jnp.concatenate([a & 65535, a >> 16, b & 65535, b >> 16], axis=0)
        base = pl.multiple_of(s * SLAB_ROWS, SLAB_ROWS)
        sess[pl.ds(PAD + base, SLAB_ROWS), :] = sessions
        above = sess[pl.ds(PAD - 1 + base, SLAB_ROWS), :]
        before = pltpu.roll(jnp.where(lane_s == LANES - 1, above, sessions), 1, 1)
        value = jnp.minimum(items, ROWS) + 1
        codes[pl.ds(PAD + base, SLAB_ROWS), :] = jnp.where(
            before != sessions, -value, value
        ).astype(jnp.float32)
        is_row = items < ROWS
        owned = jnp.where(is_row, items >> 1, items >> 10) == jnp.where(is_row, pair_id, block_id)
        ident = jnp.where(is_row, OWNED + items, items & (OWNED - 1))
        rows = pl.ds(base, SLAB_ROWS)
        mask[rows, :] = hot(owned).astype(jnp.bfloat16)
        table[rows, pl.ds(LANES, LANES)] = (ident & 255).astype(jnp.float32).astype(jnp.bfloat16)
        table[rows, pl.ds(2 * LANES, LANES)] = (ident >> 8).astype(jnp.float32).astype(jnp.bfloat16)
        return carry

    lax.fori_loop(0, SLABS, unpack, 0, unroll=4)
    for r in range(0, EVENT_ROWS, 128):
        rows = pl.ds(r, 128)
        table[rows, pl.ds(3 * LANES, LANES)] = codes[pl.ds(PAD - 1 + r, 128), :].astype(jnp.bfloat16)
        table[rows, pl.ds(4 * LANES, LANES)] = codes[pl.ds(PAD + r, 128), :].astype(jnp.bfloat16)
        table[rows, pl.ds(5 * LANES, LANES)] = codes[pl.ds(PAD + 1 + r, 128), :].astype(jnp.bfloat16)

    upto = hot(iota((LANES, LANES), 0) <= iota((LANES, LANES), 1)).astype(jnp.bfloat16)
    owned = mask[...]
    rank = jnp.dot(owned, upto, preferred_element_type=jnp.float32)
    table[:, pl.ds(0, LANES)] = (rank * owned.astype(jnp.float32)).astype(jnp.bfloat16)
    per_row = nt_dot(jnp.ones((8, LANES), jnp.bfloat16), owned)
    groups = EVENT_ROWS // LANES
    grouped = jnp.concatenate(
        [per_row[:1, g * LANES : (g + 1) * LANES] for g in range(groups)], axis=0
    )
    inside = jnp.dot(grouped.astype(jnp.bfloat16), upto, preferred_element_type=jnp.float32)
    ends, starts, base = [], [], jnp.zeros((1, 1), jnp.float32)
    for g in range(groups):
        ends.append(inside[g : g + 1] + base)
        starts.append(ends[g] - grouped[g : g + 1])
        base = base + inside[g : g + 1, LANES - 1 :]
    owned_events = jnp.max(base).astype(jnp.int32)

    counts[...] = jnp.zeros(counts.shape, jnp.float32)
    lane_f = iota((SLOTS, LANES), 1, jnp.float32)
    row32, col32 = iota((32, 32), 0), iota((32, 32), 1)
    ahead = (row32 > WINDOW) & (col32 > WINDOW) & (col32 <= row32)
    behind = (row32 < WINDOW) & (col32 > row32) & (col32 <= WINDOW)
    between = hot(ahead | behind).astype(jnp.bfloat16)
    place = iota((32, SLOTS), 0)
    in_window = (place != WINDOW) & (place <= 2 * WINDOW)
    row_ids = iota((ROWS, SLOTS), 0, jnp.float32)
    col_ids = iota((SLOTS, COLS), 1, jnp.float32)

    def chunk(step, carry):
        slot = (step * SLOTS + iota((SLOTS, LANES), 0)).astype(jnp.float32)
        picks, first = [], jnp.zeros((SLOTS, LANES), jnp.float32)
        for g in range(groups):
            here = (slot >= starts[g]) & (slot < ends[g])
            first += jnp.where(here, starts[g], 0.0)
            picks.append(hot(here).astype(jnp.bfloat16))
        pick = jnp.concatenate(picks, axis=1)
        got = jnp.dot(pick, table[...], preferred_element_type=jnp.float32)
        ordinal = slot[:, :1] + 1.0 - jnp.sum(first, axis=1, keepdims=True)
        chosen = got[:, :LANES] == ordinal
        ident = got[:, LANES : 2 * LANES] + 256.0 * got[:, 2 * LANES : 3 * LANES]
        column = jnp.sum(jnp.where(chosen, ident + 1.0, 0.0), axis=1, keepdims=True) - 1.0
        at_lane = jnp.sum(jnp.where(chosen, lane_f, 0.0), axis=1, keepdims=True)
        source = at_lane.astype(jnp.int32) + (iota((SLOTS, LANES), 1) - WINDOW)
        index = source & (LANES - 1)
        parts = [
            jnp.take_along_axis(got[:, k * LANES : (k + 1) * LANES], index, axis=1, mode="promise_in_bounds")
            for k in (3, 4, 5)
        ]
        window = jnp.where(source < 0, parts[0], jnp.where(source < LANES, parts[1], parts[2]))
        window = window.T[:32]
        breaks = hot(window < 0.0).astype(jnp.bfloat16)
        crossed = jnp.dot(between, breaks, preferred_element_type=jnp.float32)
        linked = (crossed == 0.0) & in_window
        near = jnp.where(linked, jnp.abs(window) - 1.0, 255.0)
        weight = jnp.sum(hot(linked), axis=0, keepdims=True)
        pairs = jnp.zeros((ROWS, SLOTS), jnp.float32)
        for d in range(2 * WINDOW + 1):
            if d != WINDOW:
                pairs += hot(near[d : d + 1] == row_ids)
        pairs = jnp.concatenate([pairs, jnp.broadcast_to(weight, (16, SLOTS))], axis=0)
        column_hot = hot(column == col_ids).astype(jnp.bfloat16)
        counts[...] += jnp.dot(
            pairs.astype(jnp.bfloat16), column_hot, preferred_element_type=jnp.float32
        )
        return carry

    lax.fori_loop(0, (owned_events + SLOTS - 1) // SLOTS, chunk, 0)

    def both(row_first, row_second):
        mine_f, its_f = own_ref[:, row_first, :], other_ref[:, row_first, :]
        mine_s, its_s = own_ref[:, row_second, :], other_ref[:, row_second, :]
        return jnp.where(half == 0, mine_f, its_f), jnp.where(half == 0, its_s, mine_s)

    start_items, end_items = both(0, 15)
    start_sess, end_sess = both(16, 23)
    start_sess, end_sess = start_sess & 65535, end_sess >> 16
    slab_row = iota((SLABS, LANES), 0)
    end_items = pltpu.roll(end_items, 1, 0)
    end_sess = jnp.where(slab_row == 0, -1, pltpu.roll(end_sess, 1, 0))
    cross = jnp.zeros((SLABS, LANES), jnp.float32)
    lane = iota((SLABS, LANES), 1)
    for d in range(1, WINDOW + 1):
        before = pltpu.roll(end_sess, d, 1)
        after = pltpu.roll(start_sess, LANES - d, 1)
        cross += hot((lane < d) & (before == start_sess))
        cross += hot((lane >= LANES - d) & (after == end_sess))
    cross_items = jnp.where(lane < LANES // 2, start_items, end_items)
    margins = jnp.sum(own_ref[:, MARGIN_ROW, :], axis=0, keepdims=True).astype(jnp.float32)
    item_row = iota((ROWS, LANES), 0)
    held = jnp.where(item_row == iota((ROWS, LANES), 1), margins, 0.0)
    for s in range(SLABS):
        held += jnp.where(cross_items[s : s + 1] == item_row, cross[s : s + 1], 0.0)
    row_margin = jnp.sum(held, axis=1, keepdims=True)
    totals = jnp.sum(own_ref[:, TOTAL_ROW, :], axis=0, keepdims=True).astype(jnp.float32)
    totals = totals + jnp.sum(cross, axis=0, keepdims=True)
    pair_total = jnp.sum(totals, axis=1, keepdims=True)

    positive = ppmi(
        counts[pl.ds(0, ROWS), :], row_margin, counts[pl.ds(ROWS, 1), :], pair_total
    )
    copy.wait()
    row_words = jnp.where(half == 0, own_ref[:WORDS, BITS_ROW, :], other_ref[:WORDS, BITS_ROW, :])
    fill_signs(jnp.concatenate([words[...], row_words], axis=1), signs)
    result = project(positive, signs)
    for s in range(SLABS):
        out_ref[s] = result[s * ROWS_DEV : (s + 1) * ROWS_DEV]


def all_events(where, items, sessions, bits, interpret=False):
    return pl.pallas_call(
        lambda *refs: all_events_kernel(where, *refs),
        out_shape=jax.ShapeDtypeStruct((SLABS, PAYLOAD, LANES), jnp.int32),
        grid=(1,),
        in_specs=[
            pl.BlockSpec((SLAB_ROWS, LANES), lambda i: (0, 0)),
            pl.BlockSpec((SLAB_ROWS, LANES), lambda i: (0, 0)),
            pl.BlockSpec((WORDS, LANES), lambda i: (0, 0)),
        ],
        out_specs=pl.BlockSpec((SLABS, PAYLOAD, LANES), lambda i: (0, 0, 0)),
        compiler_params=pltpu.CompilerParams(vmem_limit_bytes=VMEM_BYTES),
        interpret=interpret,
        name="all_events",
    )(items, sessions, bits)


def from_all(where, own, other, bits, interpret=False):
    return pl.pallas_call(
        lambda *refs: from_all_kernel(where, *refs),
        out_shape=jax.ShapeDtypeStruct((SLABS, ROWS_DEV, SKETCH), jnp.float32),
        in_specs=[
            pl.BlockSpec(memory_space=pltpu.VMEM),
            pl.BlockSpec(memory_space=pltpu.VMEM),
            pl.BlockSpec(memory_space=pl.ANY),
        ],
        out_specs=pl.BlockSpec(memory_space=pltpu.VMEM),
        scratch_shapes=[
            pltpu.VMEM((PAD + EVENT_ROWS, LANES), jnp.int32),
            pltpu.VMEM((2 * PAD + EVENT_ROWS, LANES), jnp.float32),
            pltpu.VMEM((EVENT_ROWS, LANES), jnp.bfloat16),
            pltpu.VMEM((EVENT_ROWS, 6 * LANES), jnp.bfloat16),
            pltpu.VMEM((ROWS + 16, COLS), jnp.float32),
            pltpu.VMEM((WORDS, OWNED), jnp.int32),
            pltpu.VMEM((16 * WORD_BITS, COLS), jnp.bfloat16),
            pltpu.SemaphoreType.DMA,
        ],
        compiler_params=pltpu.CompilerParams(vmem_limit_bytes=VMEM_BYTES),
        interpret=interpret,
        name="from_all",
    )(own, other, bits)


def route_kernel(where, items_hbm, sessions_hbm, out_ref, items_v, sessions_v, codes, table, near_rows, one_hots, pair_rows, sems):
    slab, band = where()
    get_items = pltpu.make_async_copy(items_hbm, items_v, sems.at[0])
    get_sessions = pltpu.make_async_copy(sessions_hbm, sessions_v, sems.at[1])
    get_items.start()
    get_sessions.start()
    get_items.wait()
    get_sessions.wait()
    items, sessions = items_v[...], sessions_v[...]
    shape = items.shape
    row, lane = iota(shape, 0), iota(shape, 1)
    above = jnp.where(row == 0, -1, pltpu.roll(sessions, 1, 0))
    below = jnp.where(row == SLAB_ROWS - 1, -1, pltpu.roll(sessions, SLAB_ROWS - 1, 0))
    earlier_links = jnp.zeros(shape, jnp.float32)
    later_links = jnp.zeros(shape, jnp.float32)
    for d in range(1, WINDOW + 1):
        earlier = pltpu.roll(jnp.where(lane >= LANES - d, above, sessions), d, 1)
        later = pltpu.roll(jnp.where(lane < d, below, sessions), LANES - d, 1)
        earlier_links += hot(earlier == sessions)
        later_links += hot(later == sessions)
    weights = earlier_links + later_links

    one, none = jnp.ones((), jnp.bfloat16), jnp.zeros((), jnp.bfloat16)
    item_codes = jnp.minimum(items, 255).astype(jnp.float32).astype(jnp.bfloat16)
    row_ids = iota((ROWS, LANES), 0, jnp.float32).astype(jnp.bfloat16)
    for r in range(SLAB_ROWS):
        same = item_codes[r : r + 1] == row_ids
        one_hots[:, pl.ds(r * LANES, LANES)] = jnp.where(same, one, none)
        pair_rows[pl.ds(ROWS, 16), pl.ds(r * LANES, LANES)] = jnp.broadcast_to(
            weights[r : r + 1], (16, LANES)
        ).astype(jnp.bfloat16)
    total = jnp.sum(weights, axis=0, keepdims=True)
    first_link = (iota(shape, 1, jnp.float32) - earlier_links).astype(jnp.bfloat16)
    place = iota((LANES, LANES), 0, jnp.float32).astype(jnp.bfloat16)
    sooner = iota((LANES, LANES), 0) < iota((LANES, LANES), 1)
    sooner = jnp.where(sooner, place, jnp.full((), -64.0, jnp.bfloat16))
    last = (iota((16, LANES), 0, jnp.float32) - 16.0).astype(jnp.bfloat16)
    ordered = jnp.zeros((ROWS + 16, ROWS), jnp.float32)
    no_links = jnp.zeros((LANES - 16, LANES), jnp.bfloat16)
    for r in range(SLAB_ROWS):
        begin = first_link[r : r + 1]
        links = jnp.where(sooner >= begin, one, none)
        if r == 0:
            pairs = jnp.dot(one_hots[:, pl.ds(0, LANES)], links, preferred_element_type=jnp.float32)
        else:
            links = jnp.concatenate([no_links, jnp.where(last >= begin, one, none), links], axis=0)
            pairs = jnp.dot(
                one_hots[:, pl.ds((r - 1) * LANES, 2 * LANES)], links, preferred_element_type=jnp.float32
            )
        pair_rows[pl.ds(0, ROWS), pl.ds(r * LANES, LANES)] = pairs.astype(jnp.bfloat16)
        if r % 8 == 7:
            ready = pl.ds((r - 7) * LANES, 8 * LANES)
            ordered += nt_dot(pair_rows[:, ready], one_hots[:, ready])
    margin = ordered[ROWS : ROWS + 1]
    ordered = ordered[:ROWS]
    row_pairs = ordered + ordered.T
    item_row = iota((ROWS, LANES), 0)

    before = pltpu.roll(jnp.where(lane == LANES - 1, above, sessions), 1, 1)
    value = jnp.minimum(items, ROWS) + 1
    edge = jnp.full((PAD, LANES), -(ROWS + 1.0), jnp.float32)
    codes[pl.ds(0, PAD), :] = edge
    codes[pl.ds(PAD + SLAB_ROWS, PAD), :] = edge
    codes[pl.ds(PAD, SLAB_ROWS), :] = jnp.where(before != sessions, -value, value).astype(jnp.float32)
    inside = items - band * (SLABS * OWNED)
    wide = (items >= ROWS) & (inside >= 0) & (inside < SLABS * OWNED)
    inside = jnp.where(wide, inside, 0)
    owner = jnp.where(wide, inside >> 10, -1)
    owner_row = iota((SLABS, LANES), 0)
    marks = [hot(owner[r : r + 1] == owner_row) for r in range(SLAB_ROWS)]
    upto = hot(iota((LANES, LANES), 0) <= iota((LANES, LANES), 1)).astype(jnp.bfloat16)
    ranks = jnp.dot(
        jnp.concatenate(marks, axis=0).astype(jnp.bfloat16), upto, preferred_element_type=jnp.float32
    )
    ranks = [ranks[r * SLABS : (r + 1) * SLABS] for r in range(SLAB_ROWS)]
    per_row = jnp.zeros((SLABS, LANES), jnp.float32)
    for r in range(SLAB_ROWS):
        per_row = jnp.where(lane == r, ranks[r][:, LANES - 1 :], per_row)
    ends = jnp.dot(per_row.astype(jnp.bfloat16), upto, preferred_element_type=jnp.float32)
    starts = ends - per_row
    block = jnp.where(items >= ROWS, items >> 10, -1)
    sixteen = iota((16, LANES), 0)
    upper = [hot((block[r : r + 1] >> 4) == sixteen) for r in range(SLAB_ROWS)]
    lower = [hot((block[r : r + 1] & 15) == sixteen) for r in range(SLAB_ROWS)]
    loads = nt_dot(
        jnp.concatenate(upper, axis=1).astype(jnp.bfloat16),
        jnp.concatenate(lower, axis=1).astype(jnp.bfloat16),
    )
    most = jnp.max(jnp.max(loads, axis=0, keepdims=True), axis=1, keepdims=True)
    orders = [
        jnp.sum(marks[r] * (ranks[r] + starts[:, r : r + 1]), axis=0, keepdims=True)
        for r in range(SLAB_ROWS)
    ]
    table[pl.ds(SLAB_ROWS, LANES - SLAB_ROWS), :] = jnp.zeros((LANES - SLAB_ROWS, 5 * LANES), jnp.bfloat16)
    row_codes = codes[pl.ds(PAD, SLAB_ROWS), :]
    left = jnp.where(lane >= LANES - 32, codes[pl.ds(PAD - 1, SLAB_ROWS), :], row_codes)
    right = jnp.where(lane < 32, codes[pl.ds(PAD + 1, SLAB_ROWS), :], row_codes)
    fields = [
        jnp.minimum(jnp.concatenate(orders, axis=0), 255.0),
        (inside & 255).astype(jnp.float32),
        (inside >> 8).astype(jnp.float32),
        pltpu.roll(left, 32, 1),
        pltpu.roll(right, LANES - 32, 1),
    ]
    for k, field in enumerate(fields):
        table[pl.ds(0, SLAB_ROWS), pl.ds(k * LANES, LANES)] = field.astype(jnp.bfloat16)
    slot = iota((QUOTA, LANES), 0, jnp.float32)
    picks = [
        hot((slot >= starts[s : s + 1]) & (slot < ends[s : s + 1])).astype(jnp.bfloat16)
        for s in range(SLABS)
    ]
    got = jnp.dot(jnp.concatenate(picks, axis=0), table[...], preferred_element_type=jnp.float32)
    big = (SLABS * QUOTA, LANES)
    number, lanes = iota(big, 0), iota(big, 1)
    target = (number >> 5).astype(jnp.float32) * 4.0
    high = got[:, 2 * LANES : 3 * LANES] - target
    ordinal = ((number & (QUOTA - 1)) + 1).astype(jnp.float32)
    chosen = (got[:, :LANES] == ordinal) & (high >= 0.0) & (high < 4.0)
    ident = got[:, LANES : 2 * LANES] + 256.0 * high + 1.0
    found = jnp.sum(
        jnp.where(chosen, ident * LANES + lanes.astype(jnp.float32), 0.0), axis=1, keepdims=True
    ).astype(jnp.int32)
    column = (((found >> 7) - 1) & 4095).astype(jnp.float32)
    at_lane = found & (LANES - 1)
    index = ((at_lane & (HALF - 1)) + (32 - WINDOW) + lanes) & (LANES - 1)
    reach = jnp.where(at_lane < HALF, got[:, 3 * LANES : 4 * LANES], got[:, 4 * LANES :])
    window = jnp.take_along_axis(reach, index, axis=1, mode="promise_in_bounds")
    from_lane, to_lane = iota((LANES, LANES), 0), iota((LANES, LANES), 1)
    ahead = (to_lane > WINDOW) & (from_lane > WINDOW) & (from_lane <= to_lane)
    behind = (to_lane < WINDOW) & (from_lane > to_lane) & (from_lane <= WINDOW)
    between = hot(ahead | behind).astype(jnp.bfloat16)
    crossed = jnp.dot(
        hot(window < 0.0).astype(jnp.bfloat16), between, preferred_element_type=jnp.float32
    )
    linked = (crossed == 0.0) & (lanes <= 2 * WINDOW)
    near = jnp.where(linked, jnp.abs(window) - 1.0, NONE)
    near = jnp.where(lanes == WINDOW, column, near)
    near_rows[...] = (near + 4096.0 * pltpu.roll(near, LANES - 16, 1)).astype(jnp.int32)

    whole = jnp.where(item_row == iota((ROWS, LANES), 1), ordered, row_pairs).astype(jnp.int32)
    packed = pltpu.roll(whole, HALF, 1) + jnp.where(iota((ROWS, LANES), 1) >= HALF, whole * 65536, 0)
    ends_lane = iota((1, LANES), 1)
    spare = jnp.where(most > QUOTA, 1, 0)
    total = jnp.sum(total, axis=1, keepdims=True).astype(jnp.int32)
    margin = margin.astype(jnp.int32)

    def edges(values, single):
        both = jnp.where(ends_lane < LANES - 32, pltpu.roll(values[:1], HALF, 1), values[SLAB_ROWS - 1 :])
        return jnp.where(ends_lane == SPOT, single, both)

    common = jnp.concatenate(
        [pltpu.roll(margin, HALF, 1), margin, edges(items, total), edges(sessions, spare)], axis=0
    )
    sixteenth = iota((8, LANES), 1) >> 4
    for s in range(SLABS):
        rows = jnp.concatenate([packed[s * ROWS_DEV : (s + 1) * ROWS_DEV], common], axis=0)
        for g in range(QUOTA // 8):
            part = near_rows[pl.ds(s * QUOTA + 8 * g, 8), :]
            rows = jnp.where(sixteenth == g, pltpu.roll(part, 16 * g, 1) if g else part, rows)
        out_ref[s] = rows


def count_pairs(near, skip):
    slots = near.shape[1]
    place = iota(near.shape, 0)
    real = near < NONE
    for d in skip:
        real = real & (place != d)
    weight = jnp.sum(hot(real), axis=0, keepdims=True)
    row_ids = iota((ROWS, slots), 0, jnp.float32).astype(COUNT)
    one, none = jnp.ones((), COUNT), jnp.zeros((), COUNT)
    pairs = jnp.zeros((ROWS, slots), COUNT)
    near = near.astype(COUNT)
    for d in range(near.shape[0]):
        if d not in skip:
            pairs += jnp.where(near[d : d + 1] == row_ids, one, none)
    weight = jnp.broadcast_to(weight, (16, slots)).astype(jnp.bfloat16)
    return jnp.concatenate([pairs.astype(jnp.bfloat16), weight], axis=0)


def sketch_kernel(
    where, got_ref, row_bits_ref, bits_hbm, out_ref, spoilt_ref, counts, table, words, wide_signs, sem
):
    slab, band = where()
    copy = pltpu.make_async_copy(
        bits_hbm.at[:, pl.ds(pl.multiple_of(slab * OWNED, OWNED), OWNED)], words, sem
    )
    copy.start()

    slab_row, lane = iota((SLABS, LANES), 0), iota((SLABS, LANES), 1)
    raw_items, raw_sessions = got_ref[:, 6, :], got_ref[:, 7, :]
    edge_items = jnp.where(lane < HALF, pltpu.roll(raw_items, HALF, 1), raw_items)
    edge_sessions = jnp.where(lane < HALF, pltpu.roll(raw_sessions, HALF, 1), raw_sessions)
    spoilt_ref[0, 0] = jnp.max(jnp.where(lane == SPOT, raw_sessions, 0))
    end_items = pltpu.roll(edge_items, 1, 0)
    end_sess = jnp.where(slab_row == 0, -1, pltpu.roll(edge_sessions, 1, 0))
    cross = jnp.zeros((SLABS, LANES), jnp.float32)
    for d in range(1, WINDOW + 1):
        before = pltpu.roll(end_sess, d, 1)
        after = pltpu.roll(edge_sessions, LANES - d, 1)
        cross += hot((lane < d) & (before == edge_sessions))
        cross += hot((lane >= LANES - d) & (after == end_sess))
    items = jnp.where(lane < HALF, edge_items, end_items)
    over = jnp.where(
        lane < HALF,
        hot((edge_sessions == end_sess[:, LANES - 1 :]) & (lane < WINDOW)),
        hot((end_sess == edge_sessions[:, :1]) & (lane >= LANES - WINDOW)),
    )
    partner = jnp.where(over > 0.0, jnp.minimum(items, ROWS).astype(jnp.float32), NONE)
    is_row = items < ROWS
    row_owner = jnp.where(band == 0, slab, -1)
    owned = jnp.where(is_row, items >> 2, items >> 10) == jnp.where(is_row, row_owner, band * SLABS + slab)
    owned = hot(owned & (cross > 0.0))
    local_id = jnp.where(is_row, OWNED + items, items & (OWNED - 1))
    upto = hot(iota((LANES, LANES), 0) <= iota((LANES, LANES), 1)).astype(jnp.bfloat16)
    blank = jnp.zeros((LANES - SLABS, LANES), jnp.float32)
    marks = jnp.concatenate([owned, blank], axis=0).astype(jnp.bfloat16)
    rank = jnp.dot(marks, upto, preferred_element_type=jnp.float32)
    per_row = nt_dot(jnp.ones((8, LANES), jnp.bfloat16), marks)
    ends = jnp.dot(per_row.astype(jnp.bfloat16), upto, preferred_element_type=jnp.float32)
    starts = (ends - per_row)[:1]
    ends = ends[:1]
    crossing = jnp.max(ends).astype(jnp.int32)
    fields = [
        rank[:SLABS] * owned,
        (local_id & 255).astype(jnp.float32),
        (local_id >> 8).astype(jnp.float32),
        partner,
    ]
    for k, field in enumerate(fields):
        table[:, pl.ds(k * LANES, LANES)] = jnp.concatenate([field, blank], axis=0).astype(jnp.bfloat16)
    slot_lane = iota((LANES, LANES), 1)
    col_ids = iota((LANES, COLS), 1, jnp.float32)

    def crossed(step):
        slot = (step * LANES + iota((LANES, LANES), 0)).astype(jnp.float32)
        here = (slot >= starts) & (slot < ends)
        first = jnp.sum(jnp.where(here, starts, 0.0), axis=1, keepdims=True)
        got = jnp.dot(hot(here).astype(jnp.bfloat16), table[...], preferred_element_type=jnp.float32)
        chosen = got[:, :LANES] == slot[:, :1] + 1.0 - first
        ident = got[:, LANES : 2 * LANES] + 256.0 * got[:, 2 * LANES : 3 * LANES]
        column = jnp.sum(jnp.where(chosen, ident + 1.0, 0.0), axis=1, keepdims=True) - 1.0
        at = jnp.sum(jnp.where(chosen, slot_lane, 0), axis=1, keepdims=True)
        reach = LANES - WINDOW
        other_side = jnp.where(at < HALF, hot(slot_lane >= reach + at), hot(slot_lane <= at - reach))
        near = jnp.where(other_side > 0.0, got[:, 3 * LANES :], NONE).T
        near = jnp.concatenate([near[:16], near[LANES - 16 :]], axis=0)
        pairs = count_pairs(near, (15, 16))
        column_hot = hot(column == col_ids).astype(jnp.bfloat16)
        return jnp.dot(pairs, column_hot, preferred_element_type=jnp.float32)

    first_crossed = crossed(0)

    windows = got_ref[...].reshape(SLABS * MESSAGE, LANES).T[:HALF]
    low, high = (windows & 4095).astype(jnp.float32), (windows >> 12).astype(jnp.float32)
    within = first_crossed[:, :OWNED]
    for g in range(QUOTA // 8):
        near = jnp.concatenate([low[16 * g : 16 * g + 16], high[16 * g : 16 * g + 16]], axis=0)
        ident = near[WINDOW : WINDOW + 1]
        column_hot = hot(ident == iota((OWNED, ident.shape[1]), 0, jnp.float32)).astype(jnp.bfloat16)
        within += nt_dot(count_pairs(near, (WINDOW, 31)), column_hot)
    counts[:, pl.ds(0, OWNED)] = within

    low_sum = jnp.zeros((MESSAGE, LANES), jnp.int32)
    high_sum = jnp.zeros((MESSAGE, LANES), jnp.int32)
    for s in range(SLABS):
        word = got_ref[s]
        low_sum += word & 65535
        high_sum += (word >> 16) & 65535
    mine = jnp.where(iota((MESSAGE, LANES), 1) < HALF, pltpu.roll(low_sum, HALF, 1), high_sum)
    item_row, item_lane = iota((ROWS, LANES), 0), iota((ROWS, LANES), 1)
    placed = jnp.zeros((ROWS, LANES), jnp.int32)
    for q in range(ROWS_DEV):
        placed = jnp.where(item_row == row_owner * ROWS_DEV + q, mine[q : q + 1], placed)
    placed = jnp.where(item_row == item_lane, 2 * placed, placed).astype(jnp.float32)
    counts[pl.ds(0, ROWS), pl.ds(OWNED, ROWS)] = placed.T + first_crossed[:ROWS, OWNED:]

    def chunk(step, carry):
        counts[...] += crossed(step)
        return carry

    lax.fori_loop(1, (crossing + LANES - 1) // LANES, chunk, 0)

    margin_low = jnp.sum(got_ref[:, 4, :], axis=0, keepdims=True)
    margin_high = jnp.sum(got_ref[:, 5, :], axis=0, keepdims=True)
    margins = jnp.where(item_lane[:1] < HALF, pltpu.roll(margin_low, HALF, 1), margin_high)
    held = jnp.where(item_row == item_lane, margins.astype(jnp.float32), 0.0)
    edge_codes = jnp.minimum(items, 255).astype(jnp.float32).astype(jnp.bfloat16)
    edge_rows = item_row.astype(jnp.float32).astype(jnp.bfloat16)
    edge_cross = cross.astype(jnp.bfloat16)
    for first in range(0, SLABS, 16):
        part = jnp.zeros((ROWS, LANES), jnp.bfloat16)
        for s in range(first, first + 16):
            same = edge_codes[s : s + 1] == edge_rows
            part += jnp.where(same, edge_cross[s : s + 1], jnp.zeros((), jnp.bfloat16))
        held += part.astype(jnp.float32)
    row_margin = jnp.sum(held, axis=1, keepdims=True)
    totals = jnp.where(lane == SPOT, raw_items, 0).astype(jnp.float32) + cross
    pair_total = jnp.sum(jnp.sum(totals, axis=0, keepdims=True), axis=1, keepdims=True)
    col_margin = jnp.concatenate(
        [counts[pl.ds(ROWS, 1), pl.ds(0, OWNED)], jnp.sum(held.T, axis=0, keepdims=True)], axis=1
    )
    positive = ppmi(counts[pl.ds(0, ROWS), :], row_margin, col_margin, pair_total)
    copy.wait()
    held_words = jnp.concatenate([words[...], row_bits_ref[...]], axis=1)
    for b in range(WORD_BITS):
        sign = jnp.where((held_words >> b) & 1 == 1, 1.0, -1.0)
        for j in range(COLS // LANES):
            wide_signs[j, pl.ds(b, WORDS, stride=WORD_BITS), :] = sign[:, j * LANES : (j + 1) * LANES]
    parts = two_parts(positive)
    signs = [wide_signs[j, pl.ds(0, SKETCH), :].astype(jnp.bfloat16) for j in range(COLS // LANES)]
    result = nt_dot(parts, jnp.concatenate(signs, axis=1))
    result = result[:ROWS] + result[ROWS:]
    for s in range(SLABS):
        out_ref[s] = result[s * ROWS_DEV : (s + 1) * ROWS_DEV]


def route(where, items, sessions, interpret=False):
    return pl.pallas_call(
        lambda *refs: route_kernel(where, *refs),
        out_shape=jax.ShapeDtypeStruct((SLABS, MESSAGE, LANES), jnp.int32),
        in_specs=[pl.BlockSpec(memory_space=pltpu.HBM)] * 2,
        out_specs=pl.BlockSpec(memory_space=pltpu.VMEM),
        scratch_shapes=[
            pltpu.VMEM((SLAB_ROWS, LANES), jnp.int32),
            pltpu.VMEM((SLAB_ROWS, LANES), jnp.int32),
            pltpu.VMEM((2 * PAD + SLAB_ROWS, LANES), jnp.float32),
            pltpu.VMEM((LANES, 5 * LANES), jnp.bfloat16),
            pltpu.VMEM((SLABS * QUOTA, LANES), jnp.int32),
            pltpu.VMEM((ROWS, SLAB_ROWS * LANES), jnp.bfloat16),
            pltpu.VMEM((ROWS + 16, SLAB_ROWS * LANES), jnp.bfloat16),
            pltpu.SemaphoreType.DMA((2,)),
        ],
        compiler_params=pltpu.CompilerParams(vmem_limit_bytes=VMEM_BYTES),
        interpret=interpret,
        name="route_events",
    )(items, sessions)


def sketch_part(where, got, bits, interpret=False):
    return pl.pallas_call(
        lambda *refs: sketch_kernel(where, *refs),
        out_shape=(
            jax.ShapeDtypeStruct((SLABS, ROWS_DEV, SKETCH), jnp.float32),
            jax.ShapeDtypeStruct((1, 1), jnp.int32),
        ),
        grid=(1,),
        in_specs=[
            pl.BlockSpec((SLABS, MESSAGE, LANES), lambda i: (0, 0, 0)),
            pl.BlockSpec((WORDS, LANES), lambda i: (0, 0)),
            pl.BlockSpec(memory_space=pltpu.HBM),
        ],
        out_specs=(
            pl.BlockSpec((SLABS, ROWS_DEV, SKETCH), lambda i: (0, 0, 0)),
            pl.BlockSpec(memory_space=pltpu.SMEM),
        ),
        scratch_shapes=[
            pltpu.VMEM((ROWS + 16, COLS), jnp.float32),
            pltpu.VMEM((LANES, 4 * LANES), jnp.bfloat16),
            pltpu.VMEM((WORDS, OWNED), jnp.int32),
            pltpu.VMEM((COLS // LANES, 16 * WORD_BITS, LANES), jnp.float32),
            pltpu.SemaphoreType.DMA,
        ],
        compiler_params=pltpu.CompilerParams(vmem_limit_bytes=VMEM_BYTES),
        interpret=interpret,
        name="sketch_part",
    )(got, bits, bits)


def shares(part):
    rows = jnp.sum(lax.all_to_all(part, "stream", 0, 0, tiled=True), axis=0)
    spread = jnp.broadcast_to(rows[None], (BANDS,) + rows.shape)
    return lax.all_to_all(spread, "item", 0, 0, tiled=True)


def local(event_items, event_sessions, sketch_bits):
    def where():
        return lax.axis_index("stream"), lax.axis_index("item")

    items = event_items.reshape(SLAB_ROWS, LANES)
    sessions = event_sessions.reshape(SLAB_ROWS, LANES)

    def from_every_event(_):
        message = all_events(where, items, sessions, sketch_bits)
        own = lax.all_to_all(message, "stream", 0, 0, tiled=True)
        other = lax.ppermute(own, "item", [(i, i ^ 1) for i in range(BANDS)])
        return shares(from_all(where, own, other, sketch_bits))

    routed = lax.all_to_all(route(where, items, sessions), "stream", 0, 0, tiled=True)
    part, spoilt = sketch_part(where, routed, sketch_bits)
    gathered = lax.cond(spoilt[0, 0] > 0, from_every_event, lambda kept: kept, shares(part))
    return jnp.sum(gathered, axis=0) / math.sqrt(EVENT_ROWS * LANES)


def solution(mesh):
    placed = (P("stream"), P("stream"), P(None, "item"))
    return jax.shard_map(
        local, mesh=mesh, in_specs=placed, out_specs=P("stream", None), check_vma=False
    )
```

```python
import math

import jax
import jax.numpy as jnp
from jax import lax
from jax.experimental import pallas as pl
from jax.experimental.pallas import tpu as pltpu
from jax.sharding import PartitionSpec as P

SKETCH = 256
WINDOW = 15
ROWS = 128
ROWS_DEV = 4
LANES = 128
SLABS = 32
BANDS = 8
SLAB_ROWS = 32
HALF_ROWS = SLAB_ROWS // 2
PAYLOAD = 32
EVENT_ROWS = SLABS * SLAB_ROWS
OWNED = 1024
COLS = OWNED + ROWS
WORD_BITS = 18
WORDS = 15
SLOTS = 384
PAD = 8
MARGIN_ROW, TOTAL_ROW, BITS_ROW = 24, 25, 26
QUOTA = 32
MESSAGE = 8
HALF = LANES // 2
NONE = 255.0
SPOT = HALF + 16
VMEM_BYTES = 48 << 20
COUNT = jnp.bfloat16


def iota(shape, axis, dtype=jnp.int32):
    out = lax.broadcasted_iota(jnp.int32, shape, axis)
    return out if dtype == jnp.int32 else out.astype(dtype)


def nt_dot(left, right):
    return lax.dot_general(
        left, right, (((1,), (1,)), ((), ())), preferred_element_type=jnp.float32
    )


def hot(mask):
    return jnp.where(mask, 1.0, 0.0)


def ppmi(count, row_margin, col_margin, pair_total):
    log_ratio = (
        jnp.log(jnp.maximum(count, 1.0))
        + jnp.log(pair_total)
        - jnp.log(jnp.maximum(row_margin, 1.0))
        - jnp.log(jnp.maximum(col_margin, 1.0))
    )
    return jnp.where(count > 0, jnp.maximum(log_ratio, 0.0), 0.0)


def split(values):
    high = values.astype(jnp.bfloat16)
    rest = values - high.astype(jnp.float32)
    mid = rest.astype(jnp.bfloat16)
    low = (rest - mid.astype(jnp.float32)).astype(jnp.bfloat16)
    return jnp.concatenate([high, mid, low], axis=0)


def two_parts(values):
    high = values.astype(jnp.bfloat16)
    low = (values - high.astype(jnp.float32)).astype(jnp.bfloat16)
    return jnp.concatenate([high, low], axis=0)


def joined(parts):
    third = parts.shape[0] // 3
    return parts[:third] + (parts[third : 2 * third] + parts[2 * third :])


def fill_signs(held_words, signs):
    held_words = jnp.concatenate([held_words, jnp.zeros((1, COLS), jnp.int32)], axis=0)
    for b in range(WORD_BITS):
        signs[pl.ds(b * 16, 16), :] = jnp.where((held_words >> b) & 1 == 1, 1.0, -1.0).astype(jnp.bfloat16)


def project(positive, signs):
    by_bit = joined(nt_dot(split(positive), signs[...]))
    have = iota((16 * WORD_BITS, SKETCH), 0)
    want = iota((16 * WORD_BITS, SKETCH), 1)
    order = hot((have & 15) * WORD_BITS + (have >> 4) == want).astype(jnp.bfloat16)
    return joined(jnp.dot(split(by_bit), order, preferred_element_type=jnp.float32))


def all_events_kernel(where, items_ref, sessions_ref, bits_ref, out_ref):
    _, band = where()
    half = lax.rem(band, 2)
    items, sessions = items_ref[...], sessions_ref[...]
    shape = items.shape
    row, lane = iota(shape, 0), iota(shape, 1)
    above = jnp.where(row == 0, -1, pltpu.roll(sessions, 1, 0))
    below = jnp.where(row == SLAB_ROWS - 1, -1, pltpu.roll(sessions, SLAB_ROWS - 1, 0))
    weights = jnp.zeros(shape, jnp.float32)
    for d in range(1, WINDOW + 1):
        earlier = pltpu.roll(jnp.where(lane >= LANES - d, above, sessions), d, 1)
        later = pltpu.roll(jnp.where(lane < d, below, sessions), LANES - d, 1)
        weights += hot(earlier == sessions) + hot(later == sessions)
    held = jnp.zeros((ROWS, LANES), jnp.float32)
    item_row = iota((ROWS, LANES), 0)
    for r in range(SLAB_ROWS):
        held += jnp.where(items[r : r + 1] == item_row, weights[r : r + 1], 0.0)
    margin = jnp.sum(held.T, axis=0, keepdims=True).astype(jnp.int32)
    total = jnp.sum(weights, axis=0, keepdims=True).astype(jnp.int32)
    own_items = jnp.where(half == 0, items[:HALF_ROWS], items[HALF_ROWS:])
    own_sessions = jnp.where(half == 0, sessions[:HALF_ROWS], sessions[HALF_ROWS:])
    pairs = own_sessions[:8] + own_sessions[8:] * 65536
    slab, _ = where()
    word = bits_ref[...]
    one = jnp.sum(
        jnp.where(iota(word.shape, 0) == jnp.minimum(slab, WORDS - 1), word, 0),
        axis=0,
        keepdims=True,
    )
    extra = jnp.concatenate([margin, total, one, jnp.zeros((5, LANES), jnp.int32)], axis=0)
    message = jnp.concatenate([own_items, pairs, extra], axis=0)
    for s in range(SLABS):
        out_ref[s] = message


def from_all_kernel(
    where, own_ref, other_ref, bits_hbm, out_ref,
    sess, codes, mask, table, counts, words, signs, sem,
):
    slab, band = where()
    half = lax.rem(band, 2)
    copy = pltpu.make_async_copy(
        bits_hbm.at[:, pl.ds(pl.multiple_of(slab * OWNED, OWNED), OWNED)],
        words,
        sem,
    )
    copy.start()
    lane_s = iota((SLAB_ROWS, LANES), 1)
    block_id = band * SLABS + slab
    pair_id = jnp.where(band < 2, 2 * slab + half, -1)

    edge = jnp.full((PAD, LANES), -(ROWS + 1.0), jnp.float32)
    codes[pl.ds(0, PAD), :] = edge
    codes[pl.ds(PAD + EVENT_ROWS, PAD), :] = edge
    sess[pl.ds(0, PAD), :] = jnp.full((PAD, LANES), -1, jnp.int32)

    def halves(s):
        mine, its = own_ref[s], other_ref[s]
        return jnp.where(half == 0, mine, its), jnp.where(half == 0, its, mine)

    def unpack(s, carry):
        first, second = halves(s)
        items = jnp.concatenate([first[:16], second[:16]], axis=0)
        a, b = first[16:24], second[16:24]
        sessions = jnp.concatenate([a & 65535, a >> 16, b & 65535, b >> 16], axis=0)
        base = pl.multiple_of(s * SLAB_ROWS, SLAB_ROWS)
        sess[pl.ds(PAD + base, SLAB_ROWS), :] = sessions
        above = sess[pl.ds(PAD - 1 + base, SLAB_ROWS), :]
        before = pltpu.roll(jnp.where(lane_s == LANES - 1, above, sessions), 1, 1)
        value = jnp.minimum(items, ROWS) + 1
        codes[pl.ds(PAD + base, SLAB_ROWS), :] = jnp.where(
            before != sessions, -value, value
        ).astype(jnp.float32)
        is_row = items < ROWS
        owned = jnp.where(is_row, items >> 1, items >> 10) == jnp.where(is_row, pair_id, block_id)
        ident = jnp.where(is_row, OWNED + items, items & (OWNED - 1))
        rows = pl.ds(base, SLAB_ROWS)
        mask[rows, :] = hot(owned).astype(jnp.bfloat16)
        table[rows, pl.ds(LANES, LANES)] = (ident & 255).astype(jnp.float32).astype(jnp.bfloat16)
        table[rows, pl.ds(2 * LANES, LANES)] = (ident >> 8).astype(jnp.float32).astype(jnp.bfloat16)
        return carry

    lax.fori_loop(0, SLABS, unpack, 0, unroll=4)
    for r in range(0, EVENT_ROWS, 128):
        rows = pl.ds(r, 128)
        table[rows, pl.ds(3 * LANES, LANES)] = codes[pl.ds(PAD - 1 + r, 128), :].astype(jnp.bfloat16)
        table[rows, pl.ds(4 * LANES, LANES)] = codes[pl.ds(PAD + r, 128), :].astype(jnp.bfloat16)
        table[rows, pl.ds(5 * LANES, LANES)] = codes[pl.ds(PAD + 1 + r, 128), :].astype(jnp.bfloat16)

    upto = hot(iota((LANES, LANES), 0) <= iota((LANES, LANES), 1)).astype(jnp.bfloat16)
    owned = mask[...]
    rank = jnp.dot(owned, upto, preferred_element_type=jnp.float32)
    table[:, pl.ds(0, LANES)] = (rank * owned.astype(jnp.float32)).astype(jnp.bfloat16)
    per_row = nt_dot(jnp.ones((8, LANES), jnp.bfloat16), owned)
    groups = EVENT_ROWS // LANES
    grouped = jnp.concatenate(
        [per_row[:1, g * LANES : (g + 1) * LANES] for g in range(groups)], axis=0
    )
    inside = jnp.dot(grouped.astype(jnp.bfloat16), upto, preferred_element_type=jnp.float32)
    ends, starts, base = [], [], jnp.zeros((1, 1), jnp.float32)
    for g in range(groups):
        ends.append(inside[g : g + 1] + base)
        starts.append(ends[g] - grouped[g : g + 1])
        base = base + inside[g : g + 1, LANES - 1 :]
    owned_events = jnp.max(base).astype(jnp.int32)

    counts[...] = jnp.zeros(counts.shape, jnp.float32)
    lane_f = iota((SLOTS, LANES), 1, jnp.float32)
    row32, col32 = iota((32, 32), 0), iota((32, 32), 1)
    ahead = (row32 > WINDOW) & (col32 > WINDOW) & (col32 <= row32)
    behind = (row32 < WINDOW) & (col32 > row32) & (col32 <= WINDOW)
    between = hot(ahead | behind).astype(jnp.bfloat16)
    place = iota((32, SLOTS), 0)
    in_window = (place != WINDOW) & (place <= 2 * WINDOW)
    row_ids = iota((ROWS, SLOTS), 0, jnp.float32)
    col_ids = iota((SLOTS, COLS), 1, jnp.float32)

    def chunk(step, carry):
        slot = (step * SLOTS + iota((SLOTS, LANES), 0)).astype(jnp.float32)
        picks, first = [], jnp.zeros((SLOTS, LANES), jnp.float32)
        for g in range(groups):
            here = (slot >= starts[g]) & (slot < ends[g])
            first += jnp.where(here, starts[g], 0.0)
            picks.append(hot(here).astype(jnp.bfloat16))
        pick = jnp.concatenate(picks, axis=1)
        got = jnp.dot(pick, table[...], preferred_element_type=jnp.float32)
        ordinal = slot[:, :1] + 1.0 - jnp.sum(first, axis=1, keepdims=True)
        chosen = got[:, :LANES] == ordinal
        ident = got[:, LANES : 2 * LANES] + 256.0 * got[:, 2 * LANES : 3 * LANES]
        column = jnp.sum(jnp.where(chosen, ident + 1.0, 0.0), axis=1, keepdims=True) - 1.0
        at_lane = jnp.sum(jnp.where(chosen, lane_f, 0.0), axis=1, keepdims=True)
        source = at_lane.astype(jnp.int32) + (iota((SLOTS, LANES), 1) - WINDOW)
        index = source & (LANES - 1)
        parts = [
            jnp.take_along_axis(got[:, k * LANES : (k + 1) * LANES], index, axis=1, mode="promise_in_bounds")
            for k in (3, 4, 5)
        ]
        window = jnp.where(source < 0, parts[0], jnp.where(source < LANES, parts[1], parts[2]))
        window = window.T[:32]
        breaks = hot(window < 0.0).astype(jnp.bfloat16)
        crossed = jnp.dot(between, breaks, preferred_element_type=jnp.float32)
        linked = (crossed == 0.0) & in_window
        near = jnp.where(linked, jnp.abs(window) - 1.0, 255.0)
        weight = jnp.sum(hot(linked), axis=0, keepdims=True)
        pairs = jnp.zeros((ROWS, SLOTS), jnp.float32)
        for d in range(2 * WINDOW + 1):
            if d != WINDOW:
                pairs += hot(near[d : d + 1] == row_ids)
        pairs = jnp.concatenate([pairs, jnp.broadcast_to(weight, (16, SLOTS))], axis=0)
        column_hot = hot(column == col_ids).astype(jnp.bfloat16)
        counts[...] += jnp.dot(
            pairs.astype(jnp.bfloat16), column_hot, preferred_element_type=jnp.float32
        )
        return carry

    lax.fori_loop(0, (owned_events + SLOTS - 1) // SLOTS, chunk, 0)

    def both(row_first, row_second):
        mine_f, its_f = own_ref[:, row_first, :], other_ref[:, row_first, :]
        mine_s, its_s = own_ref[:, row_second, :], other_ref[:, row_second, :]
        return jnp.where(half == 0, mine_f, its_f), jnp.where(half == 0, its_s, mine_s)

    start_items, end_items = both(0, 15)
    start_sess, end_sess = both(16, 23)
    start_sess, end_sess = start_sess & 65535, end_sess >> 16
    slab_row = iota((SLABS, LANES), 0)
    end_items = pltpu.roll(end_items, 1, 0)
    end_sess = jnp.where(slab_row == 0, -1, pltpu.roll(end_sess, 1, 0))
    cross = jnp.zeros((SLABS, LANES), jnp.float32)
    lane = iota((SLABS, LANES), 1)
    for d in range(1, WINDOW + 1):
        before = pltpu.roll(end_sess, d, 1)
        after = pltpu.roll(start_sess, LANES - d, 1)
        cross += hot((lane < d) & (before == start_sess))
        cross += hot((lane >= LANES - d) & (after == end_sess))
    cross_items = jnp.where(lane < LANES // 2, start_items, end_items)
    margins = jnp.sum(own_ref[:, MARGIN_ROW, :], axis=0, keepdims=True).astype(jnp.float32)
    item_row = iota((ROWS, LANES), 0)
    held = jnp.where(item_row == iota((ROWS, LANES), 1), margins, 0.0)
    for s in range(SLABS):
        held += jnp.where(cross_items[s : s + 1] == item_row, cross[s : s + 1], 0.0)
    row_margin = jnp.sum(held, axis=1, keepdims=True)
    totals = jnp.sum(own_ref[:, TOTAL_ROW, :], axis=0, keepdims=True).astype(jnp.float32)
    totals = totals + jnp.sum(cross, axis=0, keepdims=True)
    pair_total = jnp.sum(totals, axis=1, keepdims=True)

    positive = ppmi(
        counts[pl.ds(0, ROWS), :], row_margin, counts[pl.ds(ROWS, 1), :], pair_total
    )
    copy.wait()
    row_words = jnp.where(half == 0, own_ref[:WORDS, BITS_ROW, :], other_ref[:WORDS, BITS_ROW, :])
    fill_signs(jnp.concatenate([words[...], row_words], axis=1), signs)
    result = project(positive, signs)
    for s in range(SLABS):
        out_ref[s] = result[s * ROWS_DEV : (s + 1) * ROWS_DEV]


def all_events(where, items, sessions, bits, interpret=False):
    return pl.pallas_call(
        lambda *refs: all_events_kernel(where, *refs),
        out_shape=jax.ShapeDtypeStruct((SLABS, PAYLOAD, LANES), jnp.int32),
        grid=(1,),
        in_specs=[
            pl.BlockSpec((SLAB_ROWS, LANES), lambda i: (0, 0)),
            pl.BlockSpec((SLAB_ROWS, LANES), lambda i: (0, 0)),
            pl.BlockSpec((WORDS, LANES), lambda i: (0, 0)),
        ],
        out_specs=pl.BlockSpec((SLABS, PAYLOAD, LANES), lambda i: (0, 0, 0)),
        compiler_params=pltpu.CompilerParams(vmem_limit_bytes=VMEM_BYTES),
        interpret=interpret,
        name="all_events",
    )(items, sessions, bits)


def from_all(where, own, other, bits, interpret=False):
    return pl.pallas_call(
        lambda *refs: from_all_kernel(where, *refs),
        out_shape=jax.ShapeDtypeStruct((SLABS, ROWS_DEV, SKETCH), jnp.float32),
        in_specs=[
            pl.BlockSpec(memory_space=pltpu.VMEM),
            pl.BlockSpec(memory_space=pltpu.VMEM),
            pl.BlockSpec(memory_space=pl.ANY),
        ],
        out_specs=pl.BlockSpec(memory_space=pltpu.VMEM),
        scratch_shapes=[
            pltpu.VMEM((PAD + EVENT_ROWS, LANES), jnp.int32),
            pltpu.VMEM((2 * PAD + EVENT_ROWS, LANES), jnp.float32),
            pltpu.VMEM((EVENT_ROWS, LANES), jnp.bfloat16),
            pltpu.VMEM((EVENT_ROWS, 6 * LANES), jnp.bfloat16),
            pltpu.VMEM((ROWS + 16, COLS), jnp.float32),
            pltpu.VMEM((WORDS, OWNED), jnp.int32),
            pltpu.VMEM((16 * WORD_BITS, COLS), jnp.bfloat16),
            pltpu.SemaphoreType.DMA,
        ],
        compiler_params=pltpu.CompilerParams(vmem_limit_bytes=VMEM_BYTES),
        interpret=interpret,
        name="from_all",
    )(own, other, bits)


def route_kernel(where, items_hbm, sessions_hbm, out_ref, items_v, sessions_v, codes, table, near_rows, one_hots, pair_rows, sems):
    slab, band = where()
    get_items = pltpu.make_async_copy(items_hbm, items_v, sems.at[0])
    get_sessions = pltpu.make_async_copy(sessions_hbm, sessions_v, sems.at[1])
    get_items.start()
    get_sessions.start()
    get_items.wait()
    get_sessions.wait()
    items, sessions = items_v[...], sessions_v[...]
    shape = items.shape
    row, lane = iota(shape, 0), iota(shape, 1)
    above = jnp.where(row == 0, -1, pltpu.roll(sessions, 1, 0))
    below = jnp.where(row == SLAB_ROWS - 1, -1, pltpu.roll(sessions, SLAB_ROWS - 1, 0))
    earlier_links = jnp.zeros(shape, jnp.float32)
    later_links = jnp.zeros(shape, jnp.float32)
    for d in range(1, WINDOW + 1):
        earlier = pltpu.roll(jnp.where(lane >= LANES - d, above, sessions), d, 1)
        later = pltpu.roll(jnp.where(lane < d, below, sessions), LANES - d, 1)
        earlier_links += hot(earlier == sessions)
        later_links += hot(later == sessions)
    weights = earlier_links + later_links

    one, none = jnp.ones((), jnp.bfloat16), jnp.zeros((), jnp.bfloat16)
    item_codes = jnp.minimum(items, 255).astype(jnp.float32).astype(jnp.bfloat16)
    row_ids = iota((ROWS, LANES), 0, jnp.float32).astype(jnp.bfloat16)
    for r in range(SLAB_ROWS):
        same = item_codes[r : r + 1] == row_ids
        one_hots[:, pl.ds(r * LANES, LANES)] = jnp.where(same, one, none)
        pair_rows[pl.ds(ROWS, 16), pl.ds(r * LANES, LANES)] = jnp.broadcast_to(
            weights[r : r + 1], (16, LANES)
        ).astype(jnp.bfloat16)
    total = jnp.sum(weights, axis=0, keepdims=True)
    first_link = (iota(shape, 1, jnp.float32) - earlier_links).astype(jnp.bfloat16)
    place = iota((LANES, LANES), 0, jnp.float32).astype(jnp.bfloat16)
    sooner = iota((LANES, LANES), 0) < iota((LANES, LANES), 1)
    sooner = jnp.where(sooner, place, jnp.full((), -64.0, jnp.bfloat16))
    last = (iota((16, LANES), 0, jnp.float32) - 16.0).astype(jnp.bfloat16)
    ordered = jnp.zeros((ROWS + 16, ROWS), jnp.float32)
    no_links = jnp.zeros((LANES - 16, LANES), jnp.bfloat16)
    for r in range(SLAB_ROWS):
        begin = first_link[r : r + 1]
        links = jnp.where(sooner >= begin, one, none)
        if r == 0:
            pairs = jnp.dot(one_hots[:, pl.ds(0, LANES)], links, preferred_element_type=jnp.float32)
        else:
            links = jnp.concatenate([no_links, jnp.where(last >= begin, one, none), links], axis=0)
            pairs = jnp.dot(
                one_hots[:, pl.ds((r - 1) * LANES, 2 * LANES)], links, preferred_element_type=jnp.float32
            )
        pair_rows[pl.ds(0, ROWS), pl.ds(r * LANES, LANES)] = pairs.astype(jnp.bfloat16)
        if r % 8 == 7:
            ready = pl.ds((r - 7) * LANES, 8 * LANES)
            ordered += nt_dot(pair_rows[:, ready], one_hots[:, ready])
    margin = ordered[ROWS : ROWS + 1]
    ordered = ordered[:ROWS]
    row_pairs = ordered + ordered.T
    item_row = iota((ROWS, LANES), 0)

    before = pltpu.roll(jnp.where(lane == LANES - 1, above, sessions), 1, 1)
    value = jnp.minimum(items, ROWS) + 1
    edge = jnp.full((PAD, LANES), -(ROWS + 1.0), jnp.float32)
    codes[pl.ds(0, PAD), :] = edge
    codes[pl.ds(PAD + SLAB_ROWS, PAD), :] = edge
    codes[pl.ds(PAD, SLAB_ROWS), :] = jnp.where(before != sessions, -value, value).astype(jnp.float32)
    inside = items - band * (SLABS * OWNED)
    wide = (items >= ROWS) & (inside >= 0) & (inside < SLABS * OWNED)
    inside = jnp.where(wide, inside, 0)
    owner = jnp.where(wide, inside >> 10, -1)
    owner_row = iota((SLABS, LANES), 0)
    marks = [hot(owner[r : r + 1] == owner_row) for r in range(SLAB_ROWS)]
    upto = hot(iota((LANES, LANES), 0) <= iota((LANES, LANES), 1)).astype(jnp.bfloat16)
    ranks = jnp.dot(
        jnp.concatenate(marks, axis=0).astype(jnp.bfloat16), upto, preferred_element_type=jnp.float32
    )
    ranks = [ranks[r * SLABS : (r + 1) * SLABS] for r in range(SLAB_ROWS)]
    per_row = jnp.zeros((SLABS, LANES), jnp.float32)
    for r in range(SLAB_ROWS):
        per_row = jnp.where(lane == r, ranks[r][:, LANES - 1 :], per_row)
    ends = jnp.dot(per_row.astype(jnp.bfloat16), upto, preferred_element_type=jnp.float32)
    starts = ends - per_row
    block = jnp.where(items >= ROWS, items >> 10, -1)
    sixteen = iota((16, LANES), 0)
    upper = [hot((block[r : r + 1] >> 4) == sixteen) for r in range(SLAB_ROWS)]
    lower = [hot((block[r : r + 1] & 15) == sixteen) for r in range(SLAB_ROWS)]
    loads = nt_dot(
        jnp.concatenate(upper, axis=1).astype(jnp.bfloat16),
        jnp.concatenate(lower, axis=1).astype(jnp.bfloat16),
    )
    most = jnp.max(jnp.max(loads, axis=0, keepdims=True), axis=1, keepdims=True)
    orders = [
        jnp.sum(marks[r] * (ranks[r] + starts[:, r : r + 1]), axis=0, keepdims=True)
        for r in range(SLAB_ROWS)
    ]
    table[pl.ds(SLAB_ROWS, LANES - SLAB_ROWS), :] = jnp.zeros((LANES - SLAB_ROWS, 5 * LANES), jnp.bfloat16)
    row_codes = codes[pl.ds(PAD, SLAB_ROWS), :]
    left = jnp.where(lane >= LANES - 32, codes[pl.ds(PAD - 1, SLAB_ROWS), :], row_codes)
    right = jnp.where(lane < 32, codes[pl.ds(PAD + 1, SLAB_ROWS), :], row_codes)
    fields = [
        jnp.minimum(jnp.concatenate(orders, axis=0), 255.0),
        (inside & 255).astype(jnp.float32),
        (inside >> 8).astype(jnp.float32),
        pltpu.roll(left, 32, 1),
        pltpu.roll(right, LANES - 32, 1),
    ]
    for k, field in enumerate(fields):
        table[pl.ds(0, SLAB_ROWS), pl.ds(k * LANES, LANES)] = field.astype(jnp.bfloat16)
    slot = iota((QUOTA, LANES), 0, jnp.float32).astype(jnp.bfloat16)
    from_slot = jnp.minimum(starts, 255.0).astype(jnp.bfloat16)
    to_slot = jnp.minimum(ends, 255.0).astype(jnp.bfloat16)
    picks = [
        jnp.where((slot >= from_slot[s : s + 1]) & (slot < to_slot[s : s + 1]), one, none)
        for s in range(SLABS)
    ]
    got = jnp.dot(jnp.concatenate(picks, axis=0), table[...], preferred_element_type=jnp.float32)
    big = (SLABS * QUOTA, LANES)
    number, lanes = iota(big, 0), iota(big, 1)
    target = (number >> 5).astype(jnp.float32) * 4.0
    high = got[:, 2 * LANES : 3 * LANES] - target
    ordinal = ((number & (QUOTA - 1)) + 1).astype(jnp.float32)
    chosen = (got[:, :LANES] == ordinal) & (high >= 0.0) & (high < 4.0)
    ident = got[:, LANES : 2 * LANES] + 256.0 * high + 1.0
    found = jnp.sum(
        jnp.where(chosen, ident * LANES + lanes.astype(jnp.float32), 0.0), axis=1, keepdims=True
    ).astype(jnp.int32)
    column = (((found >> 7) - 1) & 4095).astype(jnp.float32)
    at_lane = found & (LANES - 1)
    index = ((at_lane & (HALF - 1)) + (32 - WINDOW) + lanes) & (LANES - 1)
    reach = jnp.where(at_lane < HALF, got[:, 3 * LANES : 4 * LANES], got[:, 4 * LANES :])
    window = jnp.take_along_axis(reach, index, axis=1, mode="promise_in_bounds")
    from_lane, to_lane = iota((LANES, LANES), 0), iota((LANES, LANES), 1)
    ahead = (to_lane > WINDOW) & (from_lane > WINDOW) & (from_lane <= to_lane)
    behind = (to_lane < WINDOW) & (from_lane > to_lane) & (from_lane <= WINDOW)
    between = hot(ahead | behind).astype(jnp.bfloat16)
    crossed = jnp.dot(
        hot(window < 0.0).astype(jnp.bfloat16), between, preferred_element_type=jnp.float32
    )
    linked = (crossed == 0.0) & (lanes <= 2 * WINDOW)
    near = jnp.where(linked, jnp.abs(window) - 1.0, NONE)
    near = jnp.where(lanes == WINDOW, column, near)
    near_rows[...] = (near + 4096.0 * pltpu.roll(near, LANES - 16, 1)).astype(jnp.int32)

    whole = jnp.where(item_row == iota((ROWS, LANES), 1), ordered, row_pairs).astype(jnp.int32)
    packed = pltpu.roll(whole, HALF, 1) + jnp.where(iota((ROWS, LANES), 1) >= HALF, whole * 65536, 0)
    ends_lane = iota((1, LANES), 1)
    spare = jnp.where(most > QUOTA, 1, 0)
    total = jnp.sum(total, axis=1, keepdims=True).astype(jnp.int32)
    margin = margin.astype(jnp.int32)

    def edges(values, single):
        both = jnp.where(ends_lane < LANES - 32, pltpu.roll(values[:1], HALF, 1), values[SLAB_ROWS - 1 :])
        return jnp.where(ends_lane == SPOT, single, both)

    common = jnp.concatenate(
        [pltpu.roll(margin, HALF, 1), margin, edges(items, total), edges(sessions, spare)], axis=0
    )
    sixteenth = iota((8, LANES), 1) >> 4
    for s in range(SLABS):
        rows = jnp.concatenate([packed[s * ROWS_DEV : (s + 1) * ROWS_DEV], common], axis=0)
        for g in range(QUOTA // 8):
            part = near_rows[pl.ds(s * QUOTA + 8 * g, 8), :]
            rows = jnp.where(sixteenth == g, pltpu.roll(part, 16 * g, 1) if g else part, rows)
        out_ref[s] = rows


def count_pairs(near, skip):
    slots = near.shape[1]
    place = iota(near.shape, 0)
    real = near < NONE
    for d in skip:
        real = real & (place != d)
    weight = jnp.sum(hot(real), axis=0, keepdims=True)
    row_ids = iota((ROWS, slots), 0, jnp.float32).astype(COUNT)
    one, none = jnp.ones((), COUNT), jnp.zeros((), COUNT)
    pairs = jnp.zeros((ROWS, slots), COUNT)
    near = near.astype(COUNT)
    for d in range(near.shape[0]):
        if d not in skip:
            pairs += jnp.where(near[d : d + 1] == row_ids, one, none)
    weight = jnp.broadcast_to(weight, (16, slots)).astype(jnp.bfloat16)
    return jnp.concatenate([pairs.astype(jnp.bfloat16), weight], axis=0)


def sketch_kernel(
    where, got_ref, row_bits_ref, bits_hbm, out_ref, spoilt_ref, counts, table, words, wide_signs, sem
):
    slab, band = where()
    copy = pltpu.make_async_copy(
        bits_hbm.at[:, pl.ds(pl.multiple_of(slab * OWNED, OWNED), OWNED)], words, sem
    )
    copy.start()

    slab_row, lane = iota((SLABS, LANES), 0), iota((SLABS, LANES), 1)
    raw_items, raw_sessions = got_ref[:, 6, :], got_ref[:, 7, :]
    edge_items = jnp.where(lane < HALF, pltpu.roll(raw_items, HALF, 1), raw_items)
    edge_sessions = jnp.where(lane < HALF, pltpu.roll(raw_sessions, HALF, 1), raw_sessions)
    spoilt_ref[0, 0] = jnp.max(jnp.where(lane == SPOT, raw_sessions, 0))
    end_items = pltpu.roll(edge_items, 1, 0)
    end_sess = jnp.where(slab_row == 0, -1, pltpu.roll(edge_sessions, 1, 0))
    cross = jnp.zeros((SLABS, LANES), jnp.float32)
    for d in range(1, WINDOW + 1):
        before = pltpu.roll(end_sess, d, 1)
        after = pltpu.roll(edge_sessions, LANES - d, 1)
        cross += hot((lane < d) & (before == edge_sessions))
        cross += hot((lane >= LANES - d) & (after == end_sess))
    items = jnp.where(lane < HALF, edge_items, end_items)
    over = jnp.where(
        lane < HALF,
        hot((edge_sessions == end_sess[:, LANES - 1 :]) & (lane < WINDOW)),
        hot((end_sess == edge_sessions[:, :1]) & (lane >= LANES - WINDOW)),
    )
    partner = jnp.where(over > 0.0, jnp.minimum(items, ROWS).astype(jnp.float32), NONE)
    is_row = items < ROWS
    row_owner = jnp.where(band == 0, slab, -1)
    owned = jnp.where(is_row, items >> 2, items >> 10) == jnp.where(is_row, row_owner, band * SLABS + slab)
    owned = hot(owned & (cross > 0.0))
    local_id = jnp.where(is_row, OWNED + items, items & (OWNED - 1))
    upto = hot(iota((LANES, LANES), 0) <= iota((LANES, LANES), 1)).astype(jnp.bfloat16)
    blank = jnp.zeros((LANES - SLABS, LANES), jnp.float32)
    marks = jnp.concatenate([owned, blank], axis=0).astype(jnp.bfloat16)
    rank = jnp.dot(marks, upto, preferred_element_type=jnp.float32)
    per_row = nt_dot(jnp.ones((8, LANES), jnp.bfloat16), marks)
    ends = jnp.dot(per_row.astype(jnp.bfloat16), upto, preferred_element_type=jnp.float32)
    starts = (ends - per_row)[:1]
    ends = ends[:1]
    crossing = jnp.max(ends).astype(jnp.int32)
    fields = [
        rank[:SLABS] * owned,
        (local_id & 255).astype(jnp.float32),
        (local_id >> 8).astype(jnp.float32),
        partner,
    ]
    for k, field in enumerate(fields):
        table[:, pl.ds(k * LANES, LANES)] = jnp.concatenate([field, blank], axis=0).astype(jnp.bfloat16)
    slot_lane = iota((LANES, LANES), 1)
    col_ids = iota((LANES, COLS), 1, jnp.float32)

    def crossed(step):
        slot = (step * LANES + iota((LANES, LANES), 0)).astype(jnp.float32)
        here = (slot >= starts) & (slot < ends)
        first = jnp.sum(jnp.where(here, starts, 0.0), axis=1, keepdims=True)
        got = jnp.dot(hot(here).astype(jnp.bfloat16), table[...], preferred_element_type=jnp.float32)
        chosen = got[:, :LANES] == slot[:, :1] + 1.0 - first
        ident = got[:, LANES : 2 * LANES] + 256.0 * got[:, 2 * LANES : 3 * LANES]
        column = jnp.sum(jnp.where(chosen, ident + 1.0, 0.0), axis=1, keepdims=True) - 1.0
        at = jnp.sum(jnp.where(chosen, slot_lane, 0), axis=1, keepdims=True)
        reach = LANES - WINDOW
        other_side = jnp.where(at < HALF, hot(slot_lane >= reach + at), hot(slot_lane <= at - reach))
        near = jnp.where(other_side > 0.0, got[:, 3 * LANES :], NONE).T
        near = jnp.concatenate([near[:16], near[LANES - 16 :]], axis=0)
        pairs = count_pairs(near, (15, 16))
        column_hot = hot(column == col_ids).astype(jnp.bfloat16)
        return jnp.dot(pairs, column_hot, preferred_element_type=jnp.float32)

    first_crossed = crossed(0)

    windows = got_ref[...].reshape(SLABS * MESSAGE, LANES).T[:HALF]
    low, high = (windows & 4095).astype(jnp.float32), (windows >> 12).astype(jnp.float32)
    within = first_crossed[:, :OWNED]
    for g in range(QUOTA // 8):
        near = jnp.concatenate([low[16 * g : 16 * g + 16], high[16 * g : 16 * g + 16]], axis=0)
        ident = near[WINDOW : WINDOW + 1]
        column_hot = hot(ident == iota((OWNED, ident.shape[1]), 0, jnp.float32)).astype(jnp.bfloat16)
        within += nt_dot(count_pairs(near, (WINDOW, 31)), column_hot)
    counts[:, pl.ds(0, OWNED)] = within

    low_sum = jnp.zeros((MESSAGE, LANES), jnp.int32)
    high_sum = jnp.zeros((MESSAGE, LANES), jnp.int32)
    for s in range(SLABS):
        word = got_ref[s]
        low_sum += word & 65535
        high_sum += (word >> 16) & 65535
    mine = jnp.where(iota((MESSAGE, LANES), 1) < HALF, pltpu.roll(low_sum, HALF, 1), high_sum)
    item_row, item_lane = iota((ROWS, LANES), 0), iota((ROWS, LANES), 1)
    placed = jnp.zeros((ROWS, LANES), jnp.int32)
    for q in range(ROWS_DEV):
        placed = jnp.where(item_row == row_owner * ROWS_DEV + q, mine[q : q + 1], placed)
    placed = jnp.where(item_row == item_lane, 2 * placed, placed).astype(jnp.float32)
    counts[pl.ds(0, ROWS), pl.ds(OWNED, ROWS)] = placed.T + first_crossed[:ROWS, OWNED:]

    def chunk(step, carry):
        counts[...] += crossed(step)
        return carry

    lax.fori_loop(1, (crossing + LANES - 1) // LANES, chunk, 0)

    margin_low = jnp.sum(got_ref[:, 4, :], axis=0, keepdims=True)
    margin_high = jnp.sum(got_ref[:, 5, :], axis=0, keepdims=True)
    margins = jnp.where(item_lane[:1] < HALF, pltpu.roll(margin_low, HALF, 1), margin_high)
    held = jnp.where(item_row == item_lane, margins.astype(jnp.float32), 0.0)
    edge_codes = jnp.minimum(items, 255).astype(jnp.float32).astype(jnp.bfloat16)
    edge_rows = item_row.astype(jnp.float32).astype(jnp.bfloat16)
    edge_cross = cross.astype(jnp.bfloat16)
    for first in range(0, SLABS, 16):
        part = jnp.zeros((ROWS, LANES), jnp.bfloat16)
        for s in range(first, first + 16):
            same = edge_codes[s : s + 1] == edge_rows
            part += jnp.where(same, edge_cross[s : s + 1], jnp.zeros((), jnp.bfloat16))
        held += part.astype(jnp.float32)
    row_margin = jnp.sum(held, axis=1, keepdims=True)
    totals = jnp.where(lane == SPOT, raw_items, 0).astype(jnp.float32) + cross
    pair_total = jnp.sum(jnp.sum(totals, axis=0, keepdims=True), axis=1, keepdims=True)
    col_margin = jnp.concatenate(
        [counts[pl.ds(ROWS, 1), pl.ds(0, OWNED)], jnp.sum(held.T, axis=0, keepdims=True)], axis=1
    )
    positive = ppmi(counts[pl.ds(0, ROWS), :], row_margin, col_margin, pair_total)
    copy.wait()
    held_words = jnp.concatenate([words[...], row_bits_ref[...]], axis=1)
    for b in range(WORD_BITS):
        sign = jnp.where((held_words >> b) & 1 == 1, 1.0, -1.0)
        for j in range(COLS // LANES):
            wide_signs[j, pl.ds(b, WORDS, stride=WORD_BITS), :] = sign[:, j * LANES : (j + 1) * LANES]
    parts = two_parts(positive)
    signs = [wide_signs[j, pl.ds(0, SKETCH), :].astype(jnp.bfloat16) for j in range(COLS // LANES)]
    result = nt_dot(parts, jnp.concatenate(signs, axis=1))
    result = result[:ROWS] + result[ROWS:]
    for s in range(SLABS):
        out_ref[s] = result[s * ROWS_DEV : (s + 1) * ROWS_DEV]


def route(where, items, sessions, interpret=False):
    return pl.pallas_call(
        lambda *refs: route_kernel(where, *refs),
        out_shape=jax.ShapeDtypeStruct((SLABS, MESSAGE, LANES), jnp.int32),
        in_specs=[pl.BlockSpec(memory_space=pltpu.HBM)] * 2,
        out_specs=pl.BlockSpec(memory_space=pltpu.VMEM),
        scratch_shapes=[
            pltpu.VMEM((SLAB_ROWS, LANES), jnp.int32),
            pltpu.VMEM((SLAB_ROWS, LANES), jnp.int32),
            pltpu.VMEM((2 * PAD + SLAB_ROWS, LANES), jnp.float32),
            pltpu.VMEM((LANES, 5 * LANES), jnp.bfloat16),
            pltpu.VMEM((SLABS * QUOTA, LANES), jnp.int32),
            pltpu.VMEM((ROWS, SLAB_ROWS * LANES), jnp.bfloat16),
            pltpu.VMEM((ROWS + 16, SLAB_ROWS * LANES), jnp.bfloat16),
            pltpu.SemaphoreType.DMA((2,)),
        ],
        compiler_params=pltpu.CompilerParams(vmem_limit_bytes=VMEM_BYTES),
        interpret=interpret,
        name="route_events",
    )(items, sessions)


def sketch_part(where, got, bits, interpret=False):
    return pl.pallas_call(
        lambda *refs: sketch_kernel(where, *refs),
        out_shape=(
            jax.ShapeDtypeStruct((SLABS, ROWS_DEV, SKETCH), jnp.float32),
            jax.ShapeDtypeStruct((1, 1), jnp.int32),
        ),
        grid=(1,),
        in_specs=[
            pl.BlockSpec((SLABS, MESSAGE, LANES), lambda i: (0, 0, 0)),
            pl.BlockSpec((WORDS, LANES), lambda i: (0, 0)),
            pl.BlockSpec(memory_space=pltpu.HBM),
        ],
        out_specs=(
            pl.BlockSpec((SLABS, ROWS_DEV, SKETCH), lambda i: (0, 0, 0)),
            pl.BlockSpec(memory_space=pltpu.SMEM),
        ),
        scratch_shapes=[
            pltpu.VMEM((ROWS + 16, COLS), jnp.float32),
            pltpu.VMEM((LANES, 4 * LANES), jnp.bfloat16),
            pltpu.VMEM((WORDS, OWNED), jnp.int32),
            pltpu.VMEM((COLS // LANES, 16 * WORD_BITS, LANES), jnp.float32),
            pltpu.SemaphoreType.DMA,
        ],
        compiler_params=pltpu.CompilerParams(vmem_limit_bytes=VMEM_BYTES),
        interpret=interpret,
        name="sketch_part",
    )(got, bits, bits)


def shares(part):
    rows = jnp.sum(lax.all_to_all(part, "stream", 0, 0, tiled=True), axis=0)
    spread = jnp.broadcast_to(rows[None], (BANDS,) + rows.shape)
    return lax.all_to_all(spread, "item", 0, 0, tiled=True)


def local(event_items, event_sessions, sketch_bits):
    def where():
        return lax.axis_index("stream"), lax.axis_index("item")

    items = event_items.reshape(SLAB_ROWS, LANES)
    sessions = event_sessions.reshape(SLAB_ROWS, LANES)

    def from_every_event(_):
        message = all_events(where, items, sessions, sketch_bits)
        own = lax.all_to_all(message, "stream", 0, 0, tiled=True)
        other = lax.ppermute(own, "item", [(i, i ^ 1) for i in range(BANDS)])
        return shares(from_all(where, own, other, sketch_bits))

    routed = lax.all_to_all(route(where, items, sessions), "stream", 0, 0, tiled=True)
    part, spoilt = sketch_part(where, routed, sketch_bits)
    gathered = lax.cond(spoilt[0, 0] > 0, from_every_event, lambda kept: kept, shares(part))
    return jnp.sum(gathered, axis=0) / math.sqrt(EVENT_ROWS * LANES)


def solution(mesh):
    placed = (P("stream"), P("stream"), P(None, "item"))
    return jax.shard_map(
        local, mesh=mesh, in_specs=placed, out_specs=P("stream", None), check_vma=False
    )
```
